32 devices in a mesh: facet: 8 (over z, x), freq: 4 (over y, core).
Axes of the slice: x: 2, y: 2, z: 4, core: 2. Of those that a mesh axis runs over, the one named last changes fastest.
Arguments:
- facet_image: bfloat16 [8, 2, 128, 4096], P('facet', None, 'freq'), may hold values from -6 to 6
- facet_offsets: int32 [8, 2], replicated, may hold values from 0 to 32767
- subgrid_rows: int32 [8], replicated, may hold values from 0 to 32767
- column_offset: int32 [1], replicated, may hold values from 0 to 32767
- uv_coords: int32 [2, 64, 8, 512], P(None, ('freq', 'facet')), may hold values from 0 to 255
- observed: bfloat16 [2, 64, 8, 512], P(None, ('freq', 'facet')), may hold values from -6 to 6
Outputs:
- image_residual: bfloat16 [8, 2, 128, 4096], P('facet', None, 'freq')
- residual_vis: bfloat16 [2, 64, 8, 512], P(None, ('freq', 'facet'))
The draws below stay inside these ranges and needn't reach their ends.
All inputs are finite; a program needn't handle non-finite values.
Results may differ from the reference program's by a relative error of at most 0.024.
Values may be sent and summed in bfloat16 or wider, within the bound.
No kernel may reach another device: no remote copies, remote signals or barrier semaphores. Data moves between devices by JAX's collectives and lax.ppermute only.
A program may use at most 64 MiB of HBM per device.

```python
import math
import jax
import jax.numpy as jnp
from jax import lax

IMAGE = 32768
FACET_W = 4096
CONTRIB = 128
SUBGRID = 256
PATCH = 32
VIS_PATCH = 512
FACETS = 8
FACET_ROWS = 128
COL_STEP = 8
ROW_STEP = 256
SUBGRIDS = 8
SIDE = 8
STEP = 128
PERIOD = 256


def with_ends(drawn, own_key, least, high):
    index_at = [jax.random.randint(jax.random.fold_in(own_key, axis), (), 0, length) for axis, length in enumerate(drawn.shape)]
    widest = drawn.shape.index(max(drawn.shape))
    neighbour = index_at[:widest] + [(index_at[widest] + 1) % drawn.shape[widest]] + index_at[widest + 1:]
    return drawn.at[tuple(index_at)].set(least).at[tuple(neighbour)].set(high)


def levels(rng, shape, shards, smallest, high):
    loudness, own = 1.0, jax.random.fold_in(rng, 6)
    for dim, shards_of in shards:
        steps = jnp.exp(jax.random.uniform(jax.random.fold_in(own, dim), (shards_of,), jnp.float32, smallest / len(shards), high / len(shards)))
        loudness = loudness * jnp.repeat(steps, shape[dim] // shards_of).reshape([-1 if axis == dim else 1 for axis in range(len(shape))])
    return loudness


def normal_values(rng, shape, width, limit, split=(), held_as=jnp.bfloat16):
    array = width * jax.random.normal(rng, shape, jnp.float32)
    if split:
        array = array * levels(rng, shape, split, -0.22, 0.18)
    return jnp.clip(array, -limit, limit).astype(held_as)


def setup_inputs(seed: int = 0) -> dict:
    streams_of = jax.random.split(jax.random.key(seed), 7)
    return {
        "facet_image": normal_values(streams_of[0], (FACETS, 2, FACET_ROWS, FACET_W), 1.0, 6.0, ((0, 8), (2, 4))),
        "facet_offsets": with_ends(jax.random.randint(streams_of[1], (FACETS, 2), 0, IMAGE), jax.random.fold_in(streams_of[1], 1), 0, IMAGE - 1).astype(jnp.int32),
        "subgrid_rows": with_ends(jax.random.randint(streams_of[2], (SUBGRIDS,), 0, IMAGE), jax.random.fold_in(streams_of[2], 1), 0, IMAGE - 1).astype(jnp.int32),
        "column_offset": jax.random.randint(streams_of[3], (1,), 0, IMAGE).astype(jnp.int32),
        "uv_coords": with_ends(jax.random.randint(streams_of[4], (2, SUBGRIDS * SIDE, SIDE, VIS_PATCH), 0, PERIOD), jax.random.fold_in(streams_of[4], 1), 0, PERIOD - 1).astype(jnp.int32),
        "observed": normal_values(streams_of[5], (2, SUBGRIDS * SIDE, SIDE, VIS_PATCH), 1.0, 6.0, ((1, 32),)),
    }


TWO_PI = 2.0 * math.pi

def phases(product, modulus, direction):
    angles = product.astype(jnp.float32) * (direction * TWO_PI / modulus)
    return (jnp.cos(angles).astype(jnp.bfloat16), jnp.sin(angles).astype(jnp.bfloat16))

def complex_product(pattern, left_real, left_imag, right_real, right_imag):
    lr = left_real.astype(jnp.float32)
    li = left_imag.astype(jnp.float32)
    rr = right_real.astype(jnp.float32)
    ri = right_imag.astype(jnp.float32)
    real_part = jnp.einsum(pattern, lr, rr) - jnp.einsum(pattern, li, ri)
    imag_part = jnp.einsum(pattern, lr, ri) + jnp.einsum(pattern, li, rr)
    return (real_part, imag_part)

def row_table(starts, row_ids, offset):
    frequencies = (starts[:, None] + ROW_STEP * jnp.arange(CONTRIB, dtype=jnp.int32)[None, :]) % IMAGE
    places = (offset + row_ids) % IMAGE
    return phases(frequencies[:, :, None] * places[None, None, :] % IMAGE, IMAGE, -1.0)

def column_table(column, offset, extent):
    frequencies = (column + COL_STEP * jnp.arange(CONTRIB, dtype=jnp.int32)) % IMAGE
    places = (offset + jnp.arange(extent, dtype=jnp.int32)) % IMAGE
    return phases(frequencies[:, None] * places[None, :] % IMAGE, IMAGE, -1.0)

def spread_table(row_ids, offsets):
    columns = (STEP * jnp.arange(CONTRIB, dtype=jnp.int32)[None, :] + offsets[:, None]) % IMAGE
    return phases(row_ids[None, :, None] * columns[:, None, :] % IMAGE, IMAGE, 1.0)

def patch_table(coords):
    cell_ids = jnp.arange(PATCH, dtype=jnp.int32)
    return phases(cell_ids[:, None] * coords[..., None, :] % PERIOD, PERIOD, 1.0)

def predict_and_adjoint(grid_real, grid_imag, coords_u, coords_v, seen_real, seen_imag):
    patch_rows = grid_real.shape[0] // PATCH
    vis_count = coords_u.shape[-1]

    def to_patches(grid):
        return grid.reshape(patch_rows, PATCH, SIDE, PATCH).transpose(0, 2, 1, 3)
    eu_real, eu_imag = patch_table(coords_u)
    ev_real, ev_imag = patch_table(coords_v)
    inner_real, inner_imag = complex_product('bcrs,bcst->bcrt', to_patches(grid_real), to_patches(grid_imag), ev_real, ev_imag)
    model_real = lax.optimization_barrier(jnp.sum(eu_real * inner_real - eu_imag * inner_imag, axis=2)) * (1.0 / PATCH)
    model_imag = lax.optimization_barrier(jnp.sum(eu_real * inner_imag + eu_imag * inner_real, axis=2)) * (1.0 / PATCH)
    residual_real = (seen_real.astype(jnp.float32) - model_real).astype(jnp.bfloat16)
    residual_imag = (seen_imag.astype(jnp.float32) - model_imag).astype(jnp.bfloat16)
    wide_real = residual_real.astype(jnp.float32)[:, :, None, :]
    wide_imag = residual_imag.astype(jnp.float32)[:, :, None, :]
    weighted_real = (wide_real * eu_real + wide_imag * eu_imag).astype(jnp.bfloat16)
    weighted_imag = (wide_imag * eu_real - wide_real * eu_imag).astype(jnp.bfloat16)
    grid_back_real, grid_back_imag = complex_product('bcrt,bcst->bcrs', weighted_real, weighted_imag, ev_real, -ev_imag)
    factor = 1.0 / math.sqrt(vis_count)

    def from_patches(grid):
        return (grid * factor).astype(jnp.bfloat16).transpose(0, 2, 1, 3).reshape(patch_rows * PATCH, SUBGRID)
    return (residual_real, residual_imag, from_patches(grid_back_real), from_patches(grid_back_imag))

def reference(facet_image, facet_offsets, subgrid_rows, column_offset, uv_coords, observed):
    column = column_offset[0]
    scale_cols = 1.0 / math.sqrt(FACET_W)
    scale_rows = 1.0 / math.sqrt(FACET_ROWS)
    adjoint_scale = 1.0 / math.sqrt(SUBGRIDS * CONTRIB)
    final_scale = 1.0 / math.sqrt(CONTRIB)
    all_rows = jnp.arange(FACET_ROWS, dtype=jnp.int32)

    def facet_forward(inputs):
        facet_data, offset = inputs
        col_real, col_imag = column_table(column, offset[1], FACET_W)
        raw_real, raw_imag = complex_product('xy,ky->xk', facet_data[0], facet_data[1], col_real, col_imag)
        trans_real = (raw_real * scale_cols).astype(jnp.bfloat16)
        trans_imag = (raw_imag * scale_cols).astype(jnp.bfloat16)
        row_real, row_imag = row_table(subgrid_rows, all_rows, offset[0])
        sum_real, sum_imag = complex_product('jkx,xl->jkl', row_real, row_imag, trans_real, trans_imag)
        return (jnp.stack((sum_real, sum_imag), axis=1) * scale_rows).astype(jnp.bfloat16)
    contributions = lax.map(facet_forward, (facet_image, facet_offsets))
    grid_ids = jnp.arange(SUBGRID, dtype=jnp.int32)
    spread_real, spread_imag = spread_table(grid_ids, facet_offsets[:, 0])
    cols_real, cols_imag = spread_table(grid_ids, facet_offsets[:, 1])

    def subgrid_section(inputs):
        contrib, coords, seen = inputs
        part_real, part_imag = complex_product('frk,fkl->frl', spread_real, spread_imag, contrib[:, 0], contrib[:, 1])
        part_real = part_real.astype(jnp.bfloat16)
        part_imag = part_imag.astype(jnp.bfloat16)
        grid_real, grid_imag = complex_product('frl,fsl->rs', part_real, part_imag, cols_real, cols_imag)
        grid_real = (grid_real * (1.0 / CONTRIB)).astype(jnp.bfloat16)
        grid_imag = (grid_imag * (1.0 / CONTRIB)).astype(jnp.bfloat16)
        res_real, res_imag, back_real, back_imag = predict_and_adjoint(grid_real, grid_imag, coords[0], coords[1], seen[0], seen[1])
        narrow_real, narrow_imag = complex_product('rs,fsl->frl', back_real, back_imag, cols_real, -cols_imag)
        narrow_real = narrow_real.astype(jnp.bfloat16)
        narrow_imag = narrow_imag.astype(jnp.bfloat16)
        adj_real, adj_imag = complex_product('frk,frl->fkl', spread_real, -spread_imag, narrow_real, narrow_imag)
        adjoint = (jnp.stack((adj_real, adj_imag), axis=1) * (1.0 / SUBGRID)).astype(jnp.bfloat16)
        return (jnp.stack((res_real, res_imag), axis=0), adjoint)
    coords_all = uv_coords.reshape(2, SUBGRIDS, SIDE, SIDE, VIS_PATCH).transpose(1, 0, 2, 3, 4)
    seen_all = observed.reshape(2, SUBGRIDS, SIDE, SIDE, VIS_PATCH).transpose(1, 0, 2, 3, 4)
    residuals, adjoints = lax.map(subgrid_section, (contributions.transpose(1, 0, 2, 3, 4), coords_all, seen_all))
    residual_vis = residuals.transpose(1, 0, 2, 3, 4).reshape(2, SUBGRIDS * SIDE, SIDE, VIS_PATCH)

    def facet_adjoint(inputs):
        adjoint, offset = inputs
        row_real, row_imag = row_table(subgrid_rows, all_rows, offset[0])
        sum_real, sum_imag = complex_product('jkx,jkl->xl', row_real, -row_imag, adjoint[:, 0], adjoint[:, 1])
        back_real = (sum_real * adjoint_scale).astype(jnp.bfloat16)
        back_imag = (sum_imag * adjoint_scale).astype(jnp.bfloat16)
        col_real, col_imag = column_table(column, offset[1], FACET_W)
        out_real, out_imag = complex_product('xk,ky->xy', back_real, back_imag, col_real, -col_imag)
        return (jnp.stack((out_real, out_imag), axis=0) * final_scale).astype(jnp.bfloat16)
    image_residual = lax.map(facet_adjoint, (adjoints.transpose(1, 0, 2, 3, 4), facet_offsets))
    return (image_residual, residual_vis)
```

```python
import functools
import math

import jax
import jax.numpy as jnp
from jax import lax
from jax.experimental import pallas as pl
from jax.experimental.pallas import tpu as pltpu
from jax.sharding import PartitionSpec as P

IMAGE = 32768
CONTRIB = 128
SUBGRID = 256
PATCH = 32
SIDE = 8
STEP = 128
PERIOD = 256
LANES = 128
MASK = IMAGE - 1

F32 = jnp.float32
BF16 = jnp.bfloat16


def iota(shape, axis):
    return lax.broadcasted_iota(jnp.int32, shape, axis)


def cis(turns):
    turns = turns & MASK
    quarter = (turns + IMAGE // 8) >> 13
    x = (turns - (quarter << 13)).astype(F32) * (2.0 * math.pi / IMAGE)
    x2 = x * x
    sine = x * (1.0 + x2 * (-1.0 / 6 + x2 * (1.0 / 120 - x2 * (1.0 / 5040))))
    cosine = 1.0 + x2 * (-0.5 + x2 * (1.0 / 24 + x2 * (-1.0 / 720 + x2 * (1.0 / 40320))))
    odd = (quarter & 1) == 1
    real = jnp.where(odd, sine, cosine)
    imag = jnp.where(odd, cosine, sine)
    real = jnp.where(((quarter + 1) & 2) == 2, -real, real)
    imag = jnp.where((quarter & 2) == 2, -imag, imag)
    return real, imag


def times(ar, ai, br, bi):
    return ar * br - ai * bi, ar * bi + ai * br


def block(rows):
    return jnp.concatenate([jnp.concatenate(row, axis=1) for row in rows], axis=0)


def dot(left, right):
    return lax.dot_general(left, right, (((1,), (0,)), ((), ())), preferred_element_type=F32)


def dot_t(left, right):
    return lax.dot_general(left, right, (((1,), (1,)), ((), ())), preferred_element_type=F32)


def column_tables(column, first, extent):
    col_step = IMAGE // extent
    far_count = extent // LANES
    near = ((column + col_step * iota((LANES, CONTRIB), 1)) & MASK) * iota((LANES, CONTRIB), 0)
    shape = (far_count, CONTRIB)
    far = ((column + col_step * iota(shape, 1)) & MASK) * ((first + LANES * iota(shape, 0)) & MASK)
    return cis(-near), cis(-far)


def near_weights(near):
    real, imag = near
    return block([[real, imag], [-imag, real]]).astype(BF16)


def column_kernel(column_ref, offsets_ref, image_ref, out_ref, left_ref):
    rows, extent = image_ref.shape[2:]
    far_count = extent // LANES
    first = offsets_ref[lax.axis_index("facet"), 1]
    near, (far_real, far_imag) = column_tables(column_ref[0], first, extent)
    for y1 in range(far_count):
        here = pl.ds(y1 * rows, rows)
        there = pl.ds(y1 * LANES, LANES)
        left_ref[here, :LANES] = image_ref[0, 0, :, there]
        left_ref[here, LANES:] = image_ref[0, 1, :, there]
    value = dot(left_ref[...], near_weights(near))
    real = jnp.zeros((rows, CONTRIB), F32)
    imag = jnp.zeros((rows, CONTRIB), F32)
    for y1 in range(far_count):
        part = value[y1 * rows : (y1 + 1) * rows]
        pr, pi = times(
            part[:, :CONTRIB], part[:, CONTRIB:], far_real[y1 : y1 + 1], far_imag[y1 : y1 + 1]
        )
        real += pr
        imag += pi
    scale = 1.0 / math.sqrt(extent)
    out_ref[0] = (real * scale).astype(BF16)
    out_ref[1] = (imag * scale).astype(BF16)


def spread_kernel(starts_ref, offsets_ref, piece_ref, out_ref):
    parts, _, rows, _ = piece_ref.shape
    facet_rows = parts * rows
    row_step = IMAGE // facet_rows
    block_rows = out_ref.shape[2]
    owners = SUBGRID // block_rows
    per_freq = out_ref.shape[0] // owners
    first = offsets_ref[lax.axis_index("facet"), 0]
    right = jnp.concatenate([piece_ref[q, ri] for ri in range(2) for q in range(parts)], axis=0)
    shape = (CONTRIB, facet_rows)
    contribs = []
    for j in range(per_freq):
        start = starts_ref[lax.axis_index("freq") * per_freq + j]
        turns = ((start + row_step * iota(shape, 0)) & MASK) * ((first + iota(shape, 1)) & MASK)
        rr, ri = cis(-turns)
        both = dot(block([[rr, -ri], [ri, rr]]).astype(BF16), right)
        contribs.append((both * (1.0 / math.sqrt(facet_rows))).astype(BF16))
    shape = (SUBGRID, CONTRIB)
    sr, si = cis(iota(shape, 0) * ((STEP * iota(shape, 1) + first) & MASK))
    spread = dot(
        block([[sr, -si], [si, sr]]).astype(BF16), jnp.concatenate(contribs, axis=1)
    ).astype(BF16)
    for j in range(per_freq):
        for o in range(owners):
            for ri in range(2):
                top = ri * SUBGRID + o * block_rows
                out_ref[j * owners + o, ri] = spread[
                    top : top + block_rows, j * CONTRIB : (j + 1) * CONTRIB
                ]


def patch_rows_of(row, stride):
    turn = IMAGE // PERIOD
    base = cis(iota((8, row.shape[1]), 0) * row * turn)
    blocks = [base]
    for _ in range(PATCH // 8 - 1):
        blocks.append(times(*blocks[-1], *stride))
    return (
        jnp.concatenate([b[0] for b in blocks], axis=0),
        jnp.concatenate([b[1] for b in blocks], axis=0),
    )


def grid_kernel(
    offsets_ref, in_ref, coords_ref, seen_ref, out_ref, res_ref, left_ref, back_ref, narrow_ref
):
    facets, _, block_rows, _ = in_ref.shape
    patch_rows = coords_ref.shape[1]
    vis = coords_ref.shape[3]
    turn = IMAGE // PERIOD
    shape = (facets, SUBGRID)
    firsts = jnp.zeros(shape, jnp.int32)
    for f in range(facets):
        firsts = jnp.where(iota(shape, 0) == f, offsets_ref[f, 1], firsts)
    shift_real, shift_imag = cis(firsts * iota(shape, 1))
    shape = (CONTRIB, SUBGRID)
    tr, ti = cis(iota(shape, 0) * iota(shape, 1) * STEP)
    weights = block([[tr, ti], [-ti, tr]]).astype(BF16)
    for f in range(facets):
        here = pl.ds(f * block_rows, block_rows)
        left_ref[here, :CONTRIB] = in_ref[f, 0]
        left_ref[here, CONTRIB:] = in_ref[f, 1]
    wide = dot(left_ref[...], weights)
    grid_real = jnp.zeros((block_rows, SUBGRID), F32)
    grid_imag = jnp.zeros((block_rows, SUBGRID), F32)
    for f in range(facets):
        part = wide[f * block_rows : (f + 1) * block_rows]
        pr, pi = times(
            part[:, :SUBGRID], part[:, SUBGRID:], shift_real[f : f + 1], shift_imag[f : f + 1]
        )
        grid_real += pr
        grid_imag += pi
    grid_real = (grid_real * (1.0 / CONTRIB)).astype(BF16).astype(F32)
    grid_imag = (grid_imag * (1.0 / CONTRIB)).astype(BF16).astype(F32)
    group = LANES // PATCH
    own = (iota((LANES, LANES), 0) // PATCH) == (iota((LANES, LANES), 1) // PATCH)
    factor = 1.0 / math.sqrt(vis)
    for p in range(patch_rows):
        strides = [cis(coords_ref[axis, p] * (8 * turn)) for axis in range(2)]
        for h in range(SIDE // group):
            tables = []
            for axis in range(2):
                made = [
                    patch_rows_of(
                        coords_ref[axis, p, pl.ds(c, 1), :],
                        (strides[axis][0][c : c + 1], strides[axis][1][c : c + 1]),
                    )
                    for c in range(h * group, (h + 1) * group)
                ]
                tables.append(
                    tuple(jnp.concatenate([m[ri] for m in made], axis=0) for ri in range(2))
                )
            (ur, ui), (vr, vi) = tables
            cells = (slice(p * PATCH, (p + 1) * PATCH), slice(h * LANES, (h + 1) * LANES))
            mr, mi = (
                jnp.where(own, jnp.concatenate([grid[cells]] * group, axis=0), 0.0)
                for grid in (grid_real, grid_imag)
            )
            ev = jnp.concatenate([vr, vi], axis=0).astype(BF16)
            inner = dot(block([[mr, -mi], [mi, mr]]).astype(BF16), ev)
            ir, ii = times(ur, ui, inner[:LANES], inner[LANES:])
            wr, wi = [], []
            for c in range(group):
                rows = slice(c * PATCH, (c + 1) * PATCH)
                at = h * group + c
                res = []
                for ri, value in enumerate((ir, ii)):
                    model = jnp.sum(value[rows], axis=0, keepdims=True) * (1.0 / PATCH)
                    seen = seen_ref[ri, p, pl.ds(at, 1), :].astype(F32)
                    rounded = (seen - model).astype(BF16)
                    res_ref[ri, p, pl.ds(at, 1), :] = rounded
                    res.append(rounded.astype(F32))
                wr.append(res[0] * ur[rows] + res[1] * ui[rows])
                wi.append(res[1] * ur[rows] - res[0] * ui[rows])
            back = dot_t(jnp.concatenate(wr + wi, axis=0).astype(BF16), ev)
            br = back[:LANES, :LANES] + back[LANES:, LANES:]
            bi = back[LANES:, :LANES] - back[:LANES, LANES:]
            for ri, value in enumerate((br, bi)):
                value = jnp.where(own, value, 0.0)
                total = sum(value[c * PATCH : (c + 1) * PATCH] for c in range(group))
                back_ref[ri, cells[0], cells[1]] = (total * factor).astype(BF16).astype(F32)
    for f in range(facets):
        here = pl.ds(f * block_rows, block_rows)
        nr, ni = times(
            back_ref[0], back_ref[1], shift_real[f : f + 1], -shift_imag[f : f + 1]
        )
        narrow_ref[here, :SUBGRID] = nr.astype(BF16)
        narrow_ref[here, SUBGRID:] = ni.astype(BF16)
    narrowed = dot_t(narrow_ref[...], weights).astype(BF16)
    for f in range(facets):
        for ri in range(2):
            out_ref[f, ri] = narrowed[
                f * block_rows : (f + 1) * block_rows, ri * CONTRIB : (ri + 1) * CONTRIB
            ]


def gather_kernel(starts_ref, offsets_ref, in_ref, out_ref):
    parts, _, rows, _ = out_ref.shape
    facet_rows = parts * rows
    row_step = IMAGE // facet_rows
    block_rows = in_ref.shape[2]
    owners = SUBGRID // block_rows
    per_freq = in_ref.shape[0] // owners
    first = offsets_ref[lax.axis_index("facet"), 0]
    shape = (CONTRIB, SUBGRID)
    sr, si = cis(iota(shape, 1) * ((STEP * iota(shape, 0) + first) & MASK))
    right = block(
        [
            [
                jnp.concatenate([in_ref[j * owners + o, ri] for o in range(owners)], axis=0)
                for j in range(per_freq)
            ]
            for ri in range(2)
        ]
    )
    adjoint = dot(block([[sr, si], [-si, sr]]).astype(BF16), right)
    adjoint = (adjoint * (1.0 / SUBGRID)).astype(BF16)
    shape = (facet_rows, CONTRIB)
    total = jnp.zeros((2 * facet_rows, CONTRIB), F32)
    for j in range(per_freq):
        start = starts_ref[lax.axis_index("freq") * per_freq + j]
        turns = ((start + row_step * iota(shape, 1)) & MASK) * ((first + iota(shape, 0)) & MASK)
        rr, ri = cis(-turns)
        total += dot(
            block([[rr, ri], [-ri, rr]]).astype(BF16), adjoint[:, j * CONTRIB : (j + 1) * CONTRIB]
        )
    total = total.astype(BF16)
    for q in range(parts):
        for ri in range(2):
            top = ri * facet_rows + q * rows
            out_ref[q, ri] = total[top : top + rows]


def image_kernel(subgrids, column_ref, offsets_ref, in_ref, out_ref, left_ref):
    parts = in_ref.shape[0]
    rows, extent = out_ref.shape[2:]
    far_count = extent // LANES
    first = offsets_ref[lax.axis_index("facet"), 1]
    near, (far_real, far_imag) = column_tables(column_ref[0], first, extent)
    scale = 1.0 / math.sqrt(subgrids * CONTRIB)
    real, imag = (
        sum(in_ref[q, ri].astype(F32) for q in range(parts)) * scale for ri in range(2)
    )
    for y1 in range(far_count):
        here = pl.ds(y1 * rows, rows)
        ar, ai = times(real, imag, far_real[y1 : y1 + 1], -far_imag[y1 : y1 + 1])
        left_ref[here, :CONTRIB] = ar.astype(BF16)
        left_ref[here, CONTRIB:] = ai.astype(BF16)
    value = dot_t(left_ref[...], near_weights(near)) * (1.0 / math.sqrt(CONTRIB))
    value = value.astype(BF16)
    for y1 in range(far_count):
        for ri in range(2):
            out_ref[0, ri, :, pl.ds(y1 * LANES, LANES)] = value[
                y1 * rows : (y1 + 1) * rows, ri * LANES : (ri + 1) * LANES
            ]


def call(kernel, name, small, operands, outs, scratch=()):
    smem = pl.BlockSpec(memory_space=pltpu.SMEM)
    vmem = pl.BlockSpec(memory_space=pltpu.VMEM)
    return pl.pallas_call(
        kernel,
        name=name,
        out_shape=outs,
        in_specs=[smem] * len(small) + [vmem] * len(operands),
        out_specs=jax.tree.map(lambda _: vmem, outs),
        scratch_shapes=list(scratch),
        compiler_params=pltpu.CompilerParams(vmem_limit_bytes=40 * 1024 * 1024),
    )(*small, *operands)


def on_device(facet_image, facet_offsets, subgrid_rows, column_offset, uv_coords, observed):
    shape = jax.ShapeDtypeStruct
    rows, extent = facet_image.shape[2:]
    facets = lax.axis_size("facet")
    parts = lax.axis_size("freq")
    subgrids = subgrid_rows.shape[0]
    patch_rows = uv_coords.shape[1]
    block_rows = patch_rows * PATCH
    far_rows = extent // LANES * rows
    transformed = call(
        column_kernel,
        "column",
        (column_offset, facet_offsets),
        (facet_image,),
        shape((2, rows, CONTRIB), BF16),
        (pltpu.VMEM((far_rows, 2 * LANES), BF16),),
    )
    piece = lax.all_gather(transformed, "freq", axis=0, tiled=False)
    outgoing = call(
        spread_kernel,
        "spread",
        (subgrid_rows, facet_offsets),
        (piece,),
        shape((facets, 2, block_rows, CONTRIB), BF16),
    )
    incoming = lax.all_to_all(outgoing, "facet", split_axis=0, concat_axis=0, tiled=True)
    narrowed, residual_vis = call(
        grid_kernel,
        "grid",
        (facet_offsets,),
        (incoming, uv_coords, observed),
        (shape(incoming.shape, BF16), shape(observed.shape, BF16)),
        (
            pltpu.VMEM((facets * block_rows, 2 * CONTRIB), BF16),
            pltpu.VMEM((2, block_rows, SUBGRID), F32),
            pltpu.VMEM((facets * block_rows, 2 * SUBGRID), BF16),
        ),
    )
    returned = lax.all_to_all(narrowed, "facet", split_axis=0, concat_axis=0, tiled=True)
    partial = call(
        gather_kernel,
        "gather",
        (subgrid_rows, facet_offsets),
        (returned,),
        shape((parts, 2, rows, CONTRIB), BF16),
    )
    shared = lax.all_to_all(partial, "freq", split_axis=0, concat_axis=0, tiled=True)
    image_residual = call(
        functools.partial(image_kernel, subgrids),
        "image",
        (column_offset, facet_offsets),
        (shared,),
        shape(facet_image.shape, BF16),
        (pltpu.VMEM((far_rows, 2 * LANES), BF16),),
    )
    return (image_residual, residual_vis)


def solution(mesh):
    return jax.shard_map(
        on_device,
        mesh=mesh,
        in_specs=(
            P("facet", None, "freq", None),
            P(),
            P(),
            P(),
            P(None, ("freq", "facet"), None, None),
            P(None, ("freq", "facet"), None, None),
        ),
        out_specs=(P("facet", None, "freq", None), P(None, ("freq", "facet"), None, None)),
        check_vma=False,
    )
```

```python
import functools
import math

import jax
import jax.numpy as jnp
from jax import lax
from jax.experimental import pallas as pl
from jax.experimental.pallas import tpu as pltpu
from jax.sharding import PartitionSpec as P

IMAGE = 32768
CONTRIB = 128
SUBGRID = 256
PATCH = 32
SIDE = 8
STEP = 128
PERIOD = 256
LANES = 128
MASK = IMAGE - 1

F32 = jnp.float32
BF16 = jnp.bfloat16


def iota(shape, axis):
    return lax.broadcasted_iota(jnp.int32, shape, axis)


def cis(turns):
    turns = turns & MASK
    quarter = (turns + IMAGE // 8) >> 13
    x = (turns - (quarter << 13)).astype(F32) * (2.0 * math.pi / IMAGE)
    x2 = x * x
    sine = x * (1.0 + x2 * (-1.0 / 6 + x2 * (1.0 / 120 - x2 * (1.0 / 5040))))
    cosine = 1.0 + x2 * (-0.5 + x2 * (1.0 / 24 + x2 * (-1.0 / 720 + x2 * (1.0 / 40320))))
    odd = (quarter & 1) == 1
    real = jnp.where(odd, sine, cosine)
    imag = jnp.where(odd, cosine, sine)
    real = jnp.where(((quarter + 1) & 2) == 2, -real, real)
    imag = jnp.where((quarter & 2) == 2, -imag, imag)
    return real, imag


def times(ar, ai, br, bi):
    return ar * br - ai * bi, ar * bi + ai * br


def block(rows):
    return jnp.concatenate([jnp.concatenate(row, axis=1) for row in rows], axis=0)


def dot(left, right):
    return lax.dot_general(left, right, (((1,), (0,)), ((), ())), preferred_element_type=F32)


def dot_t(left, right):
    return lax.dot_general(left, right, (((1,), (1,)), ((), ())), preferred_element_type=F32)


def dot_0(left, right):
    return lax.dot_general(left, right, (((0,), (0,)), ((), ())), preferred_element_type=F32)


def column_tables(column, first, extent):
    col_step = IMAGE // extent
    far_count = extent // LANES
    near = ((column + col_step * iota((LANES, CONTRIB), 1)) & MASK) * iota((LANES, CONTRIB), 0)
    shape = (far_count, CONTRIB)
    far = ((column + col_step * iota(shape, 1)) & MASK) * ((first + LANES * iota(shape, 0)) & MASK)
    return cis(-near), cis(-far)


def near_weights(near):
    real, imag = near
    return block([[real, imag], [-imag, real]]).astype(BF16)


def column_kernel(column_ref, offsets_ref, image_ref, out_ref, left_ref):
    rows, extent = image_ref.shape[2:]
    far_count = extent // LANES
    first = offsets_ref[1, lax.axis_index("facet")]
    near, (far_real, far_imag) = column_tables(column_ref[0], first, extent)
    for y1 in range(far_count):
        here = pl.ds(y1 * rows, rows)
        there = pl.ds(y1 * LANES, LANES)
        left_ref[here, :LANES] = image_ref[0, 0, :, there]
        left_ref[here, LANES:] = image_ref[0, 1, :, there]
    value = dot(left_ref[...], near_weights(near))
    real = jnp.zeros((rows, CONTRIB), F32)
    imag = jnp.zeros((rows, CONTRIB), F32)
    for y1 in range(far_count):
        part = value[y1 * rows : (y1 + 1) * rows]
        pr, pi = times(
            part[:, :CONTRIB], part[:, CONTRIB:], far_real[y1 : y1 + 1], far_imag[y1 : y1 + 1]
        )
        real += pr
        imag += pi
    scale = 1.0 / math.sqrt(extent)
    both = jnp.stack([(real * scale).astype(BF16), (imag * scale).astype(BF16)])
    for copy in range(out_ref.shape[0]):
        out_ref[copy] = both


def row_tables(starts_ref, offsets_ref, facets, block_rows, facet_rows):
    half_step = IMAGE // facet_rows // 2
    owners = SUBGRID // block_rows
    index = lax.axis_index("freq") * lax.axis_size("facet") + lax.axis_index("facet")
    start = starts_ref[index // owners]
    shape = (block_rows, facet_rows)
    row = (index % owners) * block_rows + iota(shape, 0)
    half = (STEP // 2) * row - half_step * iota(shape, 1)
    top = cis(CONTRIB * half)[1]
    low = cis(half)[1]
    even = (half & (IMAGE // 2 - 1)) == 0
    limit = jnp.where((half & MASK) == 0, float(CONTRIB), -float(CONTRIB))
    kernel = jnp.where(even, limit, top / jnp.where(even, 1.0, low))
    tables = []
    for f in range(facets):
        first = offsets_ref[0, f]
        shift = (facet_rows - first % facet_rows) % facet_rows
        rolled = pltpu.roll(kernel, shift, 1)
        place = first + iota(shape, 1)
        half = (STEP // 2) * row - half_step * (place & (facet_rows - 1))
        turns = row * first - start * (place & MASK) + (CONTRIB - 1) * half
        real, imag = cis(turns)
        tables.append((rolled * real, rolled * imag))
    return tables


def patch_rows_of(row, stride):
    turn = IMAGE // PERIOD
    base = cis(iota((8, row.shape[1]), 0) * row * turn)
    blocks = [base]
    for _ in range(PATCH // 8 - 1):
        blocks.append(times(*blocks[-1], *stride))
    return (
        jnp.concatenate([b[0] for b in blocks], axis=0),
        jnp.concatenate([b[1] for b in blocks], axis=0),
    )


def grid_kernel(
    starts_ref,
    offsets_ref,
    own_ref,
    other_ref,
    coords_ref,
    seen_ref,
    keep_ref,
    give_ref,
    res_ref,
    pieces_ref,
    rows_ref,
    left_ref,
    back_ref,
    narrow_ref,
):
    facets = offsets_ref.shape[1]
    pairs = own_ref.shape[0] // facets
    piece_rows = own_ref.shape[2]
    facet_rows = 2 * pairs * piece_rows
    patch_rows = coords_ref.shape[1]
    block_rows = patch_rows * PATCH
    vis = coords_ref.shape[3]
    turn = IMAGE // PERIOD
    core = lax.axis_index("freq") % 2
    for f in range(facets):
        for y in range(pairs):
            for ri in range(2):
                pieces_ref[f, ri, 2 * y + core] = own_ref[y * facets + f, ri]
                pieces_ref[f, ri, 2 * y + 1 - core] = other_ref[y * facets + f, ri]
    tables = row_tables(starts_ref, offsets_ref, facets, block_rows, facet_rows)
    scale = 1.0 / math.sqrt(facet_rows)
    for f, (mr, mi) in enumerate(tables):
        mr, mi = mr.astype(BF16), mi.astype(BF16)
        rows_ref[f] = block([[mr, -mi], [mi, mr]])
        part = dot(rows_ref[f], pieces_ref[f].reshape(2 * facet_rows, CONTRIB)) * scale
        here = pl.ds(f * block_rows, block_rows)
        left_ref[here, :CONTRIB] = part[:block_rows].astype(BF16)
        left_ref[here, CONTRIB:] = part[block_rows:].astype(BF16)
    shape = (facets, SUBGRID)
    firsts = jnp.zeros(shape, jnp.int32)
    for f in range(facets):
        firsts = jnp.where(iota(shape, 0) == f, offsets_ref[1, f], firsts)
    shift_real, shift_imag = cis(firsts * iota(shape, 1))
    shape = (CONTRIB, SUBGRID)
    tr, ti = cis(iota(shape, 0) * iota(shape, 1) * STEP)
    weights = block([[tr, ti], [-ti, tr]]).astype(BF16)
    wide = dot(left_ref[...], weights)
    grid_real = jnp.zeros((block_rows, SUBGRID), F32)
    grid_imag = jnp.zeros((block_rows, SUBGRID), F32)
    for f in range(facets):
        part = wide[f * block_rows : (f + 1) * block_rows]
        pr, pi = times(
            part[:, :SUBGRID], part[:, SUBGRID:], shift_real[f : f + 1], shift_imag[f : f + 1]
        )
        grid_real += pr
        grid_imag += pi
    grid_real = (grid_real * (1.0 / CONTRIB)).astype(BF16).astype(F32)
    grid_imag = (grid_imag * (1.0 / CONTRIB)).astype(BF16).astype(F32)
    group = LANES // PATCH
    own = (iota((LANES, LANES), 0) // PATCH) == (iota((LANES, LANES), 1) // PATCH)
    factor = 1.0 / math.sqrt(vis)
    for p in range(patch_rows):
        strides = [cis(coords_ref[axis, p] * (8 * turn)) for axis in range(2)]
        for h in range(SIDE // group):
            tables = []
            for axis in range(2):
                made = [
                    patch_rows_of(
                        coords_ref[axis, p, pl.ds(c, 1), :],
                        (strides[axis][0][c : c + 1], strides[axis][1][c : c + 1]),
                    )
                    for c in range(h * group, (h + 1) * group)
                ]
                tables.append(
                    tuple(jnp.concatenate([m[ri] for m in made], axis=0) for ri in range(2))
                )
            (ur, ui), (vr, vi) = tables
            cells = (slice(p * PATCH, (p + 1) * PATCH), slice(h * LANES, (h + 1) * LANES))
            mr, mi = (
                jnp.where(own, jnp.concatenate([grid[cells]] * group, axis=0), 0.0)
                for grid in (grid_real, grid_imag)
            )
            ev = jnp.concatenate([vr, vi], axis=0).astype(BF16)
            inner = dot(block([[mr, -mi], [mi, mr]]).astype(BF16), ev)
            ir, ii = times(ur, ui, inner[:LANES], inner[LANES:])
            wr, wi = [], []
            for c in range(group):
                rows = slice(c * PATCH, (c + 1) * PATCH)
                at = h * group + c
                res = []
                for ri, value in enumerate((ir, ii)):
                    model = jnp.sum(value[rows], axis=0, keepdims=True) * (1.0 / PATCH)
                    seen = seen_ref[ri, p, pl.ds(at, 1), :].astype(F32)
                    rounded = (seen - model).astype(BF16)
                    res_ref[ri, p, pl.ds(at, 1), :] = rounded
                    res.append(rounded.astype(F32))
                wr.append(res[0] * ur[rows] + res[1] * ui[rows])
                wi.append(res[1] * ur[rows] - res[0] * ui[rows])
            back = dot_t(jnp.concatenate(wr + wi, axis=0).astype(BF16), ev)
            br = back[:LANES, :LANES] + back[LANES:, LANES:]
            bi = back[LANES:, :LANES] - back[:LANES, LANES:]
            for ri, value in enumerate((br, bi)):
                value = jnp.where(own, value, 0.0)
                total = sum(value[c * PATCH : (c + 1) * PATCH] for c in range(group))
                back_ref[ri, cells[0], cells[1]] = (total * factor).astype(BF16).astype(F32)
    for f in range(facets):
        here = pl.ds(f * block_rows, block_rows)
        nr, ni = times(
            back_ref[0], back_ref[1], shift_real[f : f + 1], -shift_imag[f : f + 1]
        )
        narrow_ref[here, :SUBGRID] = nr.astype(BF16)
        narrow_ref[here, SUBGRID:] = ni.astype(BF16)
    narrowed = dot_t(narrow_ref[...], weights).astype(BF16)
    for f in range(facets):
        part = narrowed[f * block_rows : (f + 1) * block_rows]
        part = jnp.concatenate([part[:, :CONTRIB], part[:, CONTRIB:]], axis=0)
        back = (dot_0(rows_ref[f], part) * (1.0 / SUBGRID)).astype(BF16)
        pieces_ref[f] = back.reshape(2, 2 * pairs, piece_rows, CONTRIB)
        for y in range(pairs):
            for ri in range(2):
                keep_ref[y * facets + f, ri] = pieces_ref[f, ri, 2 * y + core]
                give_ref[y * facets + f, ri] = pieces_ref[f, ri, 2 * y + 1 - core]


def image_kernel(subgrids, column_ref, offsets_ref, in_ref, out_ref, left_ref):
    parts = in_ref.shape[0]
    rows, extent = out_ref.shape[2:]
    far_count = extent // LANES
    first = offsets_ref[1, lax.axis_index("facet")]
    near, (far_real, far_imag) = column_tables(column_ref[0], first, extent)
    scale = 1.0 / math.sqrt(subgrids * CONTRIB)
    real, imag = (
        sum(in_ref[q, ri].astype(F32) for q in range(parts)) * scale for ri in range(2)
    )
    for y1 in range(far_count):
        here = pl.ds(y1 * rows, rows)
        ar, ai = times(real, imag, far_real[y1 : y1 + 1], -far_imag[y1 : y1 + 1])
        left_ref[here, :CONTRIB] = ar.astype(BF16)
        left_ref[here, CONTRIB:] = ai.astype(BF16)
    value = dot_t(left_ref[...], near_weights(near)) * (1.0 / math.sqrt(CONTRIB))
    value = value.astype(BF16)
    for y1 in range(far_count):
        for ri in range(2):
            out_ref[0, ri, :, pl.ds(y1 * LANES, LANES)] = value[
                y1 * rows : (y1 + 1) * rows, ri * LANES : (ri + 1) * LANES
            ]


def call(kernel, name, small, operands, outs, scratch=()):
    smem = pl.BlockSpec(memory_space=pltpu.SMEM)
    vmem = pl.BlockSpec(memory_space=pltpu.VMEM)
    return pl.pallas_call(
        kernel,
        name=name,
        out_shape=outs,
        in_specs=[smem] * len(small) + [vmem] * len(operands),
        out_specs=jax.tree.map(lambda _: vmem, outs),
        scratch_shapes=list(scratch),
        compiler_params=pltpu.CompilerParams(vmem_limit_bytes=40 * 1024 * 1024),
    )(*small, *operands)


def on_device(facet_image, facet_offsets, subgrid_rows, column_offset, uv_coords, observed):
    shape = jax.ShapeDtypeStruct
    rows, extent = facet_image.shape[2:]
    facets = lax.axis_size("facet")
    parts = lax.axis_size("freq")
    subgrids = subgrid_rows.shape[0]
    block_rows = uv_coords.shape[1] * PATCH
    far_rows = extent // LANES * rows
    members = facets * parts // 2
    groups = [
        [(2 * y + c) * facets + f for y in range(parts // 2) for f in range(facets)]
        for c in range(2)
    ]
    offsets = facet_offsets.T

    def exchange(value):
        return lax.all_to_all(
            value, ("freq", "facet"), split_axis=0, concat_axis=0, axis_index_groups=groups, tiled=True
        )

    def swap(value):
        return lax.ppermute(value, "freq", [(q, q ^ 1) for q in range(parts)])

    pieces = shape((members, 2, rows, CONTRIB), BF16)
    transformed = call(
        column_kernel,
        "column",
        (column_offset, offsets),
        (facet_image,),
        pieces,
        (pltpu.VMEM((far_rows, 2 * LANES), BF16),),
    )
    own = exchange(transformed)
    other = swap(own)
    keep, give, residual_vis = call(
        grid_kernel,
        "grid",
        (subgrid_rows, offsets),
        (own, other, uv_coords, observed),
        (pieces, pieces, shape(observed.shape, BF16)),
        (
            pltpu.VMEM((facets, 2, parts, rows, CONTRIB), BF16),
            pltpu.VMEM((facets, 2 * block_rows, 2 * parts * rows), BF16),
            pltpu.VMEM((facets * block_rows, 2 * CONTRIB), BF16),
            pltpu.VMEM((2, block_rows, SUBGRID), F32),
            pltpu.VMEM((facets * block_rows, 2 * SUBGRID), BF16),
        ),
    )
    partial = (keep.astype(F32) + swap(give).astype(F32)).astype(BF16)
    image_residual = call(
        functools.partial(image_kernel, subgrids),
        "image",
        (column_offset, offsets),
        (exchange(partial),),
        shape(facet_image.shape, BF16),
        (pltpu.VMEM((far_rows, 2 * LANES), BF16),),
    )
    return (image_residual, residual_vis)


def solution(mesh):
    return jax.shard_map(
        on_device,
        mesh=mesh,
        in_specs=(
            P("facet", None, "freq", None),
            P(),
            P(),
            P(),
            P(None, ("freq", "facet"), None, None),
            P(None, ("freq", "facet"), None, None),
        ),
        out_specs=(P("facet", None, "freq", None), P(None, ("freq", "facet"), None, None)),
        check_vma=False,
    )
```

```python
import functools
import math

import jax
import jax.numpy as jnp
from jax import lax
from jax.experimental import pallas as pl
from jax.experimental.pallas import tpu as pltpu
from jax.sharding import PartitionSpec as P

IMAGE = 32768
CONTRIB = 128
SUBGRID = 256
PATCH = 32
SIDE = 8
STEP = 128
PERIOD = 256
LANES = 128
MASK = IMAGE - 1

F32 = jnp.float32
BF16 = jnp.bfloat16


def iota(shape, axis):
    return lax.broadcasted_iota(jnp.int32, shape, axis)


def cis(turns):
    turns = turns & MASK
    quarter = (turns + IMAGE // 8) >> 13
    x = (turns - (quarter << 13)).astype(F32) * (2.0 * math.pi / IMAGE)
    x2 = x * x
    sine = x * (1.0 + x2 * (-1.0 / 6 + x2 * (1.0 / 120 - x2 * (1.0 / 5040))))
    cosine = 1.0 + x2 * (-0.5 + x2 * (1.0 / 24 + x2 * (-1.0 / 720 + x2 * (1.0 / 40320))))
    odd = (quarter & 1) == 1
    real = jnp.where(odd, sine, cosine)
    imag = jnp.where(odd, cosine, sine)
    real = jnp.where(((quarter + 1) & 2) == 2, -real, real)
    imag = jnp.where((quarter & 2) == 2, -imag, imag)
    return real, imag


def times(ar, ai, br, bi):
    return ar * br - ai * bi, ar * bi + ai * br


def block(rows):
    return jnp.concatenate([jnp.concatenate(row, axis=1) for row in rows], axis=0)


def dot(left, right):
    return lax.dot_general(left, right, (((1,), (0,)), ((), ())), preferred_element_type=F32)


def dot_t(left, right):
    return lax.dot_general(left, right, (((1,), (1,)), ((), ())), preferred_element_type=F32)


def dot_0(left, right):
    return lax.dot_general(left, right, (((0,), (0,)), ((), ())), preferred_element_type=F32)


def column_tables(column, first, extent):
    col_step = IMAGE // extent
    far_count = extent // LANES
    near = ((column + col_step * iota((LANES, CONTRIB), 1)) & MASK) * iota((LANES, CONTRIB), 0)
    shape = (far_count, CONTRIB)
    far = ((column + col_step * iota(shape, 1)) & MASK) * ((first + LANES * iota(shape, 0)) & MASK)
    return cis(-near), cis(-far)


def near_weights(near):
    real, imag = near
    return block([[real, imag], [-imag, real]]).astype(BF16)


def column_kernel(column_ref, offsets_ref, image_ref, out_ref, left_ref):
    rows, extent = image_ref.shape[2:]
    far_count = extent // LANES
    first = offsets_ref[1, lax.axis_index("facet")]
    near, (far_real, far_imag) = column_tables(column_ref[0], first, extent)
    for y1 in range(far_count):
        here = pl.ds(y1 * rows, rows)
        there = pl.ds(y1 * LANES, LANES)
        left_ref[here, :LANES] = image_ref[0, 0, :, there]
        left_ref[here, LANES:] = image_ref[0, 1, :, there]
    value = dot(left_ref[...], near_weights(near))
    real = jnp.zeros((rows, CONTRIB), F32)
    imag = jnp.zeros((rows, CONTRIB), F32)
    for y1 in range(far_count):
        part = value[y1 * rows : (y1 + 1) * rows]
        pr, pi = times(
            part[:, :CONTRIB], part[:, CONTRIB:], far_real[y1 : y1 + 1], far_imag[y1 : y1 + 1]
        )
        real += pr
        imag += pi
    scale = 1.0 / math.sqrt(extent)
    both = jnp.stack([(real * scale).astype(BF16), (imag * scale).astype(BF16)])
    for copy in range(out_ref.shape[0]):
        out_ref[copy] = both


def row_tables(starts_ref, offsets_ref, facets, block_rows, facet_rows):
    half_step = IMAGE // facet_rows // 2
    owners = SUBGRID // block_rows
    index = lax.axis_index("freq") * lax.axis_size("facet") + lax.axis_index("facet")
    start = starts_ref[index // owners]
    shape = (block_rows, facet_rows)
    row = (index % owners) * block_rows + iota(shape, 0)
    half = (STEP // 2) * row - half_step * iota(shape, 1)
    top = cis(CONTRIB * half)[1]
    low = cis(half)[1]
    even = (half & (IMAGE // 2 - 1)) == 0
    limit = jnp.where((half & MASK) == 0, float(CONTRIB), -float(CONTRIB))
    kernel = jnp.where(even, limit, top / jnp.where(even, 1.0, low))
    tables = []
    for f in range(facets):
        first = offsets_ref[0, f]
        shift = (facet_rows - first % facet_rows) % facet_rows
        rolled = pltpu.roll(kernel, shift, 1)
        place = first + iota(shape, 1)
        half = (STEP // 2) * row - half_step * (place & (facet_rows - 1))
        turns = row * first - start * (place & MASK) + (CONTRIB - 1) * half
        real, imag = cis(turns)
        tables.append((rolled * real, rolled * imag))
    return tables


def patch_rows_of(row, stride):
    turn = IMAGE // PERIOD
    base = cis(iota((8, row.shape[1]), 0) * row * turn)
    blocks = [base]
    for _ in range(PATCH // 8 - 1):
        blocks.append(times(*blocks[-1], *stride))
    return (
        jnp.concatenate([b[0] for b in blocks], axis=0),
        jnp.concatenate([b[1] for b in blocks], axis=0),
    )


def table_kernel(
    starts_ref, offsets_ref, coords_ref, rows_ref, weights_ref, shift_ref, eu_ref, ev_ref
):
    facets = offsets_ref.shape[1]
    patch_rows = coords_ref.shape[1]
    block_rows = patch_rows * PATCH
    turn = IMAGE // PERIOD
    tables = row_tables(starts_ref, offsets_ref, facets, block_rows, rows_ref.shape[2] // 2)
    for f, (mr, mi) in enumerate(tables):
        mr, mi = mr.astype(BF16), mi.astype(BF16)
        rows_ref[f] = block([[mr, -mi], [mi, mr]])
    shape = (facets, SUBGRID)
    firsts = jnp.zeros(shape, jnp.int32)
    for f in range(facets):
        firsts = jnp.where(iota(shape, 0) == f, offsets_ref[1, f], firsts)
    shift_ref[0], shift_ref[1] = cis(firsts * iota(shape, 1))
    shape = (CONTRIB, SUBGRID)
    tr, ti = cis(iota(shape, 0) * iota(shape, 1) * STEP)
    weights_ref[...] = block([[tr, ti], [-ti, tr]]).astype(BF16)
    group = LANES // PATCH
    for p in range(patch_rows):
        for axis, ref in enumerate((eu_ref, ev_ref)):
            sr, si = cis(coords_ref[axis, p] * (8 * turn))
            for c in range(SIDE):
                made = patch_rows_of(
                    coords_ref[axis, p, pl.ds(c, 1), :], (sr[c : c + 1], si[c : c + 1])
                )
                for ri in range(2):
                    here = pl.ds(ri * LANES + c % group * PATCH, PATCH)
                    ref[p, c // group, here, :] = made[ri].astype(BF16)


def grid_kernel(
    own_ref,
    other_ref,
    rows_ref,
    weights_ref,
    shift_ref,
    eu_ref,
    ev_ref,
    seen_ref,
    keep_ref,
    give_ref,
    res_ref,
    pieces_ref,
    left_ref,
    back_ref,
    narrow_ref,
):
    facets = rows_ref.shape[0]
    pairs = own_ref.shape[0] // facets
    piece_rows = own_ref.shape[2]
    facet_rows = 2 * pairs * piece_rows
    patch_rows = seen_ref.shape[1]
    block_rows = patch_rows * PATCH
    vis = seen_ref.shape[3]
    core = lax.axis_index("freq") % 2
    for f in range(facets):
        for y in range(pairs):
            for ri in range(2):
                pieces_ref[f, ri, 2 * y + core] = own_ref[y * facets + f, ri]
                pieces_ref[f, ri, 2 * y + 1 - core] = other_ref[y * facets + f, ri]
    scale = 1.0 / math.sqrt(facet_rows)
    for f in range(facets):
        part = dot(rows_ref[f], pieces_ref[f].reshape(2 * facet_rows, CONTRIB)) * scale
        here = pl.ds(f * block_rows, block_rows)
        left_ref[here, :CONTRIB] = part[:block_rows].astype(BF16)
        left_ref[here, CONTRIB:] = part[block_rows:].astype(BF16)
    weights = weights_ref[...]
    shift_real, shift_imag = shift_ref[0], shift_ref[1]
    wide = dot(left_ref[...], weights)
    grid_real = jnp.zeros((block_rows, SUBGRID), F32)
    grid_imag = jnp.zeros((block_rows, SUBGRID), F32)
    for f in range(facets):
        part = wide[f * block_rows : (f + 1) * block_rows]
        pr, pi = times(
            part[:, :SUBGRID], part[:, SUBGRID:], shift_real[f : f + 1], shift_imag[f : f + 1]
        )
        grid_real += pr
        grid_imag += pi
    grid_real = (grid_real * (1.0 / CONTRIB)).astype(BF16).astype(F32)
    grid_imag = (grid_imag * (1.0 / CONTRIB)).astype(BF16).astype(F32)
    group = LANES // PATCH
    own = (iota((LANES, LANES), 0) // PATCH) == (iota((LANES, LANES), 1) // PATCH)
    factor = 1.0 / math.sqrt(vis)
    for p in range(patch_rows):
        for h in range(SIDE // group):
            ur, ui = eu_ref[p, h, :LANES].astype(F32), eu_ref[p, h, LANES:].astype(F32)
            cells = (slice(p * PATCH, (p + 1) * PATCH), slice(h * LANES, (h + 1) * LANES))
            mr, mi = (
                jnp.where(own, jnp.concatenate([grid[cells]] * group, axis=0), 0.0)
                for grid in (grid_real, grid_imag)
            )
            ev = ev_ref[p, h]
            inner = dot(block([[mr, -mi], [mi, mr]]).astype(BF16), ev)
            ir, ii = times(ur, ui, inner[:LANES], inner[LANES:])
            wr, wi = [], []
            for c in range(group):
                rows = slice(c * PATCH, (c + 1) * PATCH)
                at = h * group + c
                res = []
                for ri, value in enumerate((ir, ii)):
                    model = jnp.sum(value[rows], axis=0, keepdims=True) * (1.0 / PATCH)
                    seen = seen_ref[ri, p, pl.ds(at, 1), :].astype(F32)
                    rounded = (seen - model).astype(BF16)
                    res_ref[ri, p, pl.ds(at, 1), :] = rounded
                    res.append(rounded.astype(F32))
                wr.append(res[0] * ur[rows] + res[1] * ui[rows])
                wi.append(res[1] * ur[rows] - res[0] * ui[rows])
            back = dot_t(jnp.concatenate(wr + wi, axis=0).astype(BF16), ev)
            br = back[:LANES, :LANES] + back[LANES:, LANES:]
            bi = back[LANES:, :LANES] - back[:LANES, LANES:]
            for ri, value in enumerate((br, bi)):
                value = jnp.where(own, value, 0.0)
                total = sum(value[c * PATCH : (c + 1) * PATCH] for c in range(group))
                back_ref[ri, cells[0], cells[1]] = (total * factor).astype(BF16).astype(F32)
    for f in range(facets):
        here = pl.ds(f * block_rows, block_rows)
        nr, ni = times(
            back_ref[0], back_ref[1], shift_real[f : f + 1], -shift_imag[f : f + 1]
        )
        narrow_ref[here, :SUBGRID] = nr.astype(BF16)
        narrow_ref[here, SUBGRID:] = ni.astype(BF16)
    narrowed = dot_t(narrow_ref[...], weights).astype(BF16)
    for f in range(facets):
        part = narrowed[f * block_rows : (f + 1) * block_rows]
        part = jnp.concatenate([part[:, :CONTRIB], part[:, CONTRIB:]], axis=0)
        back = (dot_0(rows_ref[f], part) * (1.0 / SUBGRID)).astype(BF16)
        pieces_ref[f] = back.reshape(2, 2 * pairs, piece_rows, CONTRIB)
        for y in range(pairs):
            for ri in range(2):
                keep_ref[y * facets + f, ri] = pieces_ref[f, ri, 2 * y + core]
                give_ref[y * facets + f, ri] = pieces_ref[f, ri, 2 * y + 1 - core]


def image_kernel(subgrids, column_ref, offsets_ref, in_ref, out_ref, left_ref):
    parts = in_ref.shape[0]
    rows, extent = out_ref.shape[2:]
    far_count = extent // LANES
    first = offsets_ref[1, lax.axis_index("facet")]
    near, (far_real, far_imag) = column_tables(column_ref[0], first, extent)
    scale = 1.0 / math.sqrt(subgrids * CONTRIB)
    real, imag = (
        sum(in_ref[q, ri].astype(F32) for q in range(parts)) * scale for ri in range(2)
    )
    for y1 in range(far_count):
        here = pl.ds(y1 * rows, rows)
        ar, ai = times(real, imag, far_real[y1 : y1 + 1], -far_imag[y1 : y1 + 1])
        left_ref[here, :CONTRIB] = ar.astype(BF16)
        left_ref[here, CONTRIB:] = ai.astype(BF16)
    value = dot_t(left_ref[...], near_weights(near)) * (1.0 / math.sqrt(CONTRIB))
    value = value.astype(BF16)
    for y1 in range(far_count):
        for ri in range(2):
            out_ref[0, ri, :, pl.ds(y1 * LANES, LANES)] = value[
                y1 * rows : (y1 + 1) * rows, ri * LANES : (ri + 1) * LANES
            ]


def call(kernel, name, small, operands, outs, scratch=()):
    smem = pl.BlockSpec(memory_space=pltpu.SMEM)
    vmem = pl.BlockSpec(memory_space=pltpu.VMEM)
    return pl.pallas_call(
        kernel,
        name=name,
        out_shape=outs,
        in_specs=[smem] * len(small) + [vmem] * len(operands),
        out_specs=jax.tree.map(lambda _: vmem, outs),
        scratch_shapes=list(scratch),
        compiler_params=pltpu.CompilerParams(vmem_limit_bytes=40 * 1024 * 1024),
    )(*small, *operands)


def on_device(facet_image, facet_offsets, subgrid_rows, column_offset, uv_coords, observed):
    shape = jax.ShapeDtypeStruct
    rows, extent = facet_image.shape[2:]
    facets = lax.axis_size("facet")
    parts = lax.axis_size("freq")
    subgrids = subgrid_rows.shape[0]
    block_rows = uv_coords.shape[1] * PATCH
    far_rows = extent // LANES * rows
    members = facets * parts // 2
    groups = [
        [(2 * y + c) * facets + f for y in range(parts // 2) for f in range(facets)]
        for c in range(2)
    ]
    offsets = facet_offsets.T

    def exchange(value):
        return lax.all_to_all(
            value, ("freq", "facet"), split_axis=0, concat_axis=0, axis_index_groups=groups, tiled=True
        )

    def swap(value):
        return lax.ppermute(value, "freq", [(q, q ^ 1) for q in range(parts)])

    pieces = shape((members, 2, rows, CONTRIB), BF16)
    transformed = call(
        column_kernel,
        "column",
        (column_offset, offsets),
        (facet_image,),
        pieces,
        (pltpu.VMEM((far_rows, 2 * LANES), BF16),),
    )
    own = exchange(transformed)
    other = swap(own)
    patch_rows, vis = uv_coords.shape[1], uv_coords.shape[3]
    halves = SIDE * PATCH // LANES
    tables = call(
        table_kernel,
        "tables",
        (subgrid_rows, offsets),
        (uv_coords,),
        (
            shape((facets, 2 * block_rows, 2 * parts * rows), BF16),
            shape((2 * CONTRIB, 2 * SUBGRID), BF16),
            shape((2, facets, SUBGRID), F32),
            shape((patch_rows, halves, 2 * LANES, vis), BF16),
            shape((patch_rows, halves, 2 * LANES, vis), BF16),
        ),
    )
    keep, give, residual_vis = call(
        grid_kernel,
        "grid",
        (),
        (own, other, *tables, observed),
        (pieces, pieces, shape(observed.shape, BF16)),
        (
            pltpu.VMEM((facets, 2, parts, rows, CONTRIB), BF16),
            pltpu.VMEM((facets * block_rows, 2 * CONTRIB), BF16),
            pltpu.VMEM((2, block_rows, SUBGRID), F32),
            pltpu.VMEM((facets * block_rows, 2 * SUBGRID), BF16),
        ),
    )
    partial = (keep.astype(F32) + swap(give).astype(F32)).astype(BF16)
    image_residual = call(
        functools.partial(image_kernel, subgrids),
        "image",
        (column_offset, offsets),
        (exchange(partial),),
        shape(facet_image.shape, BF16),
        (pltpu.VMEM((far_rows, 2 * LANES), BF16),),
    )
    return (image_residual, residual_vis)


def solution(mesh):
    return jax.shard_map(
        on_device,
        mesh=mesh,
        in_specs=(
            P("facet", None, "freq", None),
            P(),
            P(),
            P(),
            P(None, ("freq", "facet"), None, None),
            P(None, ("freq", "facet"), None, None),
        ),
        out_specs=(P("facet", None, "freq", None), P(None, ("freq", "facet"), None, None)),
        check_vma=False,
    )
```

```python
import functools
import math

import jax
import jax.numpy as jnp
from jax import lax
from jax.experimental import pallas as pl
from jax.experimental.pallas import tpu as pltpu
from jax.sharding import PartitionSpec as P

IMAGE = 32768
CONTRIB = 128
SUBGRID = 256
PATCH = 32
SIDE = 8
STEP = 128
PERIOD = 256
LANES = 128
MASK = IMAGE - 1

F32 = jnp.float32
BF16 = jnp.bfloat16


def iota(shape, axis):
    return lax.broadcasted_iota(jnp.int32, shape, axis)


def cis(turns):
    turns = turns & MASK
    quarter = (turns + IMAGE // 8) >> 13
    x = (turns - (quarter << 13)).astype(F32) * (2.0 * math.pi / IMAGE)
    x2 = x * x
    sine = x * (1.0 + x2 * (-1.0 / 6 + x2 * (1.0 / 120 - x2 * (1.0 / 5040))))
    cosine = 1.0 + x2 * (-0.5 + x2 * (1.0 / 24 + x2 * (-1.0 / 720 + x2 * (1.0 / 40320))))
    odd = (quarter & 1) == 1
    real = jnp.where(odd, sine, cosine)
    imag = jnp.where(odd, cosine, sine)
    real = jnp.where(((quarter + 1) & 2) == 2, -real, real)
    imag = jnp.where((quarter & 2) == 2, -imag, imag)
    return real, imag


def times(ar, ai, br, bi):
    return ar * br - ai * bi, ar * bi + ai * br


def times_conj(ar, ai, br, bi):
    return ar * br + ai * bi, ai * br - ar * bi


def block(rows):
    return jnp.concatenate([jnp.concatenate(row, axis=1) for row in rows], axis=0)


def dot(left, right):
    return lax.dot_general(left, right, (((1,), (0,)), ((), ())), preferred_element_type=F32)


def dot_t(left, right):
    return lax.dot_general(left, right, (((1,), (1,)), ((), ())), preferred_element_type=F32)


def dot_0(left, right):
    return lax.dot_general(left, right, (((0,), (0,)), ((), ())), preferred_element_type=F32)


def column_tables(column, first, extent):
    col_step = IMAGE // extent
    far_count = extent // LANES
    near = ((column + col_step * iota((LANES, CONTRIB), 1)) & MASK) * iota((LANES, CONTRIB), 0)
    shape = (far_count, CONTRIB)
    far = ((column + col_step * iota(shape, 1)) & MASK) * ((first + LANES * iota(shape, 0)) & MASK)
    return cis(-near), cis(-far)


def near_weights(near):
    real, imag = near
    return block([[real, imag], [-imag, real]]).astype(BF16)


CHUNK = 8
GROUP = LANES // PATCH


def cell_of(lane):
    half, inside = lane // LANES, lane % LANES
    return (half * GROUP + inside % GROUP) * PATCH + inside // GROUP


def column_kernel(
    column_ref,
    offsets_hbm,
    image_hbm,
    coords_hbm,
    seen_hbm,
    out_ref,
    near_ref,
    far_ref,
    weights_ref,
    coords_ref,
    seen_ref,
    left_ref,
    offsets_ref,
    small_sem,
    image_sem,
    later_sem,
):
    rows, extent = image_hbm.shape[2:]
    far_count = extent // LANES
    small = pltpu.make_async_copy(offsets_hbm, offsets_ref, small_sem)
    small.start()
    large = []
    for ri in range(2):
        copy = pltpu.make_async_copy(image_hbm.at[0, ri], left_ref.at[ri], image_sem.at[ri])
        copy.start()
        large.append(copy)
    later = [
        pltpu.make_async_copy(coords_hbm, coords_ref, later_sem.at[0]),
        pltpu.make_async_copy(seen_hbm, seen_ref, later_sem.at[1]),
    ]
    for copy in later:
        copy.start()
    for h in range(SUBGRID // LANES):
        shape = (CONTRIB, LANES)
        tr, ti = cis(iota(shape, 0) * cell_of(iota(shape, 1) + h * LANES) * STEP)
        weights_ref[:, 2 * h * LANES : 2 * (h + 1) * LANES] = block([[tr, ti], [-ti, tr]]).astype(BF16)
    small.wait()
    first = offsets_ref[1, lax.axis_index("facet")]
    near, far = column_tables(column_ref[0], first, extent)
    near_ref[...] = near_weights(near)
    far_ref[0], far_ref[1] = far
    real = jnp.zeros((rows, CONTRIB), F32)
    imag = jnp.zeros((rows, CONTRIB), F32)
    for copy in large:
        copy.wait()
    left = [
        jnp.concatenate([left_ref[ri, :, pl.ds(y1 * LANES, LANES)] for ri in range(2)], axis=1)
        for y1 in range(far_count)
    ]
    value = dot(jnp.concatenate(left, axis=0), near_ref[...])
    for y1 in range(far_count):
        part = value[y1 * rows : (y1 + 1) * rows]
        here = slice(y1, y1 + 1)
        pr, pi = times(part[:, :CONTRIB], part[:, CONTRIB:], far[0][here], far[1][here])
        real += pr
        imag += pi
    scale = 1.0 / math.sqrt(extent)
    both = jnp.stack([(real * scale).astype(BF16), (imag * scale).astype(BF16)])
    for member in range(out_ref.shape[0]):
        out_ref[member] = both
    for copy in later:
        copy.wait()


def row_tables(starts_ref, offsets_ref, facets, block_rows, facet_rows):
    half_step = IMAGE // facet_rows // 2
    owners = SUBGRID // block_rows
    index = lax.axis_index("freq") * lax.axis_size("facet") + lax.axis_index("facet")
    start = starts_ref[index // owners]
    shape = (block_rows, facet_rows)
    row = (index % owners) * block_rows + iota(shape, 0)
    half = (STEP // 2) * row - half_step * iota(shape, 1)
    top = cis(CONTRIB * half)[1]
    low = cis(half)[1]
    even = (half & (IMAGE // 2 - 1)) == 0
    limit = jnp.where((half & MASK) == 0, float(CONTRIB), -float(CONTRIB))
    kernel = jnp.where(even, limit, top / jnp.where(even, 1.0, low)) * (1.0 / math.sqrt(facet_rows))
    by_place = (facets, facet_rows)
    by_row = (block_rows, LANES)
    firsts = jnp.zeros(by_place, jnp.int32)
    lane_firsts = jnp.zeros(by_row, jnp.int32)
    for f in range(facets):
        firsts = jnp.where(iota(by_place, 0) == f, offsets_ref[0, f], firsts)
        lane_firsts = jnp.where(iota(by_row, 1) == f, offsets_ref[0, f], lane_firsts)
    place = firsts + iota(by_place, 1)
    place_real, place_imag = cis(
        -start * (place & MASK) - (CONTRIB - 1) * half_step * (place & (facet_rows - 1))
    )
    row_real, row_imag = cis(
        ((index % owners) * block_rows + iota(by_row, 0))
        * (lane_firsts + (CONTRIB - 1) * (STEP // 2))
    )
    tables = []
    for f in range(facets):
        shift = (facet_rows - offsets_ref[0, f] % facet_rows) % facet_rows
        rolled = pltpu.roll(kernel, shift, 1)
        real, imag = times(
            row_real[:, f : f + 1], row_imag[:, f : f + 1], place_real[f : f + 1], place_imag[f : f + 1]
        )
        tables.append((rolled * real, rolled * imag))
    return tables


def patch_powers(coords):
    twice = jnp.concatenate([coords, coords], axis=0)
    real, imag = cis(twice * (IMAGE // PERIOD))
    step = times(real, imag, real, imag)
    first = iota(twice.shape, 0) < GROUP
    power = jnp.where(first, 1.0, real), jnp.where(first, 0.0, imag)
    yield power
    for _ in range(PATCH // 2 - 1):
        power = times(*power, *step)
        yield power


def table_kernel(
    starts_hbm,
    offsets_hbm,
    coords_ref,
    rows_ref,
    shift_ref,
    eu_ref,
    ev_ref,
    starts_ref,
    offsets_ref,
    sem,
):
    small = [
        pltpu.make_async_copy(starts_hbm, starts_ref, sem.at[0]),
        pltpu.make_async_copy(offsets_hbm, offsets_ref, sem.at[1]),
    ]
    for copy in small:
        copy.start()
    facets = offsets_ref.shape[1]
    patch_rows = coords_ref.shape[1]
    block_rows = patch_rows * PATCH
    for p in range(patch_rows):
        for h in range(SIDE // GROUP):
            for axis, ref in enumerate((eu_ref, ev_ref)):
                coords = coords_ref[axis, p, pl.ds(h * GROUP, GROUP), :]
                for k, power in enumerate(patch_powers(coords)):
                    for ri in range(2):
                        here = pl.ds(ri * LANES + k * 2 * GROUP, 2 * GROUP)
                        ref[p, h, here, :] = power[ri].astype(ref.dtype)
    for copy in small:
        copy.wait()
    tables = row_tables(starts_ref, offsets_ref, facets, block_rows, rows_ref.shape[2] // 2)
    for f, (mr, mi) in enumerate(tables):
        mr, mi = mr.astype(BF16), mi.astype(BF16)
        rows_ref[f] = block([[mr, -mi], [mi, mr]])
    shape = (facets, SUBGRID)
    firsts = jnp.zeros(shape, jnp.int32)
    for f in range(facets):
        firsts = jnp.where(iota(shape, 0) == f, offsets_ref[1, f], firsts)
    for ri, value in enumerate(cis(firsts * cell_of(iota(shape, 1)))):
        shift_ref[ri] = value * (1.0 / CONTRIB)


def grid_kernel(
    own_ref,
    other_ref,
    rows_ref,
    weights_ref,
    shift_ref,
    eu_ref,
    ev_ref,
    seen_ref,
    keep_ref,
    give_ref,
    res_ref,
    pieces_ref,
    left_ref,
    grid_ref,
    back_ref,
    narrow_ref,
):
    facets = rows_ref.shape[0]
    pairs = own_ref.shape[0] // facets
    piece_rows = own_ref.shape[2]
    facet_rows = 2 * pairs * piece_rows
    patch_rows = seen_ref.shape[1]
    block_rows = patch_rows * PATCH
    vis = seen_ref.shape[3]
    core = lax.axis_index("freq") % 2
    for f in range(facets):
        for y in range(pairs):
            for ri in range(2):
                pieces_ref[f, ri, 2 * y + core] = own_ref[y * facets + f, ri]
                pieces_ref[f, ri, 2 * y + 1 - core] = other_ref[y * facets + f, ri]
    for f in range(facets):
        part = dot(rows_ref[f], pieces_ref[f].reshape(2 * facet_rows, CONTRIB))
        here = pl.ds(f * block_rows, block_rows)
        left_ref[here, :CONTRIB] = part[:block_rows].astype(BF16)
        left_ref[here, CONTRIB:] = part[block_rows:].astype(BF16)
    shift_real, shift_imag = shift_ref[0], shift_ref[1]
    halves = SUBGRID // LANES
    pair = 2 * GROUP
    tile = (pair, LANES)
    same = iota(tile, 0) % GROUP == iota(tile, 1) % GROUP
    upper, lower = same & (iota(tile, 0) < GROUP), same & (iota(tile, 0) >= GROUP)
    own = iota((LANES, LANES), 0) % GROUP == iota((LANES, LANES), 1) % GROUP
    pick = (iota((PATCH, LANES), 1) // GROUP == iota((PATCH, LANES), 0)).astype(F32).astype(BF16)

    def predicted(h):
        wide = dot(left_ref[...], weights_ref[:, 2 * h * LANES : 2 * (h + 1) * LANES])
        total = [jnp.zeros((block_rows, LANES), F32)] * 2
        for f in range(facets):
            part = wide[f * block_rows : (f + 1) * block_rows]
            lanes = slice(h * LANES, (h + 1) * LANES)
            made = times(
                part[:, :LANES], part[:, LANES:], shift_real[f : f + 1, lanes], shift_imag[f : f + 1, lanes]
            )
            total = [old + new for old, new in zip(total, made)]
        for ri in range(2):
            grid_ref[h, ri] = total[ri].astype(BF16).astype(F32)

    def degrid(p, h):
        spread = []
        for ri in range(2):
            tiles = []
            for r in range(p * PATCH, (p + 1) * PATCH, 2):
                one, two = grid_ref[h, ri, pl.ds(r, 1), :], grid_ref[h, ri, pl.ds(r + 1, 1), :]
                tiles.append(jnp.where(upper, one, jnp.where(lower, two, 0.0)))
            spread.append(jnp.concatenate(tiles, axis=0).astype(BF16))
        mr, mi = spread
        return dot(block([[mr, -mi], [mi, mr]]), ev_ref[p, h])

    def weigh(p, h, inner):
        sums = [jnp.zeros((pair, vis), F32)] * 2
        for k in range(0, LANES, pair):
            made = times(
                eu_ref[p, h, pl.ds(k, pair), :],
                eu_ref[p, h, pl.ds(LANES + k, pair), :],
                inner[k : k + pair],
                inner[LANES + k : LANES + k + pair],
            )
            sums = [total + value for total, value in zip(sums, made)]
        res = []
        for ri, value in enumerate(sums):
            model = (value + pltpu.roll(value, GROUP, 0)) * (1.0 / PATCH)
            seen = seen_ref[ri, p, pl.ds(h * GROUP, GROUP), :].astype(F32)
            rounded = (jnp.concatenate([seen, seen], axis=0) - model).astype(BF16)
            res_ref[ri, p, pl.ds(h * GROUP, GROUP), :] = rounded[:GROUP]
            res.append(rounded.astype(F32))
        weighted = [[], []]
        for k in range(0, LANES, pair):
            made = times_conj(
                *res, eu_ref[p, h, pl.ds(k, pair), :], eu_ref[p, h, pl.ds(LANES + k, pair), :]
            )
            for ri in range(2):
                weighted[ri].append(made[ri])
        return jnp.concatenate(weighted[0] + weighted[1], axis=0).astype(BF16)

    def regrid(p, h, back):
        both = [
            back[:LANES, :LANES] + back[LANES:, LANES:],
            back[LANES:, :LANES] - back[:LANES, LANES:],
        ]
        both = jnp.concatenate([jnp.where(own, value, 0.0) for value in both], axis=1)
        cells = dot(pick, both.astype(BF16))
        for ri in range(2):
            back_ref[h, ri, pl.ds(p * PATCH, PATCH), :] = cells[:, ri * LANES : (ri + 1) * LANES]

    def widen(h):
        for f in range(facets):
            lanes = slice(h * LANES, (h + 1) * LANES)
            made = times_conj(
                back_ref[h, 0], back_ref[h, 1], shift_real[f : f + 1, lanes], shift_imag[f : f + 1, lanes]
            )
            for ri in range(2):
                to = (2 * h + ri) * LANES
                narrow_ref[pl.ds(f * block_rows, block_rows), to : to + LANES] = made[ri].astype(BF16)

    tasks = [(p, h) for h in range(halves) for p in range(patch_rows)]
    inner, back = {}, {}
    for h in range(halves):
        predicted(h)
        for p in range(patch_rows):
            inner[p, h] = degrid(p, h)
    for at, task in enumerate(tasks):
        left = weigh(*task, inner.pop(task))
        back[task] = dot_t(left, ev_ref[task[0], task[1]])
        if at:
            regrid(*tasks[at - 1], back.pop(tasks[at - 1]))
    regrid(*tasks[-1], back.pop(tasks[-1]))
    for h in range(halves):
        widen(h)
    narrowed = dot_t(narrow_ref[...], weights_ref[...]).astype(BF16)
    for f in range(facets):
        part = narrowed[f * block_rows : (f + 1) * block_rows]
        part = jnp.concatenate([part[:, :CONTRIB], part[:, CONTRIB:]], axis=0)
        product = dot_0(rows_ref[f], part).astype(BF16)
        pieces_ref[f] = product.reshape(2, 2 * pairs, piece_rows, CONTRIB)
        for y in range(pairs):
            for ri in range(2):
                keep_ref[y * facets + f, ri] = pieces_ref[f, ri, 2 * y + core]
                give_ref[y * facets + f, ri] = pieces_ref[f, ri, 2 * y + 1 - core]


def image_kernel(scale, in_ref, near_ref, far_ref, out_hbm, stage_ref, sem):
    parts = in_ref.shape[0]
    rows, extent = out_hbm.shape[2:]
    far_count = extent // LANES
    real, imag = (
        sum(in_ref[q, ri].astype(F32) for q in range(parts)) * scale for ri in range(2)
    )
    copies = []
    for top in range(0, far_count, CHUNK):
        left = []
        for y1 in range(top, top + CHUNK):
            ar, ai = times_conj(real, imag, far_ref[0, y1 : y1 + 1], far_ref[1, y1 : y1 + 1])
            left.append(jnp.concatenate([ar, ai], axis=1).astype(BF16))
        value = dot_t(jnp.concatenate(left, axis=0), near_ref[...])
        value = (value * (1.0 / math.sqrt(CONTRIB))).astype(BF16)
        for y1 in range(CHUNK):
            for ri in range(2):
                stage_ref[ri, :, pl.ds((top + y1) * LANES, LANES)] = value[
                    y1 * rows : (y1 + 1) * rows, ri * LANES : (ri + 1) * LANES
                ]
        for ri in range(2):
            span = pl.ds(top * LANES, CHUNK * LANES)
            copy = pltpu.make_async_copy(
                stage_ref.at[ri, :, span], out_hbm.at[0, ri, :, span], sem.at[len(copies)]
            )
            copy.start()
            copies.append(copy)
    for copy in copies:
        copy.wait()


HBM = pl.BlockSpec(memory_space=pltpu.HBM)
SMEM = pl.BlockSpec(memory_space=pltpu.SMEM)
VMEM = pl.BlockSpec(memory_space=pltpu.VMEM)


def call(kernel, name, operands, in_specs, outs, scratch=(), out_specs=None):
    return pl.pallas_call(
        kernel,
        name=name,
        out_shape=outs,
        in_specs=in_specs,
        out_specs=out_specs or jax.tree.map(lambda _: VMEM, outs),
        scratch_shapes=list(scratch),
        compiler_params=pltpu.CompilerParams(vmem_limit_bytes=40 * 1024 * 1024),
    )(*operands)


def on_device(facet_image, facet_offsets, subgrid_rows, column_offset, uv_coords, observed):
    shape = jax.ShapeDtypeStruct
    rows, extent = facet_image.shape[2:]
    facets = lax.axis_size("facet")
    parts = lax.axis_size("freq")
    subgrids = subgrid_rows.shape[0]
    block_rows = uv_coords.shape[1] * PATCH
    members = facets * parts // 2
    groups = [
        [(2 * y + c) * facets + f for y in range(parts // 2) for f in range(facets)]
        for c in range(2)
    ]
    offsets = facet_offsets.T

    def exchange(value):
        return lax.all_to_all(
            value, ("freq", "facet"), split_axis=0, concat_axis=0, axis_index_groups=groups, tiled=True
        )

    def in_hbm(value):
        return pltpu.with_memory_space_constraint(value, pltpu.HBM)

    def swap(value):
        return lax.ppermute(value, "freq", [(q, q ^ 1) for q in range(parts)])

    pieces = shape((members, 2, rows, CONTRIB), BF16)
    far_count = extent // LANES
    transformed, near, far, weights, coords, seen = call(
        column_kernel,
        "column",
        (column_offset, *map(in_hbm, (offsets, facet_image, uv_coords, observed))),
        [SMEM] + [HBM] * 4,
        (
            pieces,
            shape((2 * LANES, 2 * CONTRIB), BF16),
            shape((2, far_count, CONTRIB), F32),
            shape((2 * CONTRIB, 2 * SUBGRID), BF16),
            shape(uv_coords.shape, jnp.int32),
            shape(observed.shape, BF16),
        ),
        (
            pltpu.VMEM(facet_image.shape[1:], BF16),
            pltpu.SMEM(offsets.shape, jnp.int32),
            pltpu.SemaphoreType.DMA,
            pltpu.SemaphoreType.DMA((2,)),
            pltpu.SemaphoreType.DMA((2,)),
        ),
    )
    own = exchange(transformed)
    other = swap(own)
    patch_rows, vis = uv_coords.shape[1], uv_coords.shape[3]
    halves = SIDE * PATCH // LANES
    row_products, *tables = call(
        table_kernel,
        "tables",
        (in_hbm(subgrid_rows), in_hbm(offsets), coords),
        [HBM, HBM, VMEM],
        (
            shape((facets, 2 * block_rows, 2 * parts * rows), BF16),
            shape((2, facets, SUBGRID), F32),
            shape((patch_rows, halves, 2 * LANES, vis), F32),
            shape((patch_rows, halves, 2 * LANES, vis), BF16),
        ),
        (
            pltpu.SMEM(subgrid_rows.shape, jnp.int32),
            pltpu.SMEM(offsets.shape, jnp.int32),
            pltpu.SemaphoreType.DMA((2,)),
        ),
    )
    keep, give, residual_vis = call(
        grid_kernel,
        "grid",
        (own, other, row_products, weights, *tables, seen),
        [VMEM] * 8,
        (pieces, pieces, shape(observed.shape, BF16)),
        (
            pltpu.VMEM((facets, 2, parts, rows, CONTRIB), BF16),
            pltpu.VMEM((facets * block_rows, 2 * CONTRIB), BF16),
            pltpu.VMEM((halves, 2, block_rows, LANES), F32),
            pltpu.VMEM((halves, 2, block_rows, LANES), F32),
            pltpu.VMEM((facets * block_rows, 2 * SUBGRID), BF16),
        ),
    )
    partial = (keep.astype(F32) + swap(give).astype(F32)).astype(BF16)
    shared_scale = 1.0 / CONTRIB / math.sqrt(parts * rows)
    scale = 1.0 / (math.sqrt(vis) * SUBGRID * math.sqrt(subgrids * CONTRIB) * shared_scale)
    image_residual = call(
        functools.partial(image_kernel, scale),
        "image",
        (exchange(partial), near, far),
        [VMEM] * 3,
        shape(facet_image.shape, BF16),
        (
            pltpu.VMEM(facet_image.shape[1:], BF16),
            pltpu.SemaphoreType.DMA((2 * far_count // CHUNK,)),
        ),
        HBM,
    )
    return (image_residual, residual_vis)


def solution(mesh):
    return jax.shard_map(
        on_device,
        mesh=mesh,
        in_specs=(
            P("facet", None, "freq", None),
            P(),
            P(),
            P(),
            P(None, ("freq", "facet"), None, None),
            P(None, ("freq", "facet"), None, None),
        ),
        out_specs=(P("facet", None, "freq", None), P(None, ("freq", "facet"), None, None)),
        check_vma=False,
    )
```

```python
import functools
import math

import jax
import jax.numpy as jnp
from jax import lax
from jax.experimental import pallas as pl
from jax.experimental.pallas import tpu as pltpu
from jax.sharding import PartitionSpec as P

IMAGE = 32768
CONTRIB = 128
SUBGRID = 256
PATCH = 32
SIDE = 8
STEP = 128
PERIOD = 256
LANES = 128
MASK = IMAGE - 1

F32 = jnp.float32
BF16 = jnp.bfloat16


def iota(shape, axis):
    return lax.broadcasted_iota(jnp.int32, shape, axis)


def cis(turns):
    turns = turns & MASK
    quarter = (turns + IMAGE // 8) >> 13
    x = (turns - (quarter << 13)).astype(F32) * (2.0 * math.pi / IMAGE)
    x2 = x * x
    sine = x * (1.0 + x2 * (-1.0 / 6 + x2 * (1.0 / 120 - x2 * (1.0 / 5040))))
    cosine = 1.0 + x2 * (-0.5 + x2 * (1.0 / 24 + x2 * (-1.0 / 720 + x2 * (1.0 / 40320))))
    odd = (quarter & 1) == 1
    real = jnp.where(odd, sine, cosine)
    imag = jnp.where(odd, cosine, sine)
    real = jnp.where(((quarter + 1) & 2) == 2, -real, real)
    imag = jnp.where((quarter & 2) == 2, -imag, imag)
    return real, imag


def times(ar, ai, br, bi):
    return ar * br - ai * bi, ar * bi + ai * br


def times_conj(ar, ai, br, bi):
    return ar * br + ai * bi, ai * br - ar * bi


def block(rows):
    return jnp.concatenate([jnp.concatenate(row, axis=1) for row in rows], axis=0)


def dot(left, right):
    return lax.dot_general(left, right, (((1,), (0,)), ((), ())), preferred_element_type=F32)


def dot_t(left, right):
    return lax.dot_general(left, right, (((1,), (1,)), ((), ())), preferred_element_type=F32)


def dot_0(left, right):
    return lax.dot_general(left, right, (((0,), (0,)), ((), ())), preferred_element_type=F32)


def column_tables(column, first, extent):
    col_step = IMAGE // extent
    far_count = extent // LANES
    near = ((column + col_step * iota((LANES, CONTRIB), 1)) & MASK) * iota((LANES, CONTRIB), 0)
    shape = (far_count, CONTRIB)
    far = ((column + col_step * iota(shape, 1)) & MASK) * ((first + LANES * iota(shape, 0)) & MASK)
    return cis(-near), cis(-far)


def near_weights(near):
    real, imag = near
    return block([[real, imag], [-imag, real]]).astype(BF16)


CHUNK = 8
GROUP = LANES // PATCH


def cell_of(lane):
    half, inside = lane // LANES, lane % LANES
    return (half * GROUP + inside % GROUP) * PATCH + inside // GROUP


def column_kernel(
    column_ref,
    offsets_hbm,
    image_hbm,
    coords_hbm,
    seen_hbm,
    out_ref,
    near_ref,
    far_ref,
    weights_ref,
    coords_ref,
    seen_ref,
    left_ref,
    offsets_ref,
    small_sem,
    image_sem,
    later_sem,
):
    rows, extent = image_hbm.shape[2:]
    far_count = extent // LANES
    small = pltpu.make_async_copy(offsets_hbm, offsets_ref, small_sem)
    small.start()
    large = []
    for ri in range(2):
        copy = pltpu.make_async_copy(image_hbm.at[0, ri], left_ref.at[ri], image_sem.at[ri])
        copy.start()
        large.append(copy)
    later = [
        pltpu.make_async_copy(coords_hbm, coords_ref, later_sem.at[0]),
        pltpu.make_async_copy(seen_hbm, seen_ref, later_sem.at[1]),
    ]
    for copy in later:
        copy.start()
    for h in range(SUBGRID // LANES):
        shape = (CONTRIB, LANES)
        tr, ti = cis(iota(shape, 0) * cell_of(iota(shape, 1) + h * LANES) * STEP)
        weights_ref[:, 2 * h * LANES : 2 * (h + 1) * LANES] = block([[tr, ti], [-ti, tr]]).astype(BF16)
    small.wait()
    first = offsets_ref[1, lax.axis_index("facet")]
    near, far = column_tables(column_ref[0], first, extent)
    near_ref[...] = near_weights(near)
    far_ref[0], far_ref[1] = far
    real = jnp.zeros((rows, CONTRIB), F32)
    imag = jnp.zeros((rows, CONTRIB), F32)
    for copy in large:
        copy.wait()
    left = [
        jnp.concatenate([left_ref[ri, :, pl.ds(y1 * LANES, LANES)] for ri in range(2)], axis=1)
        for y1 in range(far_count)
    ]
    value = dot(jnp.concatenate(left, axis=0), near_ref[...])
    for y1 in range(far_count):
        part = value[y1 * rows : (y1 + 1) * rows]
        here = slice(y1, y1 + 1)
        pr, pi = times(part[:, :CONTRIB], part[:, CONTRIB:], far[0][here], far[1][here])
        real += pr
        imag += pi
    scale = 1.0 / math.sqrt(extent)
    both = jnp.stack([(real * scale).astype(BF16), (imag * scale).astype(BF16)])
    for member in range(out_ref.shape[0]):
        out_ref[member] = both
    for copy in later:
        copy.wait()


def row_tables(starts_ref, offsets_ref, facets, block_rows, facet_rows):
    half_step = IMAGE // facet_rows // 2
    owners = SUBGRID // block_rows
    index = lax.axis_index("freq") * lax.axis_size("facet") + lax.axis_index("facet")
    start = starts_ref[index // owners]
    shape = (block_rows, facet_rows)
    row = (index % owners) * block_rows + iota(shape, 0)
    half = (STEP // 2) * row - half_step * iota(shape, 1)
    top = cis(CONTRIB * half)[1]
    low = cis(half)[1]
    even = (half & (IMAGE // 2 - 1)) == 0
    limit = jnp.where((half & MASK) == 0, float(CONTRIB), -float(CONTRIB))
    kernel = jnp.where(even, limit, top / jnp.where(even, 1.0, low)) * (1.0 / math.sqrt(facet_rows))
    by_place = (facets, facet_rows)
    by_row = (block_rows, LANES)
    firsts = jnp.zeros(by_place, jnp.int32)
    lane_firsts = jnp.zeros(by_row, jnp.int32)
    for f in range(facets):
        firsts = jnp.where(iota(by_place, 0) == f, offsets_ref[0, f], firsts)
        lane_firsts = jnp.where(iota(by_row, 1) == f, offsets_ref[0, f], lane_firsts)
    place = firsts + iota(by_place, 1)
    place_real, place_imag = cis(
        -start * (place & MASK) - (CONTRIB - 1) * half_step * (place & (facet_rows - 1))
    )
    row_real, row_imag = cis(
        ((index % owners) * block_rows + iota(by_row, 0))
        * (lane_firsts + (CONTRIB - 1) * (STEP // 2))
    )
    tables = []
    for f in range(facets):
        shift = (facet_rows - offsets_ref[0, f] % facet_rows) % facet_rows
        rolled = pltpu.roll(kernel, shift, 1)
        real, imag = times(
            row_real[:, f : f + 1], row_imag[:, f : f + 1], place_real[f : f + 1], place_imag[f : f + 1]
        )
        tables.append((rolled * real, rolled * imag))
    return tables


def patch_start(coords):
    twice = jnp.concatenate([coords, coords], axis=0)
    real, imag = cis(twice * (IMAGE // PERIOD))
    first = iota(twice.shape, 0) < GROUP
    return (jnp.where(first, 1.0, real), jnp.where(first, 0.0, imag)), times(real, imag, real, imag)


def table_kernel(
    piece_rows,
    starts_hbm,
    offsets_hbm,
    coords_ref,
    rows_ref,
    shift_ref,
    eu_ref,
    ev_ref,
    starts_ref,
    offsets_ref,
    plain_ref,
    sem,
):
    small = [
        pltpu.make_async_copy(starts_hbm, starts_ref, sem.at[0]),
        pltpu.make_async_copy(offsets_hbm, offsets_ref, sem.at[1]),
    ]
    for copy in small:
        copy.start()
    facets = offsets_ref.shape[1]
    patch_rows = coords_ref.shape[1]
    block_rows = patch_rows * PATCH
    for p in range(patch_rows):
        for h in range(SIDE // GROUP):
            here = pl.ds(h * GROUP, GROUP)
            start, step = patch_start(coords_ref[0, p, here, :])
            for at, value in enumerate((*start, *step)):
                eu_ref[p, h, at] = value
            power, step = patch_start(coords_ref[1, p, here, :])
            for k in range(PATCH // 2):
                for ri in range(2):
                    to = pl.ds(ri * LANES + k * 2 * GROUP, 2 * GROUP)
                    ev_ref[p, h, to, :] = power[ri].astype(BF16)
                power = times(*power, *step)
    for copy in small:
        copy.wait()
    facet_rows = rows_ref.shape[2]
    tables = row_tables(starts_ref, offsets_ref, facets, block_rows, facet_rows)
    for f, (mr, mi) in enumerate(tables):
        plain_ref[f * 2 * block_rows : (2 * f + 1) * block_rows] = mr.astype(BF16)
        plain_ref[(2 * f + 1) * block_rows : (f + 1) * 2 * block_rows] = mi.astype(BF16)
    shape = (facet_rows, facet_rows)
    half, inside = iota(shape, 1) // (facet_rows // 2), iota(shape, 1) % (facet_rows // 2)
    core = (lax.axis_index("freq") + half) % 2
    place = (2 * (inside // piece_rows) + core) * piece_rows + inside % piece_rows
    order = (iota(shape, 0) == place).astype(F32).astype(BF16)
    ordered = dot(plain_ref[...], order).astype(BF16)
    for f in range(facets):
        rows_ref[f] = ordered[f * 2 * block_rows : (f + 1) * 2 * block_rows]
    shape = (facets, SUBGRID)
    firsts = jnp.zeros(shape, jnp.int32)
    for f in range(facets):
        firsts = jnp.where(iota(shape, 0) == f, offsets_ref[1, f], firsts)
    for ri, value in enumerate(cis(firsts * cell_of(iota(shape, 1)))):
        shift_ref[ri] = value * (1.0 / CONTRIB)


def grid_kernel(
    own_ref,
    other_ref,
    rows_ref,
    weights_ref,
    shift_ref,
    eu_ref,
    ev_ref,
    seen_ref,
    narrowed_ref,
    give_ref,
    res_hbm,
    res_ref,
    left_ref,
    grid_ref,
    back_ref,
    narrow_ref,
    res_sem,
):
    facets = rows_ref.shape[0]
    pairs = own_ref.shape[0] // facets
    patch_rows = seen_ref.shape[1]
    block_rows = patch_rows * PATCH
    vis = seen_ref.shape[3]
    for f in range(facets):
        real, imag = (
            jnp.concatenate(
                [ref[y * facets + f, ri] for ref in (own_ref, other_ref) for y in range(pairs)], axis=0
            )
            for ri in range(2)
        )
        left = jnp.concatenate([rows_ref[f, :block_rows], rows_ref[f, block_rows:]], axis=1)
        part = dot(left, block([[real, imag], [-imag, real]]))
        left_ref[pl.ds(f * block_rows, block_rows), :] = part.astype(BF16)
    shift_real, shift_imag = shift_ref[0], shift_ref[1]
    halves = SUBGRID // LANES
    pair = 2 * GROUP
    tile = (pair, LANES)
    same = iota(tile, 0) % GROUP == iota(tile, 1) % GROUP
    upper, lower = same & (iota(tile, 0) < GROUP), same & (iota(tile, 0) >= GROUP)
    own = iota((LANES, LANES), 0) % GROUP == iota((LANES, LANES), 1) % GROUP
    pick = (iota((PATCH, LANES), 1) // GROUP == iota((PATCH, LANES), 0)).astype(F32).astype(BF16)

    def predicted(h):
        wide = dot(left_ref[...], weights_ref[:, 2 * h * LANES : 2 * (h + 1) * LANES])
        total = [jnp.zeros((block_rows, LANES), F32)] * 2
        for f in range(facets):
            part = wide[f * block_rows : (f + 1) * block_rows]
            lanes = slice(h * LANES, (h + 1) * LANES)
            made = times(
                part[:, :LANES], part[:, LANES:], shift_real[f : f + 1, lanes], shift_imag[f : f + 1, lanes]
            )
            total = [old + new for old, new in zip(total, made)]
        for ri in range(2):
            grid_ref[h, ri] = total[ri].astype(BF16).astype(F32)

    def degrid(p, h):
        spread = []
        for ri in range(2):
            tiles = []
            for r in range(p * PATCH, (p + 1) * PATCH, 2):
                one, two = grid_ref[h, ri, pl.ds(r, 1), :], grid_ref[h, ri, pl.ds(r + 1, 1), :]
                tiles.append(jnp.where(upper, one, jnp.where(lower, two, 0.0)))
            spread.append(jnp.concatenate(tiles, axis=0).astype(BF16))
        mr, mi = spread
        return dot(block([[mr, -mi], [mi, mr]]), ev_ref[p, h])

    def weigh(p, h, inner):
        start, step = [tuple(eu_ref[p, h, at + ri] for ri in range(2)) for at in (0, 2)]
        rows_of = [
            (inner[k : k + pair], inner[LANES + k : LANES + k + pair]) for k in range(0, LANES, pair)
        ]
        sums = rows_of[-1]
        for new in rows_of[-2::-1]:
            sums = [old + value for old, value in zip(times(*sums, *step), new)]
        sums = times(*sums, *start)
        res = []
        for ri, value in enumerate(sums):
            model = (value + pltpu.roll(value, GROUP, 0)) * (1.0 / PATCH)
            seen = seen_ref[ri, p, pl.ds(h * GROUP, GROUP), :].astype(F32)
            rounded = (jnp.concatenate([seen, seen], axis=0) - model).astype(BF16)
            res_ref[ri, p, pl.ds(h * GROUP, GROUP), :] = rounded[:GROUP]
            res.append(rounded.astype(F32))
        weighted = [[], []]
        res = times_conj(*res, *start)
        for k in range(PATCH // 2):
            for ri in range(2):
                weighted[ri].append(res[ri])
            res = times_conj(*res, *step)
        return jnp.concatenate(weighted[0] + weighted[1], axis=0).astype(BF16)

    def regrid(p, h, back):
        both = [
            back[:LANES, :LANES] + back[LANES:, LANES:],
            back[LANES:, :LANES] - back[:LANES, LANES:],
        ]
        both = jnp.concatenate([jnp.where(own, value, 0.0) for value in both], axis=1)
        cells = dot(pick, both.astype(BF16))
        for ri in range(2):
            back_ref[h, ri, pl.ds(p * PATCH, PATCH), :] = cells[:, ri * LANES : (ri + 1) * LANES]

    def widen(h):
        for f in range(facets):
            lanes = slice(h * LANES, (h + 1) * LANES)
            made = times_conj(
                back_ref[h, 0], back_ref[h, 1], shift_real[f : f + 1, lanes], shift_imag[f : f + 1, lanes]
            )
            for ri in range(2):
                to = (2 * h + ri) * LANES
                narrow_ref[pl.ds(f * block_rows, block_rows), to : to + LANES] = made[ri].astype(BF16)

    tasks = [(p, h) for h in range(halves) for p in range(patch_rows)]
    inner, back = {}, {}
    for h in range(halves):
        predicted(h)
        for p in range(patch_rows):
            inner[p, h] = degrid(p, h)
    narrowed = []

    def finish(task):
        regrid(*task, back.pop(task))
        p, h = task
        if p == patch_rows - 1:
            widen(h)
            lanes = pl.ds(2 * h * LANES, 2 * LANES)
            narrowed.append(dot_t(narrow_ref[:, lanes], weights_ref[:, lanes]))

    for at, task in enumerate(tasks):
        left = weigh(*task, inner.pop(task))
        back[task] = dot_t(left, ev_ref[task[0], task[1]])
        if at:
            finish(tasks[at - 1])
    result = pltpu.make_async_copy(res_ref, res_hbm, res_sem)
    result.start()
    finish(tasks[-1])
    narrowed_ref[...] = sum(narrowed).astype(BF16)
    adjoint_rows(1, rows_ref, narrowed_ref, give_ref)
    result.wait()


def adjoint_rows(half, rows_ref, narrowed_ref, out_ref):
    facets, height, facet_rows = rows_ref.shape
    block_rows = height // 2
    pairs = out_ref.shape[0] // facets
    piece_rows = out_ref.shape[2]
    for f in range(facets):
        here = pl.ds(f * block_rows, block_rows)
        real, imag = narrowed_ref[here, :CONTRIB], narrowed_ref[here, CONTRIB:]
        lanes = pl.ds(half * (facet_rows // 2), facet_rows // 2)
        product = dot_0(rows_ref[f, :, lanes], block([[real, imag], [imag, -real]])).astype(BF16)
        for y in range(pairs):
            for ri in range(2):
                out_ref[y * facets + f, ri] = product[
                    y * piece_rows : (y + 1) * piece_rows, ri * CONTRIB : (ri + 1) * CONTRIB
                ]


def image_kernel(scale, in_ref, near_ref, far_ref, out_hbm, stage_ref, sem):
    parts = in_ref.shape[0]
    rows, extent = out_hbm.shape[2:]
    far_count = extent // LANES
    real, imag = (
        sum(in_ref[q, ri].astype(F32) for q in range(parts)) * scale for ri in range(2)
    )
    copies = []
    for top in range(0, far_count, CHUNK):
        left = []
        for y1 in range(top, top + CHUNK):
            ar, ai = times_conj(real, imag, far_ref[0, y1 : y1 + 1], far_ref[1, y1 : y1 + 1])
            left.append(jnp.concatenate([ar, ai], axis=1).astype(BF16))
        value = dot_t(jnp.concatenate(left, axis=0), near_ref[...])
        value = (value * (1.0 / math.sqrt(CONTRIB))).astype(BF16)
        for y1 in range(CHUNK):
            for ri in range(2):
                stage_ref[ri, :, pl.ds((top + y1) * LANES, LANES)] = value[
                    y1 * rows : (y1 + 1) * rows, ri * LANES : (ri + 1) * LANES
                ]
        for ri in range(2):
            span = pl.ds(top * LANES, CHUNK * LANES)
            copy = pltpu.make_async_copy(
                stage_ref.at[ri, :, span], out_hbm.at[0, ri, :, span], sem.at[len(copies)]
            )
            copy.start()
            copies.append(copy)
    for copy in copies:
        copy.wait()


HBM = pl.BlockSpec(memory_space=pltpu.HBM)
SMEM = pl.BlockSpec(memory_space=pltpu.SMEM)
VMEM = pl.BlockSpec(memory_space=pltpu.VMEM)


def call(kernel, name, operands, in_specs, outs, scratch=(), out_specs=None):
    return pl.pallas_call(
        kernel,
        name=name,
        out_shape=outs,
        in_specs=in_specs,
        out_specs=out_specs or jax.tree.map(lambda _: VMEM, outs),
        scratch_shapes=list(scratch),
        compiler_params=pltpu.CompilerParams(vmem_limit_bytes=40 * 1024 * 1024),
    )(*operands)


def on_device(facet_image, facet_offsets, subgrid_rows, column_offset, uv_coords, observed):
    shape = jax.ShapeDtypeStruct
    rows, extent = facet_image.shape[2:]
    facets = lax.axis_size("facet")
    parts = lax.axis_size("freq")
    subgrids = subgrid_rows.shape[0]
    block_rows = uv_coords.shape[1] * PATCH
    members = facets * parts // 2
    groups = [
        [(2 * y + c) * facets + f for y in range(parts // 2) for f in range(facets)]
        for c in range(2)
    ]
    offsets = facet_offsets.T

    def exchange(value):
        return lax.all_to_all(
            value, ("freq", "facet"), split_axis=0, concat_axis=0, axis_index_groups=groups, tiled=True
        )

    def in_hbm(value):
        return pltpu.with_memory_space_constraint(value, pltpu.HBM)

    def swap(value):
        return lax.ppermute(value, "freq", [(q, q ^ 1) for q in range(parts)])

    pieces = shape((members, 2, rows, CONTRIB), BF16)
    far_count = extent // LANES
    transformed, near, far, weights, coords, seen = call(
        column_kernel,
        "column",
        (column_offset, *map(in_hbm, (offsets, facet_image, uv_coords, observed))),
        [SMEM] + [HBM] * 4,
        (
            pieces,
            shape((2 * LANES, 2 * CONTRIB), BF16),
            shape((2, far_count, CONTRIB), F32),
            shape((2 * CONTRIB, 2 * SUBGRID), BF16),
            shape(uv_coords.shape, jnp.int32),
            shape(observed.shape, BF16),
        ),
        (
            pltpu.VMEM(facet_image.shape[1:], BF16),
            pltpu.SMEM(offsets.shape, jnp.int32),
            pltpu.SemaphoreType.DMA,
            pltpu.SemaphoreType.DMA((2,)),
            pltpu.SemaphoreType.DMA((2,)),
        ),
    )
    own = exchange(transformed)
    other = swap(own)
    patch_rows, vis = uv_coords.shape[1], uv_coords.shape[3]
    halves = SIDE * PATCH // LANES
    row_products, *tables = call(
        functools.partial(table_kernel, rows),
        "tables",
        (in_hbm(subgrid_rows), in_hbm(offsets), coords),
        [HBM, HBM, VMEM],
        (
            shape((facets, 2 * block_rows, parts * rows), BF16),
            shape((2, facets, SUBGRID), F32),
            shape((patch_rows, halves, 4, 2 * GROUP, vis), F32),
            shape((patch_rows, halves, 2 * LANES, vis), BF16),
        ),
        (
            pltpu.SMEM(subgrid_rows.shape, jnp.int32),
            pltpu.SMEM(offsets.shape, jnp.int32),
            pltpu.VMEM((facets * 2 * block_rows, parts * rows), BF16),
            pltpu.SemaphoreType.DMA((2,)),
        ),
    )
    narrowed, give, residual_vis = call(
        grid_kernel,
        "grid",
        (own, other, row_products, weights, *tables, seen),
        [VMEM] * 8,
        (
            shape((facets * block_rows, 2 * CONTRIB), BF16),
            pieces,
            shape(observed.shape, BF16),
        ),
        (
            pltpu.VMEM(observed.shape, BF16),
            pltpu.VMEM((facets * block_rows, 2 * CONTRIB), BF16),
            pltpu.VMEM((halves, 2, block_rows, LANES), F32),
            pltpu.VMEM((halves, 2, block_rows, LANES), F32),
            pltpu.VMEM((facets * block_rows, 2 * SUBGRID), BF16),
            pltpu.SemaphoreType.DMA,
        ),
        (VMEM, VMEM, HBM),
    )
    keep = call(
        functools.partial(adjoint_rows, 0),
        "keep",
        (row_products, narrowed),
        [VMEM] * 2,
        pieces,
    )
    partial = (keep.astype(F32) + swap(give).astype(F32)).astype(BF16)
    shared_scale = 1.0 / CONTRIB / math.sqrt(parts * rows)
    scale = 1.0 / (math.sqrt(vis) * SUBGRID * math.sqrt(subgrids * CONTRIB) * shared_scale)
    image_residual = call(
        functools.partial(image_kernel, scale),
        "image",
        (exchange(partial), near, far),
        [VMEM] * 3,
        shape(facet_image.shape, BF16),
        (
            pltpu.VMEM(facet_image.shape[1:], BF16),
            pltpu.SemaphoreType.DMA((2 * far_count // CHUNK,)),
        ),
        HBM,
    )
    return (image_residual, residual_vis)


def solution(mesh):
    return jax.shard_map(
        on_device,
        mesh=mesh,
        in_specs=(
            P("facet", None, "freq", None),
            P(),
            P(),
            P(),
            P(None, ("freq", "facet"), None, None),
            P(None, ("freq", "facet"), None, None),
        ),
        out_specs=(P("facet", None, "freq", None), P(None, ("freq", "facet"), None, None)),
        check_vma=False,
    )
```

```python
import functools
import math

import jax
import jax.numpy as jnp
from jax import lax
from jax.experimental import pallas as pl
from jax.experimental.pallas import tpu as pltpu
from jax.sharding import PartitionSpec as P

IMAGE = 32768
CONTRIB = 128
SUBGRID = 256
PATCH = 32
SIDE = 8
STEP = 128
PERIOD = 256
LANES = 128
MASK = IMAGE - 1

F32 = jnp.float32
BF16 = jnp.bfloat16


def iota(shape, axis):
    return lax.broadcasted_iota(jnp.int32, shape, axis)


def cis(turns):
    turns = turns & MASK
    quarter = (turns + IMAGE // 8) >> 13
    x = (turns - (quarter << 13)).astype(F32) * (2.0 * math.pi / IMAGE)
    x2 = x * x
    sine = x * (1.0 + x2 * (-1.0 / 6 + x2 * (1.0 / 120 - x2 * (1.0 / 5040))))
    cosine = 1.0 + x2 * (-0.5 + x2 * (1.0 / 24 + x2 * (-1.0 / 720 + x2 * (1.0 / 40320))))
    odd = (quarter & 1) == 1
    real = jnp.where(odd, sine, cosine)
    imag = jnp.where(odd, cosine, sine)
    real = jnp.where(((quarter + 1) & 2) == 2, -real, real)
    imag = jnp.where((quarter & 2) == 2, -imag, imag)
    return real, imag


def times(ar, ai, br, bi):
    return ar * br - ai * bi, ar * bi + ai * br


def times_conj(ar, ai, br, bi):
    return ar * br + ai * bi, ai * br - ar * bi


def block(rows):
    return jnp.concatenate([jnp.concatenate(row, axis=1) for row in rows], axis=0)


def dot(left, right):
    return lax.dot_general(left, right, (((1,), (0,)), ((), ())), preferred_element_type=F32)


def dot_t(left, right):
    return lax.dot_general(left, right, (((1,), (1,)), ((), ())), preferred_element_type=F32)


def dot_0(left, right):
    return lax.dot_general(left, right, (((0,), (0,)), ((), ())), preferred_element_type=F32)


def column_tables(column, first, extent):
    col_step = IMAGE // extent
    far_count = extent // LANES
    near = ((column + col_step * iota((LANES, CONTRIB), 1)) & MASK) * iota((LANES, CONTRIB), 0)
    shape = (far_count, CONTRIB)
    far = ((column + col_step * iota(shape, 1)) & MASK) * ((first + LANES * iota(shape, 0)) & MASK)
    return cis(-near), cis(-far)


def near_weights(near):
    real, imag = near
    return block([[real, imag], [-imag, real]]).astype(BF16)


CHUNK = 8
GROUP = LANES // PATCH


def cell_of(lane):
    half, inside = lane // LANES, lane % LANES
    return (half * GROUP + inside % GROUP) * PATCH + inside // GROUP


def column_kernel(
    column_ref,
    offsets_hbm,
    image_hbm,
    coords_hbm,
    seen_hbm,
    out_ref,
    near_ref,
    far_ref,
    weights_ref,
    coords_ref,
    seen_ref,
    left_ref,
    offsets_ref,
    small_sem,
    image_sem,
    later_sem,
):
    rows, extent = image_hbm.shape[2:]
    far_count = extent // LANES
    small = pltpu.make_async_copy(offsets_hbm, offsets_ref, small_sem)
    small.start()
    large = []
    for ri in range(2):
        copy = pltpu.make_async_copy(image_hbm.at[0, ri], left_ref.at[ri], image_sem.at[ri])
        copy.start()
        large.append(copy)
    later = [
        pltpu.make_async_copy(coords_hbm, coords_ref, later_sem.at[0]),
        pltpu.make_async_copy(seen_hbm, seen_ref, later_sem.at[1]),
    ]
    for copy in later:
        copy.start()
    for h in range(SUBGRID // LANES):
        shape = (CONTRIB, LANES)
        tr, ti = cis(iota(shape, 0) * cell_of(iota(shape, 1) + h * LANES) * STEP)
        weights_ref[:, 2 * h * LANES : 2 * (h + 1) * LANES] = block([[tr, ti], [-ti, tr]]).astype(BF16)
    small.wait()
    first = offsets_ref[1, lax.axis_index("facet")]
    near, far = column_tables(column_ref[0], first, extent)
    near_ref[...] = near_weights(near)
    far_ref[0], far_ref[1] = far
    real = jnp.zeros((rows, CONTRIB), F32)
    imag = jnp.zeros((rows, CONTRIB), F32)
    for copy in large:
        copy.wait()
    left = [
        jnp.concatenate([left_ref[ri, :, pl.ds(y1 * LANES, LANES)] for ri in range(2)], axis=1)
        for y1 in range(far_count)
    ]
    value = dot(jnp.concatenate(left, axis=0), near_ref[...])
    for y1 in range(far_count):
        part = value[y1 * rows : (y1 + 1) * rows]
        here = slice(y1, y1 + 1)
        pr, pi = times(part[:, :CONTRIB], part[:, CONTRIB:], far[0][here], far[1][here])
        real += pr
        imag += pi
    scale = 1.0 / math.sqrt(extent)
    both = jnp.stack([(real * scale).astype(BF16), (imag * scale).astype(BF16)])
    for member in range(out_ref.shape[0]):
        out_ref[member] = both
    for copy in later:
        copy.wait()


def row_of(position):
    inside = position % PATCH
    half = PATCH // 2
    return position - inside + jnp.where(inside < half, half - 1 - inside, inside)


def row_tables(starts_ref, offsets_ref, facets, block_rows, facet_rows):
    half_step = IMAGE // facet_rows // 2
    owners = SUBGRID // block_rows
    index = lax.axis_index("freq") * lax.axis_size("facet") + lax.axis_index("facet")
    start = starts_ref[index // owners]
    shape = (block_rows, facet_rows)
    row = (index % owners) * block_rows + row_of(iota(shape, 0))
    half = (STEP // 2) * row - half_step * iota(shape, 1)
    top = cis(CONTRIB * half)[1]
    low = cis(half)[1]
    even = (half & (IMAGE // 2 - 1)) == 0
    limit = jnp.where((half & MASK) == 0, float(CONTRIB), -float(CONTRIB))
    kernel = jnp.where(even, limit, top / jnp.where(even, 1.0, low)) * (1.0 / math.sqrt(facet_rows))
    by_place = (facets, facet_rows)
    by_row = (block_rows, LANES)
    firsts = jnp.zeros(by_place, jnp.int32)
    lane_firsts = jnp.zeros(by_row, jnp.int32)
    for f in range(facets):
        firsts = jnp.where(iota(by_place, 0) == f, offsets_ref[0, f], firsts)
        lane_firsts = jnp.where(iota(by_row, 1) == f, offsets_ref[0, f], lane_firsts)
    place = firsts + iota(by_place, 1)
    place_real, place_imag = cis(
        -start * (place & MASK) - (CONTRIB - 1) * half_step * (place & (facet_rows - 1))
    )
    row_real, row_imag = cis(
        ((index % owners) * block_rows + row_of(iota(by_row, 0)))
        * (lane_firsts + (CONTRIB - 1) * (STEP // 2))
    )
    tables = []
    for f in range(facets):
        shift = (facet_rows - offsets_ref[0, f] % facet_rows) % facet_rows
        rolled = pltpu.roll(kernel, shift, 1)
        real, imag = times(
            row_real[:, f : f + 1], row_imag[:, f : f + 1], place_real[f : f + 1], place_imag[f : f + 1]
        )
        tables.append((rolled * real, rolled * imag))
    return tables


def patch_start(coords):
    twice = jnp.concatenate([coords, coords], axis=0)
    real, imag = cis(twice * (IMAGE // PERIOD))
    first = iota(twice.shape, 0) < GROUP
    return (jnp.where(first, 1.0, real), jnp.where(first, 0.0, imag)), times(real, imag, real, imag)


def table_kernel(
    piece_rows,
    starts_hbm,
    offsets_hbm,
    coords_ref,
    rows_ref,
    shift_ref,
    wave_ref,
    centre_ref,
    ev_ref,
    starts_ref,
    offsets_ref,
    plain_ref,
    sem,
):
    small = [
        pltpu.make_async_copy(starts_hbm, starts_ref, sem.at[0]),
        pltpu.make_async_copy(offsets_hbm, offsets_ref, sem.at[1]),
    ]
    for copy in small:
        copy.start()
    facets = offsets_ref.shape[1]
    patch_rows = coords_ref.shape[1]
    block_rows = patch_rows * PATCH
    for p in range(patch_rows):
        for h in range(SIDE // GROUP):
            here = pl.ds(h * GROUP, GROUP)
            twice = jnp.concatenate([coords_ref[0, p, here, :]] * 2, axis=0)
            odd = jnp.where(iota(twice.shape, 0) < GROUP, 1, 3)
            half_turn = IMAGE // PERIOD // 2
            centre_ref[p, h, 0], centre_ref[p, h, 1] = cis(twice * ((PATCH - 1) * half_turn))
            power, step = cis(twice * odd * half_turn), cis(twice * (4 * half_turn))
            for k in range(PATCH // 4):
                for ri in range(2):
                    wave_ref[p, h, ri, pl.ds(k * 2 * GROUP, 2 * GROUP), :] = power[ri]
                power = times(*power, *step)
            power, step = patch_start(coords_ref[1, p, here, :])
            for k in range(PATCH // 2):
                for ri in range(2):
                    to = pl.ds(ri * LANES + k * 2 * GROUP, 2 * GROUP)
                    ev_ref[p, h, to, :] = power[ri].astype(BF16)
                power = times(*power, *step)
    for copy in small:
        copy.wait()
    facet_rows = rows_ref.shape[2] // 2
    tables = row_tables(starts_ref, offsets_ref, facets, block_rows, facet_rows)
    for f, (mr, mi) in enumerate(tables):
        plain_ref[f * 2 * block_rows : (2 * f + 1) * block_rows] = mr.astype(BF16)
        plain_ref[(2 * f + 1) * block_rows : (f + 1) * 2 * block_rows] = mi.astype(BF16)
    shape = (facet_rows, facet_rows)
    half, inside = iota(shape, 1) // (facet_rows // 2), iota(shape, 1) % (facet_rows // 2)
    core = (lax.axis_index("freq") + half) % 2
    place = (2 * (inside // piece_rows) + core) * piece_rows + inside % piece_rows
    order = (iota(shape, 0) == place).astype(F32).astype(BF16)
    ordered = dot(plain_ref[...], order).astype(BF16)
    for f in range(facets):
        here = ordered[f * 2 * block_rows : (f + 1) * 2 * block_rows]
        rows_ref[f, :, :facet_rows] = here
        rows_ref[f, :block_rows, facet_rows:] = -here[block_rows:]
        rows_ref[f, block_rows:, facet_rows:] = here[:block_rows]
    shape = (facets, SUBGRID)
    firsts = jnp.zeros(shape, jnp.int32)
    for f in range(facets):
        firsts = jnp.where(iota(shape, 0) == f, offsets_ref[1, f], firsts)
    for ri, value in enumerate(cis(firsts * cell_of(iota(shape, 1)))):
        shift_ref[ri] = value * (1.0 / CONTRIB)


def grid_kernel(
    own_ref,
    other_ref,
    rows_ref,
    weights_ref,
    shift_ref,
    wave_ref,
    centre_ref,
    ev_ref,
    seen_ref,
    narrowed_ref,
    give_ref,
    res_hbm,
    res_ref,
    left_ref,
    grid_ref,
    back_ref,
    both_ref,
    narrow_ref,
    res_sem,
):
    facets = rows_ref.shape[0]
    pairs = own_ref.shape[0] // facets
    patch_rows = seen_ref.shape[1]
    block_rows = patch_rows * PATCH
    vis = seen_ref.shape[3]
    for f in range(facets):
        right = [
            ref[y * facets + f, ri] for ri in range(2) for ref in (own_ref, other_ref) for y in range(pairs)
        ]
        part = dot(rows_ref[f], jnp.concatenate(right, axis=0)).astype(BF16)
        for ri in range(2):
            to = (pl.ds(f * block_rows, block_rows), pl.ds(ri * CONTRIB, CONTRIB))
            left_ref[to] = part[ri * block_rows : (ri + 1) * block_rows]
    shift_real, shift_imag = shift_ref[0], shift_ref[1]
    halves = SUBGRID // LANES
    pair = 2 * GROUP
    tile = (pair, LANES)
    same = iota(tile, 0) % GROUP == iota(tile, 1) % GROUP
    upper, lower = same & (iota(tile, 0) < GROUP), same & (iota(tile, 0) >= GROUP)
    own = iota((PATCH, LANES), 1) % GROUP

    def predicted(h):
        wide = dot(left_ref[...], weights_ref[:, 2 * h * LANES : 2 * (h + 1) * LANES])
        total = [jnp.zeros((block_rows, LANES), F32)] * 2
        for f in range(facets):
            part = wide[f * block_rows : (f + 1) * block_rows]
            lanes = slice(h * LANES, (h + 1) * LANES)
            made = times(
                part[:, :LANES], part[:, LANES:], shift_real[f : f + 1, lanes], shift_imag[f : f + 1, lanes]
            )
            total = [old + new for old, new in zip(total, made)]
        for ri in range(2):
            grid_ref[h, ri] = total[ri].astype(BF16).astype(F32)

    def degrid(p, h):
        middle = PATCH // 2
        made = []
        for ri in range(2):
            sums, differences = [], []
            for k in range(0, middle, 2):
                after, before = (
                    [grid_ref[h, ri, pl.ds(p * PATCH + at + k + i, 1), :] for i in range(2)]
                    for at in (middle, 0)
                )
                add = [one + two for one, two in zip(after, before)]
                take = [one - two for one, two in zip(after, before)]
                for tiles, (one, two) in ((sums, add), (differences, take)):
                    tiles.append(jnp.where(upper, one, jnp.where(lower, two, 0.0)))
            made.append([jnp.concatenate(tiles, axis=0).astype(BF16) for tiles in (sums, differences)])
        (sr, dr), (si, di) = made
        return dot(block([[sr, -si], [si, sr], [dr, -di], [di, dr]]), ev_ref[p, h])

    def weigh(p, h, inner):
        height = LANES // 2
        sums = [jnp.zeros((pair, vis), F32)] * 2
        for k in range(0, height, pair):
            cosine, sine = (wave_ref[p, h, ri, pl.ds(k, pair), :] for ri in range(2))
            sr, si, dr, di = (inner[at + k : at + k + pair] for at in range(0, 4 * height, height))
            sums = [sums[0] + (cosine * sr - sine * di), sums[1] + (cosine * si + sine * dr)]
        centre = centre_ref[p, h, 0], centre_ref[p, h, 1]
        sums = times(*(value + pltpu.roll(value, GROUP, 0) for value in sums), *centre)
        res = []
        for ri, value in enumerate(sums):
            model = value * (1.0 / PATCH)
            seen = seen_ref[ri, p, pl.ds(h * GROUP, GROUP), :].astype(F32)
            rounded = (jnp.concatenate([seen, seen], axis=0) - model).astype(BF16)
            res_ref[ri, p, pl.ds(h * GROUP, GROUP), :] = rounded[:GROUP]
            res.append(rounded.astype(F32))
        res = times_conj(*res, *centre)
        weighted = [
            wave_ref[p, h, wave, pl.ds(k, pair), :] * res[ri]
            for wave in range(2)
            for ri in range(2)
            for k in range(0, height, pair)
        ]
        return jnp.concatenate(weighted, axis=0).astype(BF16)

    def regrid(p, h, back):
        height = LANES // 2
        quarters = [back[at : at + height] for at in range(0, 4 * height, height)]
        near, far = [part[:, :LANES] for part in quarters], [part[:, LANES:] for part in quarters]
        ar, ai = near[0] + far[1], near[1] - far[0]
        br, bi = near[2] + far[3], near[3] - far[2]
        both_ref[p, h, 0, :height], both_ref[p, h, 0, height:] = ar - bi, ar + bi
        both_ref[p, h, 1, :height], both_ref[p, h, 1, height:] = ai + br, ai - br
        for ri in range(2):
            cells = both_ref[p, h, ri, pl.ds(0, PATCH, stride=GROUP), :]
            for c in range(1, GROUP):
                cells = jnp.where(own == c, both_ref[p, h, ri, pl.ds(c, PATCH, stride=GROUP), :], cells)
            back_ref[h, ri, pl.ds(p * PATCH, PATCH), :] = cells.astype(BF16).astype(F32)

    def widen(h):
        for f in range(facets):
            lanes = slice(h * LANES, (h + 1) * LANES)
            made = times_conj(
                back_ref[h, 0], back_ref[h, 1], shift_real[f : f + 1, lanes], shift_imag[f : f + 1, lanes]
            )
            for ri in range(2):
                to = (2 * h + ri) * LANES
                narrow_ref[pl.ds(f * block_rows, block_rows), to : to + LANES] = made[ri].astype(BF16)

    tasks = [(p, h) for h in range(halves) for p in range(patch_rows)]
    inner, back = {}, {}
    for h in range(halves):
        predicted(h)
        for p in range(patch_rows):
            inner[p, h] = degrid(p, h)
    narrowed = []

    def finish(task):
        regrid(*task, back.pop(task))
        p, h = task
        if p == patch_rows - 1:
            widen(h)
            lanes = pl.ds(2 * h * LANES, 2 * LANES)
            narrowed.append(dot_t(narrow_ref[:, lanes], weights_ref[:, lanes]))

    for at, task in enumerate(tasks):
        left = weigh(*task, inner.pop(task))
        back[task] = dot_t(left, ev_ref[task[0], task[1]])
        if at:
            finish(tasks[at - 1])
    result = pltpu.make_async_copy(res_ref, res_hbm, res_sem)
    result.start()
    finish(tasks[-1])
    narrowed_ref[...] = sum(narrowed).astype(BF16)
    adjoint_rows(1, rows_ref, narrowed_ref, give_ref)
    result.wait()


def adjoint_rows(half, rows_ref, narrowed_ref, out_ref):
    facets, height, facet_rows = rows_ref.shape[0], rows_ref.shape[1], rows_ref.shape[2] // 2
    block_rows = height // 2
    pairs = out_ref.shape[0] // facets
    piece_rows = out_ref.shape[2]
    for f in range(facets):
        here = pl.ds(f * block_rows, block_rows)
        real, imag = narrowed_ref[here, :CONTRIB], narrowed_ref[here, CONTRIB:]
        lanes = pl.ds(half * (facet_rows // 2), facet_rows // 2)
        product = dot_0(rows_ref[f, :, lanes], block([[real, imag], [imag, -real]])).astype(BF16)
        for y in range(pairs):
            for ri in range(2):
                out_ref[y * facets + f, ri] = product[
                    y * piece_rows : (y + 1) * piece_rows, ri * CONTRIB : (ri + 1) * CONTRIB
                ]


def image_kernel(scale, in_ref, near_ref, far_ref, out_hbm, stage_ref, sem):
    parts = in_ref.shape[0]
    rows, extent = out_hbm.shape[2:]
    far_count = extent // LANES
    real, imag = (
        sum(in_ref[q, ri].astype(F32) for q in range(parts)) * scale for ri in range(2)
    )
    copies = []
    for top in range(0, far_count, CHUNK):
        left = []
        for y1 in range(top, top + CHUNK):
            ar, ai = times_conj(real, imag, far_ref[0, y1 : y1 + 1], far_ref[1, y1 : y1 + 1])
            left.append(jnp.concatenate([ar, ai], axis=1).astype(BF16))
        value = dot_t(jnp.concatenate(left, axis=0), near_ref[...])
        value = (value * (1.0 / math.sqrt(CONTRIB))).astype(BF16)
        for y1 in range(CHUNK):
            for ri in range(2):
                stage_ref[ri, :, pl.ds((top + y1) * LANES, LANES)] = value[
                    y1 * rows : (y1 + 1) * rows, ri * LANES : (ri + 1) * LANES
                ]
        for ri in range(2):
            span = pl.ds(top * LANES, CHUNK * LANES)
            copy = pltpu.make_async_copy(
                stage_ref.at[ri, :, span], out_hbm.at[0, ri, :, span], sem.at[len(copies)]
            )
            copy.start()
            copies.append(copy)
    for copy in copies:
        copy.wait()


HBM = pl.BlockSpec(memory_space=pltpu.HBM)
SMEM = pl.BlockSpec(memory_space=pltpu.SMEM)
VMEM = pl.BlockSpec(memory_space=pltpu.VMEM)


def call(kernel, name, operands, in_specs, outs, scratch=(), out_specs=None):
    return pl.pallas_call(
        kernel,
        name=name,
        out_shape=outs,
        in_specs=in_specs,
        out_specs=out_specs or jax.tree.map(lambda _: VMEM, outs),
        scratch_shapes=list(scratch),
        compiler_params=pltpu.CompilerParams(vmem_limit_bytes=40 * 1024 * 1024),
    )(*operands)


def on_device(facet_image, facet_offsets, subgrid_rows, column_offset, uv_coords, observed):
    shape = jax.ShapeDtypeStruct
    rows, extent = facet_image.shape[2:]
    facets = lax.axis_size("facet")
    parts = lax.axis_size("freq")
    subgrids = subgrid_rows.shape[0]
    block_rows = uv_coords.shape[1] * PATCH
    members = facets * parts // 2
    groups = [
        [(2 * y + c) * facets + f for y in range(parts // 2) for f in range(facets)]
        for c in range(2)
    ]
    offsets = facet_offsets.T

    def exchange(value):
        return lax.all_to_all(
            value, ("freq", "facet"), split_axis=0, concat_axis=0, axis_index_groups=groups, tiled=True
        )

    def in_hbm(value):
        return pltpu.with_memory_space_constraint(value, pltpu.HBM)

    def swap(value):
        return lax.ppermute(value, "freq", [(q, q ^ 1) for q in range(parts)])

    pieces = shape((members, 2, rows, CONTRIB), BF16)
    far_count = extent // LANES
    transformed, near, far, weights, coords, seen = call(
        column_kernel,
        "column",
        (column_offset, *map(in_hbm, (offsets, facet_image, uv_coords, observed))),
        [SMEM] + [HBM] * 4,
        (
            pieces,
            shape((2 * LANES, 2 * CONTRIB), BF16),
            shape((2, far_count, CONTRIB), F32),
            shape((2 * CONTRIB, 2 * SUBGRID), BF16),
            shape(uv_coords.shape, jnp.int32),
            shape(observed.shape, BF16),
        ),
        (
            pltpu.VMEM(facet_image.shape[1:], BF16),
            pltpu.SMEM(offsets.shape, jnp.int32),
            pltpu.SemaphoreType.DMA,
            pltpu.SemaphoreType.DMA((2,)),
            pltpu.SemaphoreType.DMA((2,)),
        ),
    )
    own = exchange(transformed)
    other = swap(own)
    patch_rows, vis = uv_coords.shape[1], uv_coords.shape[3]
    halves = SIDE * PATCH // LANES
    row_products, *tables = call(
        functools.partial(table_kernel, rows),
        "tables",
        (in_hbm(subgrid_rows), in_hbm(offsets), coords),
        [HBM, HBM, VMEM],
        (
            shape((facets, 2 * block_rows, 2 * parts * rows), BF16),
            shape((2, facets, SUBGRID), F32),
            shape((patch_rows, halves, 2, LANES // 2, vis), F32),
            shape((patch_rows, halves, 2, 2 * GROUP, vis), F32),
            shape((patch_rows, halves, 2 * LANES, vis), BF16),
        ),
        (
            pltpu.SMEM(subgrid_rows.shape, jnp.int32),
            pltpu.SMEM(offsets.shape, jnp.int32),
            pltpu.VMEM((facets * 2 * block_rows, parts * rows), BF16),
            pltpu.SemaphoreType.DMA((2,)),
        ),
    )
    narrowed, give, residual_vis = call(
        grid_kernel,
        "grid",
        (own, other, row_products, weights, *tables, seen),
        [VMEM] * 9,
        (
            shape((facets * block_rows, 2 * CONTRIB), BF16),
            pieces,
            shape(observed.shape, BF16),
        ),
        (
            pltpu.VMEM(observed.shape, BF16),
            pltpu.VMEM((facets * block_rows, 2 * CONTRIB), BF16),
            pltpu.VMEM((halves, 2, block_rows, LANES), F32),
            pltpu.VMEM((halves, 2, block_rows, LANES), F32),
            pltpu.VMEM((patch_rows, halves, 2, LANES, LANES), F32),
            pltpu.VMEM((facets * block_rows, 2 * SUBGRID), BF16),
            pltpu.SemaphoreType.DMA,
        ),
        (VMEM, VMEM, HBM),
    )
    keep = call(
        functools.partial(adjoint_rows, 0),
        "keep",
        (row_products, narrowed),
        [VMEM] * 2,
        pieces,
    )
    partial = (keep.astype(F32) + swap(give).astype(F32)).astype(BF16)
    shared_scale = 1.0 / CONTRIB / math.sqrt(parts * rows)
    scale = 1.0 / (math.sqrt(vis) * SUBGRID * math.sqrt(subgrids * CONTRIB) * shared_scale)
    image_residual = call(
        functools.partial(image_kernel, scale),
        "image",
        (exchange(partial), near, far),
        [VMEM] * 3,
        shape(facet_image.shape, BF16),
        (
            pltpu.VMEM(facet_image.shape[1:], BF16),
            pltpu.SemaphoreType.DMA((2 * far_count // CHUNK,)),
        ),
        HBM,
    )
    return (image_residual, residual_vis)


def solution(mesh):
    return jax.shard_map(
        on_device,
        mesh=mesh,
        in_specs=(
            P("facet", None, "freq", None),
            P(),
            P(),
            P(),
            P(None, ("freq", "facet"), None, None),
            P(None, ("freq", "facet"), None, None),
        ),
        out_specs=(P("facet", None, "freq", None), P(None, ("freq", "facet"), None, None)),
        check_vma=False,
    )
```

```python
import functools
import math

import jax
import jax.numpy as jnp
from jax import lax
from jax.experimental import pallas as pl
from jax.experimental.pallas import tpu as pltpu
from jax.sharding import PartitionSpec as P

IMAGE = 32768
CONTRIB = 128
SUBGRID = 256
PATCH = 32
SIDE = 8
STEP = 128
PERIOD = 256
LANES = 128
MASK = IMAGE - 1

F32 = jnp.float32
BF16 = jnp.bfloat16


def iota(shape, axis):
    return lax.broadcasted_iota(jnp.int32, shape, axis)


def cis(turns):
    turns = turns & MASK
    quarter = (turns + IMAGE // 8) >> 13
    x = (turns - (quarter << 13)).astype(F32) * (2.0 * math.pi / IMAGE)
    x2 = x * x
    sine = x * (1.0 + x2 * (-1.0 / 6 + x2 * (1.0 / 120 - x2 * (1.0 / 5040))))
    cosine = 1.0 + x2 * (-0.5 + x2 * (1.0 / 24 + x2 * (-1.0 / 720 + x2 * (1.0 / 40320))))
    odd = (quarter & 1) == 1
    real = jnp.where(odd, sine, cosine)
    imag = jnp.where(odd, cosine, sine)
    real = jnp.where(((quarter + 1) & 2) == 2, -real, real)
    imag = jnp.where((quarter & 2) == 2, -imag, imag)
    return real, imag


def times(ar, ai, br, bi):
    return ar * br - ai * bi, ar * bi + ai * br


def times_conj(ar, ai, br, bi):
    return ar * br + ai * bi, ai * br - ar * bi


def block(rows):
    return jnp.concatenate([jnp.concatenate(row, axis=1) for row in rows], axis=0)


def dot(left, right):
    return lax.dot_general(left, right, (((1,), (0,)), ((), ())), preferred_element_type=F32)


def dot_t(left, right):
    return lax.dot_general(left, right, (((1,), (1,)), ((), ())), preferred_element_type=F32)


def dot_0(left, right):
    return lax.dot_general(left, right, (((0,), (0,)), ((), ())), preferred_element_type=F32)


def column_tables(column, first, extent):
    col_step = IMAGE // extent
    far_count = extent // LANES
    near = ((column + col_step * iota((LANES, CONTRIB), 1)) & MASK) * iota((LANES, CONTRIB), 0)
    shape = (far_count, CONTRIB)
    far = ((column + col_step * iota(shape, 1)) & MASK) * ((first + LANES * iota(shape, 0)) & MASK)
    return cis(-near), cis(-far)


def near_weights(near):
    real, imag = near
    return block([[real, imag], [-imag, real]]).astype(BF16)


CHUNK = 8
GROUP = LANES // PATCH


def cell_of(lane):
    half, inside = lane // LANES, lane % LANES
    return (half * GROUP + inside % GROUP) * PATCH + inside // GROUP


def phase_kernel(column_ref, offsets_ref, near_ref, far_ref, weights_ref):
    extent = far_ref.shape[1] * LANES
    first = offsets_ref[pl.ds(lax.axis_index("facet"), 1), 1:2]
    near, far = column_tables(column_ref[0], first, extent)
    near_ref[...] = near_weights(near)
    far_ref[0], far_ref[1] = far
    for h in range(SUBGRID // LANES):
        shape = (CONTRIB, LANES)
        tr, ti = cis(iota(shape, 0) * cell_of(iota(shape, 1) + h * LANES) * STEP)
        weights_ref[:, 2 * h * LANES : 2 * (h + 1) * LANES] = block([[tr, ti], [-ti, tr]]).astype(BF16)


def column_kernel(near_ref, far_ref, image_ref, out_ref):
    rows, extent = image_ref.shape[2:]
    far_count = extent // LANES
    real = jnp.zeros((rows, CONTRIB), F32)
    imag = jnp.zeros((rows, CONTRIB), F32)
    left = [
        jnp.concatenate([image_ref[0, ri, :, pl.ds(y1 * LANES, LANES)] for ri in range(2)], axis=1)
        for y1 in range(far_count)
    ]
    value = dot(jnp.concatenate(left, axis=0), near_ref[...])
    for y1 in range(far_count):
        part = value[y1 * rows : (y1 + 1) * rows]
        here = pl.ds(y1, 1)
        pr, pi = times(part[:, :CONTRIB], part[:, CONTRIB:], far_ref[0, here], far_ref[1, here])
        real += pr
        imag += pi
    scale = 1.0 / math.sqrt(extent)
    both = jnp.stack([(real * scale).astype(BF16), (imag * scale).astype(BF16)])
    for member in range(out_ref.shape[0]):
        out_ref[member] = both


def row_of(position):
    inside = position % PATCH
    half = PATCH // 2
    return position - inside + jnp.where(inside < half, half - 1 - inside, inside)


def row_tables(starts_ref, offsets_ref, facets, block_rows, facet_rows):
    half_step = IMAGE // facet_rows // 2
    owners = SUBGRID // block_rows
    index = lax.axis_index("freq") * lax.axis_size("facet") + lax.axis_index("facet")
    start = starts_ref[index // owners]
    shape = (block_rows, facet_rows)
    row = (index % owners) * block_rows + row_of(iota(shape, 0))
    half = (STEP // 2) * row - half_step * iota(shape, 1)
    top = cis(CONTRIB * half)[1]
    low = cis(half)[1]
    even = (half & (IMAGE // 2 - 1)) == 0
    limit = jnp.where((half & MASK) == 0, float(CONTRIB), -float(CONTRIB))
    kernel = jnp.where(even, limit, top / jnp.where(even, 1.0, low)) * (1.0 / math.sqrt(facet_rows))
    by_place = (facets, facet_rows)
    by_row = (block_rows, LANES)
    firsts = jnp.zeros(by_place, jnp.int32)
    lane_firsts = jnp.zeros(by_row, jnp.int32)
    for f in range(facets):
        firsts = jnp.where(iota(by_place, 0) == f, offsets_ref[f, 0], firsts)
        lane_firsts = jnp.where(iota(by_row, 1) == f, offsets_ref[f, 0], lane_firsts)
    place = firsts + iota(by_place, 1)
    place_real, place_imag = cis(
        -start * (place & MASK) - (CONTRIB - 1) * half_step * (place & (facet_rows - 1))
    )
    row_real, row_imag = cis(
        ((index % owners) * block_rows + row_of(iota(by_row, 0)))
        * (lane_firsts + (CONTRIB - 1) * (STEP // 2))
    )
    tables = []
    for f in range(facets):
        shift = (facet_rows - offsets_ref[f, 0] % facet_rows) % facet_rows
        rolled = pltpu.roll(kernel, shift, 1)
        real, imag = times(
            row_real[:, f : f + 1], row_imag[:, f : f + 1], place_real[f : f + 1], place_imag[f : f + 1]
        )
        tables.append((rolled * real, rolled * imag))
    return tables


def patch_start(coords):
    twice = jnp.concatenate([coords, coords], axis=0)
    real, imag = cis(twice * (IMAGE // PERIOD))
    first = iota(twice.shape, 0) < GROUP
    return (jnp.where(first, 1.0, real), jnp.where(first, 0.0, imag)), times(real, imag, real, imag)


def table_kernel(
    piece_rows,
    starts_vmem,
    offsets_vmem,
    coords_ref,
    rows_ref,
    shift_ref,
    wave_ref,
    centre_ref,
    ev_ref,
    starts_ref,
    offsets_ref,
    plain_ref,
    sem,
):
    small = [
        pltpu.make_async_copy(starts_vmem, starts_ref, sem.at[0]),
        pltpu.make_async_copy(offsets_vmem, offsets_ref, sem.at[1]),
    ]
    for copy in small:
        copy.start()
    facets = offsets_ref.shape[0]
    patch_rows = coords_ref.shape[1]
    block_rows = patch_rows * PATCH
    for p in range(patch_rows):
        for h in range(SIDE // GROUP):
            here = pl.ds(h * GROUP, GROUP)
            twice = jnp.concatenate([coords_ref[0, p, here, :]] * 2, axis=0)
            odd = jnp.where(iota(twice.shape, 0) < GROUP, 1, 3)
            half_turn = IMAGE // PERIOD // 2
            centre_ref[p, h, 0], centre_ref[p, h, 1] = cis(twice * ((PATCH - 1) * half_turn))
            power, step = cis(twice * odd * half_turn), cis(twice * (4 * half_turn))
            for k in range(PATCH // 4):
                for ri in range(2):
                    wave_ref[p, h, ri, pl.ds(k * 2 * GROUP, 2 * GROUP), :] = power[ri]
                power = times(*power, *step)
            power, step = patch_start(coords_ref[1, p, here, :])
            for k in range(PATCH // 2):
                for ri in range(2):
                    to = pl.ds(ri * LANES + k * 2 * GROUP, 2 * GROUP)
                    ev_ref[p, h, to, :] = power[ri].astype(BF16)
                power = times(*power, *step)
    for copy in small:
        copy.wait()
    facet_rows = rows_ref.shape[2] // 2
    tables = row_tables(starts_ref, offsets_ref, facets, block_rows, facet_rows)
    for f, (mr, mi) in enumerate(tables):
        plain_ref[f * 2 * block_rows : (2 * f + 1) * block_rows] = mr.astype(BF16)
        plain_ref[(2 * f + 1) * block_rows : (f + 1) * 2 * block_rows] = mi.astype(BF16)
    shape = (facet_rows, facet_rows)
    half, inside = iota(shape, 1) // (facet_rows // 2), iota(shape, 1) % (facet_rows // 2)
    core = (lax.axis_index("freq") + half) % 2
    place = (2 * (inside // piece_rows) + core) * piece_rows + inside % piece_rows
    order = (iota(shape, 0) == place).astype(F32).astype(BF16)
    ordered = dot(plain_ref[...], order).astype(BF16)
    for f in range(facets):
        here = ordered[f * 2 * block_rows : (f + 1) * 2 * block_rows]
        rows_ref[f, :, :facet_rows] = here
        rows_ref[f, :block_rows, facet_rows:] = -here[block_rows:]
        rows_ref[f, block_rows:, facet_rows:] = here[:block_rows]
    shape = (facets, SUBGRID)
    firsts = jnp.zeros(shape, jnp.int32)
    for f in range(facets):
        firsts = jnp.where(iota(shape, 0) == f, offsets_ref[f, 1], firsts)
    for ri, value in enumerate(cis(firsts * cell_of(iota(shape, 1)))):
        shift_ref[ri] = value * (1.0 / CONTRIB)


def grid_kernel(
    own_ref,
    other_ref,
    rows_ref,
    weights_ref,
    shift_ref,
    wave_ref,
    centre_ref,
    ev_ref,
    seen_ref,
    narrowed_ref,
    give_ref,
    res_hbm,
    res_ref,
    left_ref,
    grid_ref,
    back_ref,
    both_ref,
    narrow_ref,
    res_sem,
):
    facets = rows_ref.shape[0]
    pairs = own_ref.shape[0] // facets
    patch_rows = seen_ref.shape[1]
    block_rows = patch_rows * PATCH
    vis = seen_ref.shape[3]
    for f in range(facets):
        right = [
            ref[y * facets + f, ri] for ri in range(2) for ref in (own_ref, other_ref) for y in range(pairs)
        ]
        part = dot(rows_ref[f], jnp.concatenate(right, axis=0)).astype(BF16)
        for ri in range(2):
            to = (pl.ds(f * block_rows, block_rows), pl.ds(ri * CONTRIB, CONTRIB))
            left_ref[to] = part[ri * block_rows : (ri + 1) * block_rows]
    shift_real, shift_imag = shift_ref[0], shift_ref[1]
    halves = SUBGRID // LANES
    pair = 2 * GROUP
    tile = (pair, LANES)
    same = iota(tile, 0) % GROUP == iota(tile, 1) % GROUP
    upper, lower = same & (iota(tile, 0) < GROUP), same & (iota(tile, 0) >= GROUP)
    own = iota((PATCH, LANES), 1) % GROUP

    def predicted(h):
        wide = dot(left_ref[...], weights_ref[:, 2 * h * LANES : 2 * (h + 1) * LANES])
        total = [jnp.zeros((block_rows, LANES), F32)] * 2
        for f in range(facets):
            part = wide[f * block_rows : (f + 1) * block_rows]
            lanes = slice(h * LANES, (h + 1) * LANES)
            made = times(
                part[:, :LANES], part[:, LANES:], shift_real[f : f + 1, lanes], shift_imag[f : f + 1, lanes]
            )
            total = [old + new for old, new in zip(total, made)]
        for ri in range(2):
            grid_ref[h, ri] = total[ri].astype(BF16).astype(F32)

    def degrid(p, h):
        middle = PATCH // 2
        made = []
        for ri in range(2):
            sums, differences = [], []
            for k in range(0, middle, 2):
                after, before = (
                    [grid_ref[h, ri, pl.ds(p * PATCH + at + k + i, 1), :] for i in range(2)]
                    for at in (middle, 0)
                )
                add = [one + two for one, two in zip(after, before)]
                take = [one - two for one, two in zip(after, before)]
                for tiles, (one, two) in ((sums, add), (differences, take)):
                    tiles.append(jnp.where(upper, one, jnp.where(lower, two, 0.0)))
            made.append([jnp.concatenate(tiles, axis=0).astype(BF16) for tiles in (sums, differences)])
        (sr, dr), (si, di) = made
        return dot(block([[sr, -si], [si, sr], [dr, -di], [di, dr]]), ev_ref[p, h])

    def weigh(p, h, inner):
        height = LANES // 2
        sums = [jnp.zeros((pair, vis), F32)] * 2
        for k in range(0, height, pair):
            cosine, sine = (wave_ref[p, h, ri, pl.ds(k, pair), :] for ri in range(2))
            sr, si, dr, di = (inner[at + k : at + k + pair] for at in range(0, 4 * height, height))
            sums = [sums[0] + (cosine * sr - sine * di), sums[1] + (cosine * si + sine * dr)]
        centre = centre_ref[p, h, 0], centre_ref[p, h, 1]
        sums = times(*(value + pltpu.roll(value, GROUP, 0) for value in sums), *centre)
        res = []
        for ri, value in enumerate(sums):
            model = value * (1.0 / PATCH)
            seen = seen_ref[ri, p, pl.ds(h * GROUP, GROUP), :].astype(F32)
            rounded = (jnp.concatenate([seen, seen], axis=0) - model).astype(BF16)
            res_ref[ri, p, pl.ds(h * GROUP, GROUP), :] = rounded[:GROUP]
            res.append(rounded.astype(F32))
        res = times_conj(*res, *centre)
        weighted = [
            wave_ref[p, h, wave, pl.ds(k, pair), :] * res[ri]
            for wave in range(2)
            for ri in range(2)
            for k in range(0, height, pair)
        ]
        return jnp.concatenate(weighted, axis=0).astype(BF16)

    def regrid(p, h, back):
        height = LANES // 2
        quarters = [back[at : at + height] for at in range(0, 4 * height, height)]
        near, far = [part[:, :LANES] for part in quarters], [part[:, LANES:] for part in quarters]
        ar, ai = near[0] + far[1], near[1] - far[0]
        br, bi = near[2] + far[3], near[3] - far[2]
        both_ref[p, h, 0, :height], both_ref[p, h, 0, height:] = ar - bi, ar + bi
        both_ref[p, h, 1, :height], both_ref[p, h, 1, height:] = ai + br, ai - br
        for ri in range(2):
            cells = both_ref[p, h, ri, pl.ds(0, PATCH, stride=GROUP), :]
            for c in range(1, GROUP):
                cells = jnp.where(own == c, both_ref[p, h, ri, pl.ds(c, PATCH, stride=GROUP), :], cells)
            back_ref[h, ri, pl.ds(p * PATCH, PATCH), :] = cells.astype(BF16).astype(F32)

    def widen(h):
        for f in range(facets):
            lanes = slice(h * LANES, (h + 1) * LANES)
            made = times_conj(
                back_ref[h, 0], back_ref[h, 1], shift_real[f : f + 1, lanes], shift_imag[f : f + 1, lanes]
            )
            for ri in range(2):
                to = (2 * h + ri) * LANES
                narrow_ref[pl.ds(f * block_rows, block_rows), to : to + LANES] = made[ri].astype(BF16)

    tasks = [(p, h) for h in range(halves) for p in range(patch_rows)]
    inner, back = {}, {}
    for h in range(halves):
        predicted(h)
        for p in range(patch_rows):
            inner[p, h] = degrid(p, h)
    narrowed = []

    def finish(task):
        regrid(*task, back.pop(task))
        p, h = task
        if p == patch_rows - 1:
            widen(h)
            lanes = pl.ds(2 * h * LANES, 2 * LANES)
            narrowed.append(dot_t(narrow_ref[:, lanes], weights_ref[:, lanes]))

    for at, task in enumerate(tasks):
        left = weigh(*task, inner.pop(task))
        back[task] = dot_t(left, ev_ref[task[0], task[1]])
        if at:
            finish(tasks[at - 1])
    result = pltpu.make_async_copy(res_ref, res_hbm, res_sem)
    result.start()
    finish(tasks[-1])
    narrowed_ref[...] = sum(narrowed).astype(BF16)
    adjoint_rows(1, rows_ref, narrowed_ref, give_ref)
    result.wait()


def adjoint_rows(half, rows_ref, narrowed_ref, out_ref):
    facets, height, facet_rows = rows_ref.shape[0], rows_ref.shape[1], rows_ref.shape[2] // 2
    block_rows = height // 2
    pairs = out_ref.shape[0] // facets
    piece_rows = out_ref.shape[2]
    for f in range(facets):
        here = pl.ds(f * block_rows, block_rows)
        real, imag = narrowed_ref[here, :CONTRIB], narrowed_ref[here, CONTRIB:]
        lanes = pl.ds(half * (facet_rows // 2), facet_rows // 2)
        product = dot_0(rows_ref[f, :, lanes], block([[real, imag], [imag, -real]])).astype(BF16)
        for y in range(pairs):
            for ri in range(2):
                out_ref[y * facets + f, ri] = product[
                    y * piece_rows : (y + 1) * piece_rows, ri * CONTRIB : (ri + 1) * CONTRIB
                ]


def image_kernel(scale, in_ref, near_ref, far_ref, out_hbm, stage_ref, sem):
    parts = in_ref.shape[0]
    rows, extent = out_hbm.shape[2:]
    far_count = extent // LANES
    real, imag = (
        sum(in_ref[q, ri].astype(F32) for q in range(parts)) * scale for ri in range(2)
    )
    copies = []
    for top in range(0, far_count, CHUNK):
        left = []
        for y1 in range(top, top + CHUNK):
            ar, ai = times_conj(real, imag, far_ref[0, y1 : y1 + 1], far_ref[1, y1 : y1 + 1])
            left.append(jnp.concatenate([ar, ai], axis=1).astype(BF16))
        value = dot_t(jnp.concatenate(left, axis=0), near_ref[...])
        value = (value * (1.0 / math.sqrt(CONTRIB))).astype(BF16)
        for y1 in range(CHUNK):
            for ri in range(2):
                stage_ref[ri, :, pl.ds((top + y1) * LANES, LANES)] = value[
                    y1 * rows : (y1 + 1) * rows, ri * LANES : (ri + 1) * LANES
                ]
        for ri in range(2):
            span = pl.ds(top * LANES, CHUNK * LANES)
            copy = pltpu.make_async_copy(
                stage_ref.at[ri, :, span], out_hbm.at[0, ri, :, span], sem.at[len(copies)]
            )
            copy.start()
            copies.append(copy)
    for copy in copies:
        copy.wait()


HBM = pl.BlockSpec(memory_space=pltpu.HBM)
SMEM = pl.BlockSpec(memory_space=pltpu.SMEM)
VMEM = pl.BlockSpec(memory_space=pltpu.VMEM)


def call(kernel, name, operands, in_specs, outs, scratch=(), out_specs=None, flops=None):
    return pl.pallas_call(
        kernel,
        name=name,
        out_shape=outs,
        in_specs=in_specs,
        out_specs=out_specs or jax.tree.map(lambda _: VMEM, outs),
        scratch_shapes=list(scratch),
        cost_estimate=flops and pl.CostEstimate(flops=flops, bytes_accessed=0, transcendentals=0),
        compiler_params=pltpu.CompilerParams(vmem_limit_bytes=40 * 1024 * 1024),
    )(*operands)


def on_device(facet_image, facet_offsets, subgrid_rows, column_offset, uv_coords, observed):
    shape = jax.ShapeDtypeStruct
    rows, extent = facet_image.shape[2:]
    facets = lax.axis_size("facet")
    parts = lax.axis_size("freq")
    subgrids = subgrid_rows.shape[0]
    block_rows = uv_coords.shape[1] * PATCH
    members = facets * parts // 2
    groups = [
        [(2 * y + c) * facets + f for y in range(parts // 2) for f in range(facets)]
        for c in range(2)
    ]

    def exchange(value):
        return lax.all_to_all(
            value, ("freq", "facet"), split_axis=0, concat_axis=0, axis_index_groups=groups, tiled=True
        )

    def swap(value):
        return lax.ppermute(value, "freq", [(q, q ^ 1) for q in range(parts)])

    pieces = shape((members, 2, rows, CONTRIB), BF16)
    far_count = extent // LANES
    near, far, weights = call(
        phase_kernel,
        "phase",
        (column_offset, facet_offsets),
        [SMEM, VMEM],
        (
            shape((2 * LANES, 2 * CONTRIB), BF16),
            shape((2, far_count, CONTRIB), F32),
            shape((2 * CONTRIB, 2 * SUBGRID), BF16),
        ),
        flops=200_000_000,
    )
    transformed = call(
        column_kernel,
        "column",
        (near, far, facet_image),
        [VMEM] * 3,
        pieces,
    )
    own = exchange(transformed)
    other = swap(own)
    patch_rows, vis = uv_coords.shape[1], uv_coords.shape[3]
    halves = SIDE * PATCH // LANES
    row_products, *tables = call(
        functools.partial(table_kernel, rows),
        "tables",
        (subgrid_rows, facet_offsets, uv_coords),
        [VMEM, VMEM, VMEM],
        (
            shape((facets, 2 * block_rows, 2 * parts * rows), BF16),
            shape((2, facets, SUBGRID), F32),
            shape((patch_rows, halves, 2, LANES // 2, vis), F32),
            shape((patch_rows, halves, 2, 2 * GROUP, vis), F32),
            shape((patch_rows, halves, 2 * LANES, vis), BF16),
        ),
        (
            pltpu.SMEM(subgrid_rows.shape, jnp.int32),
            pltpu.SMEM(facet_offsets.shape, jnp.int32),
            pltpu.VMEM((facets * 2 * block_rows, parts * rows), BF16),
            pltpu.SemaphoreType.DMA((2,)),
        ),
    )
    narrowed, give, residual_vis = call(
        grid_kernel,
        "grid",
        (own, other, row_products, weights, *tables, observed),
        [VMEM] * 9,
        (
            shape((facets * block_rows, 2 * CONTRIB), BF16),
            pieces,
            shape(observed.shape, BF16),
        ),
        (
            pltpu.VMEM(observed.shape, BF16),
            pltpu.VMEM((facets * block_rows, 2 * CONTRIB), BF16),
            pltpu.VMEM((halves, 2, block_rows, LANES), F32),
            pltpu.VMEM((halves, 2, block_rows, LANES), F32),
            pltpu.VMEM((patch_rows, halves, 2, LANES, LANES), F32),
            pltpu.VMEM((facets * block_rows, 2 * SUBGRID), BF16),
            pltpu.SemaphoreType.DMA,
        ),
        (VMEM, VMEM, HBM),
    )
    keep = call(
        functools.partial(adjoint_rows, 0),
        "keep",
        (row_products, narrowed),
        [VMEM] * 2,
        pieces,
    )
    partial = (keep.astype(F32) + swap(give).astype(F32)).astype(BF16)
    shared_scale = 1.0 / CONTRIB / math.sqrt(parts * rows)
    scale = 1.0 / (math.sqrt(vis) * SUBGRID * math.sqrt(subgrids * CONTRIB) * shared_scale)
    image_residual = call(
        functools.partial(image_kernel, scale),
        "image",
        (exchange(partial), near, far),
        [VMEM] * 3,
        shape(facet_image.shape, BF16),
        (
            pltpu.VMEM(facet_image.shape[1:], BF16),
            pltpu.SemaphoreType.DMA((2 * far_count // CHUNK,)),
        ),
        HBM,
    )
    return (image_residual, residual_vis)


def solution(mesh):
    return jax.shard_map(
        on_device,
        mesh=mesh,
        in_specs=(
            P("facet", None, "freq", None),
            P(),
            P(),
            P(),
            P(None, ("freq", "facet"), None, None),
            P(None, ("freq", "facet"), None, None),
        ),
        out_specs=(P("facet", None, "freq", None), P(None, ("freq", "facet"), None, None)),
        check_vma=False,
    )
```

```python
import functools
import math

import jax
import jax.numpy as jnp
from jax import lax
from jax.experimental import pallas as pl
from jax.experimental.pallas import tpu as pltpu
from jax.sharding import PartitionSpec as P

IMAGE = 32768
CONTRIB = 128
SUBGRID = 256
PATCH = 32
SIDE = 8
STEP = 128
PERIOD = 256
LANES = 128
MASK = IMAGE - 1

F32 = jnp.float32
BF16 = jnp.bfloat16


def iota(shape, axis):
    return lax.broadcasted_iota(jnp.int32, shape, axis)


def cis(turns):
    turns = turns & MASK
    quarter = (turns + IMAGE // 8) >> 13
    x = (turns - (quarter << 13)).astype(F32) * (2.0 * math.pi / IMAGE)
    x2 = x * x
    sine = x * (1.0 + x2 * (-1.0 / 6 + x2 * (1.0 / 120 - x2 * (1.0 / 5040))))
    cosine = 1.0 + x2 * (-0.5 + x2 * (1.0 / 24 + x2 * (-1.0 / 720 + x2 * (1.0 / 40320))))
    odd = (quarter & 1) == 1
    real = jnp.where(odd, sine, cosine)
    imag = jnp.where(odd, cosine, sine)
    real = jnp.where(((quarter + 1) & 2) == 2, -real, real)
    imag = jnp.where((quarter & 2) == 2, -imag, imag)
    return real, imag


def times(ar, ai, br, bi):
    return ar * br - ai * bi, ar * bi + ai * br


def times_conj(ar, ai, br, bi):
    return ar * br + ai * bi, ai * br - ar * bi


def block(rows):
    return jnp.concatenate([jnp.concatenate(row, axis=1) for row in rows], axis=0)


def dot(left, right):
    return lax.dot_general(left, right, (((1,), (0,)), ((), ())), preferred_element_type=F32)


def dot_t(left, right):
    return lax.dot_general(left, right, (((1,), (1,)), ((), ())), preferred_element_type=F32)


def dot_0(left, right):
    return lax.dot_general(left, right, (((0,), (0,)), ((), ())), preferred_element_type=F32)


def column_tables(column, first, extent):
    col_step = IMAGE // extent
    far_count = extent // LANES
    near = ((column + col_step * iota((LANES, CONTRIB), 1)) & MASK) * iota((LANES, CONTRIB), 0)
    shape = (far_count, CONTRIB)
    far = ((column + col_step * iota(shape, 1)) & MASK) * ((first + LANES * iota(shape, 0)) & MASK)
    return cis(-near), cis(-far)


def near_weights(near):
    real, imag = near
    return block([[real, imag], [-imag, real]]).astype(BF16)


CHUNK = 8
GROUP = LANES // PATCH


def cell_of(lane):
    half, inside = lane // LANES, lane % LANES
    return (half * GROUP + inside % GROUP) * PATCH + inside // GROUP


def phase_kernel(column_ref, offsets_ref, near_ref, far_ref, weights_ref):
    extent = far_ref.shape[1] * LANES
    first = offsets_ref[pl.ds(lax.axis_index("facet"), 1), 1:2]
    near, far = column_tables(column_ref[0], first, extent)
    near_ref[...] = near_weights(near)
    far_ref[0], far_ref[1] = far
    for h in range(SUBGRID // LANES):
        shape = (CONTRIB, LANES)
        tr, ti = cis(iota(shape, 0) * cell_of(iota(shape, 1) + h * LANES) * STEP)
        weights_ref[:, 2 * h * LANES : 2 * (h + 1) * LANES] = block([[tr, ti], [-ti, tr]]).astype(BF16)


def column_kernel(near_ref, far_ref, image_ref, out_ref):
    rows, extent = image_ref.shape[2:]
    far_count = extent // LANES
    real = jnp.zeros((rows, CONTRIB), F32)
    imag = jnp.zeros((rows, CONTRIB), F32)
    left = [
        jnp.concatenate([image_ref[0, ri, :, pl.ds(y1 * LANES, LANES)] for ri in range(2)], axis=1)
        for y1 in range(far_count)
    ]
    value = dot(jnp.concatenate(left, axis=0), near_ref[...])
    for y1 in range(far_count):
        part = value[y1 * rows : (y1 + 1) * rows]
        here = pl.ds(y1, 1)
        pr, pi = times(part[:, :CONTRIB], part[:, CONTRIB:], far_ref[0, here], far_ref[1, here])
        real += pr
        imag += pi
    scale = 1.0 / math.sqrt(extent)
    both = jnp.stack([(real * scale).astype(BF16), (imag * scale).astype(BF16)])
    for member in range(out_ref.shape[0]):
        out_ref[member] = both


def row_of(position):
    inside = position % PATCH
    half = PATCH // 2
    return position - inside + jnp.where(inside < half, half - 1 - inside, inside)


def row_tables(starts_ref, offsets_ref, facets, block_rows, facet_rows):
    half_step = IMAGE // facet_rows // 2
    owners = SUBGRID // block_rows
    index = lax.axis_index("freq") * lax.axis_size("facet") + lax.axis_index("facet")
    start = starts_ref[index // owners]
    shape = (block_rows, facet_rows)
    row = (index % owners) * block_rows + row_of(iota(shape, 0))
    half = (STEP // 2) * row - half_step * iota(shape, 1)
    top = cis(CONTRIB * half)[1]
    low = cis(half)[1]
    even = (half & (IMAGE // 2 - 1)) == 0
    limit = jnp.where((half & MASK) == 0, float(CONTRIB), -float(CONTRIB))
    kernel = jnp.where(even, limit, top / jnp.where(even, 1.0, low)) * (1.0 / math.sqrt(facet_rows))
    by_place = (facets, facet_rows)
    by_row = (block_rows, LANES)
    firsts = jnp.zeros(by_place, jnp.int32)
    lane_firsts = jnp.zeros(by_row, jnp.int32)
    for f in range(facets):
        firsts = jnp.where(iota(by_place, 0) == f, offsets_ref[f, 0], firsts)
        lane_firsts = jnp.where(iota(by_row, 1) == f, offsets_ref[f, 0], lane_firsts)
    place = firsts + iota(by_place, 1)
    place_real, place_imag = cis(
        -start * (place & MASK) - (CONTRIB - 1) * half_step * (place & (facet_rows - 1))
    )
    row_real, row_imag = cis(
        ((index % owners) * block_rows + row_of(iota(by_row, 0)))
        * (lane_firsts + (CONTRIB - 1) * (STEP // 2))
    )
    tables = []
    for f in range(facets):
        shift = (facet_rows - offsets_ref[f, 0] % facet_rows) % facet_rows
        rolled = pltpu.roll(kernel, shift, 1)
        real, imag = times(
            row_real[:, f : f + 1], row_imag[:, f : f + 1], place_real[f : f + 1], place_imag[f : f + 1]
        )
        tables.append((rolled * real, rolled * imag))
    return tables


def patch_start(coords):
    twice = jnp.concatenate([coords, coords], axis=0)
    real, imag = cis(twice * (IMAGE // PERIOD))
    first = iota(twice.shape, 0) < GROUP
    return (jnp.where(first, 1.0, real), jnp.where(first, 0.0, imag)), times(real, imag, real, imag)


def table_kernel(
    piece_rows,
    starts_vmem,
    offsets_vmem,
    coords_ref,
    rows_ref,
    shift_ref,
    wave_ref,
    centre_ref,
    ev_ref,
    starts_ref,
    offsets_ref,
    plain_ref,
    sem,
):
    small = [
        pltpu.make_async_copy(starts_vmem, starts_ref, sem.at[0]),
        pltpu.make_async_copy(offsets_vmem, offsets_ref, sem.at[1]),
    ]
    for copy in small:
        copy.start()
    facets = offsets_ref.shape[0]
    patch_rows = coords_ref.shape[1]
    block_rows = patch_rows * PATCH
    for p in range(patch_rows):
        for h in range(SIDE // GROUP):
            here = pl.ds(h * GROUP, GROUP)
            twice = jnp.concatenate([coords_ref[0, p, here, :]] * 2, axis=0)
            odd = jnp.where(iota(twice.shape, 0) < GROUP, 1, 3)
            half_turn = IMAGE // PERIOD // 2
            centre_ref[p, h, 0], centre_ref[p, h, 1] = cis(twice * ((PATCH - 1) * half_turn))
            power, step = cis(twice * odd * half_turn), cis(twice * (4 * half_turn))
            for k in range(PATCH // 4):
                for ri in range(2):
                    wave_ref[p, h, ri, pl.ds(k * 2 * GROUP, 2 * GROUP), :] = power[ri]
                power = times(*power, *step)
            power, step = patch_start(coords_ref[1, p, here, :])
            for k in range(PATCH // 2):
                for ri in range(2):
                    to = pl.ds(ri * LANES + k * 2 * GROUP, 2 * GROUP)
                    ev_ref[p, h, to, :] = power[ri].astype(BF16)
                power = times(*power, *step)
    for copy in small:
        copy.wait()
    facet_rows = rows_ref.shape[2] // 2
    tables = row_tables(starts_ref, offsets_ref, facets, block_rows, facet_rows)
    kinds = [range(kind, facets, 2) for kind in range(2)]
    height = 2 * block_rows
    for at, f in enumerate([f for kind in kinds for f in kind]):
        mr, mi = tables[f]
        plain_ref[at * height : at * height + block_rows] = mr.astype(BF16)
        plain_ref[at * height + block_rows : (at + 1) * height] = mi.astype(BF16)
    shape = (facet_rows, facet_rows)
    half, inside = iota(shape, 1) // (facet_rows // 2), iota(shape, 1) % (facet_rows // 2)
    ordered = {}
    top = 0
    for kind, members in enumerate(kinds):
        core = (lax.axis_index("freq") + lax.axis_index("facet") + kind + half) % 2
        place = (2 * (inside // piece_rows) + core) * piece_rows + inside % piece_rows
        order = (iota(shape, 0) == place).astype(F32).astype(BF16)
        made = dot(plain_ref[top : top + len(members) * height], order).astype(BF16)
        top += len(members) * height
        for at, f in enumerate(members):
            ordered[f] = made[at * height : (at + 1) * height]
    for f in range(facets):
        here = ordered[f]
        rows_ref[f, :, :facet_rows] = here
        rows_ref[f, :block_rows, facet_rows:] = -here[block_rows:]
        rows_ref[f, block_rows:, facet_rows:] = here[:block_rows]
    shape = (facets, SUBGRID)
    firsts = jnp.zeros(shape, jnp.int32)
    for f in range(facets):
        firsts = jnp.where(iota(shape, 0) == f, offsets_ref[f, 1], firsts)
    for ri, value in enumerate(cis(firsts * cell_of(iota(shape, 1)))):
        shift_ref[ri] = value * (1.0 / CONTRIB)


def grid_kernel(
    own_ref,
    other_ref,
    rows_ref,
    weights_ref,
    shift_ref,
    wave_ref,
    centre_ref,
    ev_ref,
    seen_ref,
    narrowed_ref,
    give_ref,
    res_hbm,
    res_ref,
    left_ref,
    grid_ref,
    back_ref,
    both_ref,
    narrow_ref,
    res_sem,
):
    facets = rows_ref.shape[0]
    pairs = own_ref.shape[0] // facets
    patch_rows = seen_ref.shape[1]
    block_rows = patch_rows * PATCH
    vis = seen_ref.shape[3]
    for f in range(facets):
        right = [
            ref[y * facets + f, ri] for ri in range(2) for ref in (own_ref, other_ref) for y in range(pairs)
        ]
        part = dot(rows_ref[f], jnp.concatenate(right, axis=0)).astype(BF16)
        for ri in range(2):
            to = (pl.ds(f * block_rows, block_rows), pl.ds(ri * CONTRIB, CONTRIB))
            left_ref[to] = part[ri * block_rows : (ri + 1) * block_rows]
    shift_real, shift_imag = shift_ref[0], shift_ref[1]
    halves = SUBGRID // LANES
    pair = 2 * GROUP
    tile = (pair, LANES)
    same = iota(tile, 0) % GROUP == iota(tile, 1) % GROUP
    upper, lower = same & (iota(tile, 0) < GROUP), same & (iota(tile, 0) >= GROUP)
    own = iota((PATCH, LANES), 1) % GROUP

    def predicted(h):
        wide = dot(left_ref[...], weights_ref[:, 2 * h * LANES : 2 * (h + 1) * LANES])
        total = [jnp.zeros((block_rows, LANES), F32)] * 2
        for f in range(facets):
            part = wide[f * block_rows : (f + 1) * block_rows]
            lanes = slice(h * LANES, (h + 1) * LANES)
            made = times(
                part[:, :LANES], part[:, LANES:], shift_real[f : f + 1, lanes], shift_imag[f : f + 1, lanes]
            )
            total = [old + new for old, new in zip(total, made)]
        for ri in range(2):
            grid_ref[h, ri] = total[ri].astype(BF16).astype(F32)

    def degrid(p, h):
        middle = PATCH // 2
        made = []
        for ri in range(2):
            sums, differences = [], []
            for k in range(0, middle, 2):
                after, before = (
                    [grid_ref[h, ri, pl.ds(p * PATCH + at + k + i, 1), :] for i in range(2)]
                    for at in (middle, 0)
                )
                add = [one + two for one, two in zip(after, before)]
                take = [one - two for one, two in zip(after, before)]
                for tiles, (one, two) in ((sums, add), (differences, take)):
                    tiles.append(jnp.where(upper, one, jnp.where(lower, two, 0.0)))
            made.append([jnp.concatenate(tiles, axis=0).astype(BF16) for tiles in (sums, differences)])
        (sr, dr), (si, di) = made
        return dot(block([[sr, -si], [si, sr], [dr, -di], [di, dr]]), ev_ref[p, h])

    def weigh(p, h, inner):
        height = LANES // 2
        sums = [jnp.zeros((pair, vis), F32)] * 2
        for k in range(0, height, pair):
            cosine, sine = (wave_ref[p, h, ri, pl.ds(k, pair), :] for ri in range(2))
            sr, si, dr, di = (inner[at + k : at + k + pair] for at in range(0, 4 * height, height))
            sums = [sums[0] + (cosine * sr - sine * di), sums[1] + (cosine * si + sine * dr)]
        centre = centre_ref[p, h, 0], centre_ref[p, h, 1]
        sums = times(*(value + pltpu.roll(value, GROUP, 0) for value in sums), *centre)
        res = []
        for ri, value in enumerate(sums):
            model = value * (1.0 / PATCH)
            seen = seen_ref[ri, p, pl.ds(h * GROUP, GROUP), :].astype(F32)
            rounded = (jnp.concatenate([seen, seen], axis=0) - model).astype(BF16)
            res_ref[ri, p, pl.ds(h * GROUP, GROUP), :] = rounded[:GROUP]
            res.append(rounded.astype(F32))
        res = times_conj(*res, *centre)
        weighted = [
            wave_ref[p, h, wave, pl.ds(k, pair), :] * res[ri]
            for wave in range(2)
            for ri in range(2)
            for k in range(0, height, pair)
        ]
        return jnp.concatenate(weighted, axis=0).astype(BF16)

    def regrid(p, h, back):
        height = LANES // 2
        quarters = [back[at : at + height] for at in range(0, 4 * height, height)]
        near, far = [part[:, :LANES] for part in quarters], [part[:, LANES:] for part in quarters]
        ar, ai = near[0] + far[1], near[1] - far[0]
        br, bi = near[2] + far[3], near[3] - far[2]
        both_ref[p, h, 0, :height], both_ref[p, h, 0, height:] = ar - bi, ar + bi
        both_ref[p, h, 1, :height], both_ref[p, h, 1, height:] = ai + br, ai - br
        for ri in range(2):
            cells = both_ref[p, h, ri, pl.ds(0, PATCH, stride=GROUP), :]
            for c in range(1, GROUP):
                cells = jnp.where(own == c, both_ref[p, h, ri, pl.ds(c, PATCH, stride=GROUP), :], cells)
            back_ref[h, ri, pl.ds(p * PATCH, PATCH), :] = cells.astype(BF16).astype(F32)

    def widen(h):
        for f in range(facets):
            lanes = slice(h * LANES, (h + 1) * LANES)
            made = times_conj(
                back_ref[h, 0], back_ref[h, 1], shift_real[f : f + 1, lanes], shift_imag[f : f + 1, lanes]
            )
            for ri in range(2):
                to = (2 * h + ri) * LANES
                narrow_ref[pl.ds(f * block_rows, block_rows), to : to + LANES] = made[ri].astype(BF16)

    tasks = [(p, h) for h in range(halves) for p in range(patch_rows)]
    inner, back = {}, {}
    for h in range(halves):
        predicted(h)
        for p in range(patch_rows):
            inner[p, h] = degrid(p, h)
    narrowed = []

    def finish(task):
        regrid(*task, back.pop(task))
        p, h = task
        if p == patch_rows - 1:
            widen(h)
            lanes = pl.ds(2 * h * LANES, 2 * LANES)
            narrowed.append(dot_t(narrow_ref[:, lanes], weights_ref[:, lanes]))

    for at, task in enumerate(tasks):
        left = weigh(*task, inner.pop(task))
        back[task] = dot_t(left, ev_ref[task[0], task[1]])
        if at:
            finish(tasks[at - 1])
    result = pltpu.make_async_copy(res_ref, res_hbm, res_sem)
    result.start()
    finish(tasks[-1])
    narrowed_ref[...] = sum(narrowed).astype(BF16)
    adjoint_rows(1, rows_ref, narrowed_ref, give_ref)
    result.wait()


def adjoint_rows(half, rows_ref, narrowed_ref, out_ref):
    facets, height, facet_rows = rows_ref.shape[0], rows_ref.shape[1], rows_ref.shape[2] // 2
    block_rows = height // 2
    pairs = out_ref.shape[0] // facets
    piece_rows = out_ref.shape[2]
    for f in range(facets):
        here = pl.ds(f * block_rows, block_rows)
        real, imag = narrowed_ref[here, :CONTRIB], narrowed_ref[here, CONTRIB:]
        lanes = pl.ds(half * (facet_rows // 2), facet_rows // 2)
        product = dot_0(rows_ref[f, :, lanes], block([[real, imag], [imag, -real]])).astype(BF16)
        for y in range(pairs):
            for ri in range(2):
                out_ref[y * facets + f, ri] = product[
                    y * piece_rows : (y + 1) * piece_rows, ri * CONTRIB : (ri + 1) * CONTRIB
                ]


def image_kernel(scale, in_ref, near_ref, far_ref, out_hbm, stage_ref, sem):
    parts = in_ref.shape[0]
    rows, extent = out_hbm.shape[2:]
    far_count = extent // LANES
    real, imag = (
        sum(in_ref[q, ri].astype(F32) for q in range(parts)) * scale for ri in range(2)
    )
    copies = []
    for top in range(0, far_count, CHUNK):
        left = []
        for y1 in range(top, top + CHUNK):
            ar, ai = times_conj(real, imag, far_ref[0, y1 : y1 + 1], far_ref[1, y1 : y1 + 1])
            left.append(jnp.concatenate([ar, ai], axis=1).astype(BF16))
        value = dot_t(jnp.concatenate(left, axis=0), near_ref[...])
        value = (value * (1.0 / math.sqrt(CONTRIB))).astype(BF16)
        for y1 in range(CHUNK):
            for ri in range(2):
                stage_ref[ri, :, pl.ds((top + y1) * LANES, LANES)] = value[
                    y1 * rows : (y1 + 1) * rows, ri * LANES : (ri + 1) * LANES
                ]
        for ri in range(2):
            span = pl.ds(top * LANES, CHUNK * LANES)
            copy = pltpu.make_async_copy(
                stage_ref.at[ri, :, span], out_hbm.at[0, ri, :, span], sem.at[len(copies)]
            )
            copy.start()
            copies.append(copy)
    for copy in copies:
        copy.wait()


HBM = pl.BlockSpec(memory_space=pltpu.HBM)
SMEM = pl.BlockSpec(memory_space=pltpu.SMEM)
VMEM = pl.BlockSpec(memory_space=pltpu.VMEM)


def call(kernel, name, operands, in_specs, outs, scratch=(), out_specs=None, flops=None):
    return pl.pallas_call(
        kernel,
        name=name,
        out_shape=outs,
        in_specs=in_specs,
        out_specs=out_specs or jax.tree.map(lambda _: VMEM, outs),
        scratch_shapes=list(scratch),
        cost_estimate=flops and pl.CostEstimate(flops=flops, bytes_accessed=0, transcendentals=0),
        compiler_params=pltpu.CompilerParams(vmem_limit_bytes=40 * 1024 * 1024),
    )(*operands)


def on_device(facet_image, facet_offsets, subgrid_rows, column_offset, uv_coords, observed):
    shape = jax.ShapeDtypeStruct
    rows, extent = facet_image.shape[2:]
    facets = lax.axis_size("facet")
    parts = lax.axis_size("freq")
    subgrids = subgrid_rows.shape[0]
    block_rows = uv_coords.shape[1] * PATCH
    members = facets * parts // 2
    groups = [
        [(2 * y + (c + f) % 2) * facets + f for y in range(parts // 2) for f in range(facets)]
        for c in range(2)
    ]

    def exchange(value):
        return lax.all_to_all(
            value, ("freq", "facet"), split_axis=0, concat_axis=0, axis_index_groups=groups, tiled=True
        )

    def swap(value):
        return lax.ppermute(value, "freq", [(q, q ^ 1) for q in range(parts)])

    pieces = shape((members, 2, rows, CONTRIB), BF16)
    far_count = extent // LANES
    near, far, weights = call(
        phase_kernel,
        "phase",
        (column_offset, facet_offsets),
        [SMEM, VMEM],
        (
            shape((2 * LANES, 2 * CONTRIB), BF16),
            shape((2, far_count, CONTRIB), F32),
            shape((2 * CONTRIB, 2 * SUBGRID), BF16),
        ),
        flops=200_000_000,
    )
    transformed = call(
        column_kernel,
        "column",
        (near, far, facet_image),
        [VMEM] * 3,
        pieces,
    )
    own = exchange(transformed)
    other = swap(own)
    patch_rows, vis = uv_coords.shape[1], uv_coords.shape[3]
    halves = SIDE * PATCH // LANES
    row_products, *tables = call(
        functools.partial(table_kernel, rows),
        "tables",
        (subgrid_rows, facet_offsets, uv_coords),
        [VMEM, VMEM, VMEM],
        (
            shape((facets, 2 * block_rows, 2 * parts * rows), BF16),
            shape((2, facets, SUBGRID), F32),
            shape((patch_rows, halves, 2, LANES // 2, vis), F32),
            shape((patch_rows, halves, 2, 2 * GROUP, vis), F32),
            shape((patch_rows, halves, 2 * LANES, vis), BF16),
        ),
        (
            pltpu.SMEM(subgrid_rows.shape, jnp.int32),
            pltpu.SMEM(facet_offsets.shape, jnp.int32),
            pltpu.VMEM((facets * 2 * block_rows, parts * rows), BF16),
            pltpu.SemaphoreType.DMA((2,)),
        ),
    )
    narrowed, give, residual_vis = call(
        grid_kernel,
        "grid",
        (own, other, row_products, weights, *tables, observed),
        [VMEM] * 9,
        (
            shape((facets * block_rows, 2 * CONTRIB), BF16),
            pieces,
            shape(observed.shape, BF16),
        ),
        (
            pltpu.VMEM(observed.shape, BF16),
            pltpu.VMEM((facets * block_rows, 2 * CONTRIB), BF16),
            pltpu.VMEM((halves, 2, block_rows, LANES), F32),
            pltpu.VMEM((halves, 2, block_rows, LANES), F32),
            pltpu.VMEM((patch_rows, halves, 2, LANES, LANES), F32),
            pltpu.VMEM((facets * block_rows, 2 * SUBGRID), BF16),
            pltpu.SemaphoreType.DMA,
        ),
        (VMEM, VMEM, HBM),
    )
    keep = call(
        functools.partial(adjoint_rows, 0),
        "keep",
        (row_products, narrowed),
        [VMEM] * 2,
        pieces,
    )
    partial = (keep.astype(F32) + swap(give).astype(F32)).astype(BF16)
    shared_scale = 1.0 / CONTRIB / math.sqrt(parts * rows)
    scale = 1.0 / (math.sqrt(vis) * SUBGRID * math.sqrt(subgrids * CONTRIB) * shared_scale)
    image_residual = call(
        functools.partial(image_kernel, scale),
        "image",
        (exchange(partial), near, far),
        [VMEM] * 3,
        shape(facet_image.shape, BF16),
        (
            pltpu.VMEM(facet_image.shape[1:], BF16),
            pltpu.SemaphoreType.DMA((2 * far_count // CHUNK,)),
        ),
        HBM,
    )
    return (image_residual, residual_vis)


def solution(mesh):
    return jax.shard_map(
        on_device,
        mesh=mesh,
        in_specs=(
            P("facet", None, "freq", None),
            P(),
            P(),
            P(),
            P(None, ("freq", "facet"), None, None),
            P(None, ("freq", "facet"), None, None),
        ),
        out_specs=(P("facet", None, "freq", None), P(None, ("freq", "facet"), None, None)),
        check_vma=False,
    )
```

```python
import functools
import math

import jax
import jax.numpy as jnp
from jax import lax
from jax.experimental import pallas as pl
from jax.experimental.pallas import tpu as pltpu
from jax.sharding import PartitionSpec as P

IMAGE = 32768
CONTRIB = 128
SUBGRID = 256
PATCH = 32
SIDE = 8
STEP = 128
PERIOD = 256
LANES = 128
MASK = IMAGE - 1

F32 = jnp.float32
BF16 = jnp.bfloat16


def iota(shape, axis):
    return lax.broadcasted_iota(jnp.int32, shape, axis)


def cis(turns):
    turns = turns & MASK
    quarter = (turns + IMAGE // 8) >> 13
    x = (turns - (quarter << 13)).astype(F32) * (2.0 * math.pi / IMAGE)
    x2 = x * x
    sine = x * (1.0 + x2 * (-1.0 / 6 + x2 * (1.0 / 120 - x2 * (1.0 / 5040))))
    cosine = 1.0 + x2 * (-0.5 + x2 * (1.0 / 24 + x2 * (-1.0 / 720 + x2 * (1.0 / 40320))))
    odd = (quarter & 1) == 1
    real = jnp.where(odd, sine, cosine)
    imag = jnp.where(odd, cosine, sine)
    real = jnp.where(((quarter + 1) & 2) == 2, -real, real)
    imag = jnp.where((quarter & 2) == 2, -imag, imag)
    return real, imag


def times(ar, ai, br, bi):
    return ar * br - ai * bi, ar * bi + ai * br


def times_conj(ar, ai, br, bi):
    return ar * br + ai * bi, ai * br - ar * bi


def block(rows):
    return jnp.concatenate([jnp.concatenate(row, axis=1) for row in rows], axis=0)


def dot(left, right):
    return lax.dot_general(left, right, (((1,), (0,)), ((), ())), preferred_element_type=F32)


def dot_t(left, right):
    return lax.dot_general(left, right, (((1,), (1,)), ((), ())), preferred_element_type=F32)


def dot_0(left, right):
    return lax.dot_general(left, right, (((0,), (0,)), ((), ())), preferred_element_type=F32)


def column_tables(column, first, extent):
    col_step = IMAGE // extent
    far_count = extent // LANES
    near = ((column + col_step * iota((LANES, CONTRIB), 1)) & MASK) * iota((LANES, CONTRIB), 0)
    shape = (far_count, CONTRIB)
    far = ((column + col_step * iota(shape, 1)) & MASK) * ((first + LANES * iota(shape, 0)) & MASK)
    return cis(-near), cis(-far)


def near_weights(near):
    real, imag = near
    return block([[real, imag], [-imag, real]]).astype(BF16)


CHUNK = 8
GROUP = LANES // PATCH


def cell_of(lane):
    half, inside = lane // LANES, lane % LANES
    return (half * GROUP + inside % GROUP) * PATCH + inside // GROUP


def phase_kernel(column_ref, offsets_ref, near_ref, far_ref, weights_ref):
    extent = far_ref.shape[1] * LANES
    first = offsets_ref[pl.ds(lax.axis_index("facet"), 1), 1:2]
    near, far = column_tables(column_ref[0], first, extent)
    near_ref[...] = near_weights(near)
    far_ref[0], far_ref[1] = far
    for h in range(SUBGRID // LANES):
        shape = (CONTRIB, LANES)
        tr, ti = cis(iota(shape, 0) * cell_of(iota(shape, 1) + h * LANES) * STEP)
        weights_ref[:, 2 * h * LANES : 2 * (h + 1) * LANES] = block([[tr, ti], [-ti, tr]]).astype(BF16)


def column_kernel(near_ref, far_ref, image_ref, out_ref):
    rows, extent = image_ref.shape[2:]
    far_count = extent // LANES
    real = jnp.zeros((rows, CONTRIB), F32)
    imag = jnp.zeros((rows, CONTRIB), F32)
    left = [
        jnp.concatenate([image_ref[0, ri, :, pl.ds(y1 * LANES, LANES)] for ri in range(2)], axis=1)
        for y1 in range(far_count)
    ]
    value = dot(jnp.concatenate(left, axis=0), near_ref[...])
    for y1 in range(far_count):
        part = value[y1 * rows : (y1 + 1) * rows]
        here = pl.ds(y1, 1)
        pr, pi = times(part[:, :CONTRIB], part[:, CONTRIB:], far_ref[0, here], far_ref[1, here])
        real += pr
        imag += pi
    scale = 1.0 / math.sqrt(extent)
    both = jnp.stack([(real * scale).astype(BF16), (imag * scale).astype(BF16)])
    for member in range(out_ref.shape[0]):
        out_ref[member] = both


def row_of(position):
    inside = position % PATCH
    half = PATCH // 2
    return position - inside + jnp.where(inside < half, half - 1 - inside, inside)


def row_tables(starts_ref, offsets_ref, facets, block_rows, facet_rows):
    half_step = IMAGE // facet_rows // 2
    owners = SUBGRID // block_rows
    index = lax.axis_index("freq") * lax.axis_size("facet") + lax.axis_index("facet")
    start = starts_ref[index // owners]
    shape = (block_rows, facet_rows)
    row = (index % owners) * block_rows + row_of(iota(shape, 0))
    half = (STEP // 2) * row - half_step * iota(shape, 1)
    top = cis(CONTRIB * half)[1]
    low = cis(half)[1]
    even = (half & (IMAGE // 2 - 1)) == 0
    limit = jnp.where((half & MASK) == 0, float(CONTRIB), -float(CONTRIB))
    kernel = jnp.where(even, limit, top / jnp.where(even, 1.0, low)) * (1.0 / math.sqrt(facet_rows))
    by_place = (facets, facet_rows)
    by_row = (block_rows, LANES)
    firsts = jnp.zeros(by_place, jnp.int32)
    lane_firsts = jnp.zeros(by_row, jnp.int32)
    for f in range(facets):
        firsts = jnp.where(iota(by_place, 0) == f, offsets_ref[f, 0], firsts)
        lane_firsts = jnp.where(iota(by_row, 1) == f, offsets_ref[f, 0], lane_firsts)
    place = firsts + iota(by_place, 1)
    place_real, place_imag = cis(
        -start * (place & MASK) - (CONTRIB - 1) * half_step * (place & (facet_rows - 1))
    )
    row_real, row_imag = cis(
        ((index % owners) * block_rows + row_of(iota(by_row, 0)))
        * (lane_firsts + (CONTRIB - 1) * (STEP // 2))
    )
    tables = []
    for f in range(facets):
        shift = (facet_rows - offsets_ref[f, 0] % facet_rows) % facet_rows
        rolled = pltpu.roll(kernel, shift, 1)
        real, imag = times(
            row_real[:, f : f + 1], row_imag[:, f : f + 1], place_real[f : f + 1], place_imag[f : f + 1]
        )
        tables.append((rolled * real, rolled * imag))
    return tables


def patch_start(coords):
    twice = jnp.concatenate([coords, coords], axis=0)
    real, imag = cis(twice * (IMAGE // PERIOD))
    first = iota(twice.shape, 0) < GROUP
    return (jnp.where(first, 1.0, real), jnp.where(first, 0.0, imag)), times(real, imag, real, imag)


def table_kernel(
    piece_rows,
    starts_vmem,
    offsets_vmem,
    coords_ref,
    rows_ref,
    shift_ref,
    wave_ref,
    centre_ref,
    ev_ref,
    starts_ref,
    offsets_ref,
    plain_ref,
    sem,
):
    small = [
        pltpu.make_async_copy(starts_vmem, starts_ref, sem.at[0]),
        pltpu.make_async_copy(offsets_vmem, offsets_ref, sem.at[1]),
    ]
    for copy in small:
        copy.start()
    facets = offsets_ref.shape[0]
    patch_rows = coords_ref.shape[1]
    block_rows = patch_rows * PATCH
    for p in range(patch_rows):
        for h in range(SIDE // GROUP):
            here = pl.ds(h * GROUP, GROUP)
            twice = jnp.concatenate([coords_ref[0, p, here, :]] * 2, axis=0)
            odd = jnp.where(iota(twice.shape, 0) < GROUP, 1, 3)
            half_turn = IMAGE // PERIOD // 2
            centre_ref[p, h, 0], centre_ref[p, h, 1] = cis(twice * ((PATCH - 1) * half_turn))
            power, step = cis(twice * odd * half_turn), cis(twice * (4 * half_turn))
            for k in range(PATCH // 4):
                for ri in range(2):
                    wave_ref[p, h, ri, pl.ds(k * 2 * GROUP, 2 * GROUP), :] = power[ri]
                power = times(*power, *step)
            power, step = patch_start(coords_ref[1, p, here, :])
            for k in range(PATCH // 2):
                for ri in range(2):
                    to = pl.ds(ri * LANES + k * 2 * GROUP, 2 * GROUP)
                    ev_ref[p, h, to, :] = power[ri].astype(BF16)
                power = times(*power, *step)
    for copy in small:
        copy.wait()
    facet_rows = rows_ref.shape[2] // 2
    tables = row_tables(starts_ref, offsets_ref, facets, block_rows, facet_rows)
    kinds = [range(kind, facets, 2) for kind in range(2)]
    height = 2 * block_rows
    for at, f in enumerate([f for kind in kinds for f in kind]):
        mr, mi = tables[f]
        plain_ref[at * height : at * height + block_rows] = mr.astype(BF16)
        plain_ref[at * height + block_rows : (at + 1) * height] = mi.astype(BF16)
    shape = (facet_rows, facet_rows)
    half, inside = iota(shape, 1) // (facet_rows // 2), iota(shape, 1) % (facet_rows // 2)
    ordered = {}
    top = 0
    for kind, members in enumerate(kinds):
        pair = lax.axis_index("freq") // 2 + inside // piece_rows
        core = (lax.axis_index("freq") + lax.axis_index("facet") + kind + half + pair) % 2
        place = (2 * (inside // piece_rows) + core) * piece_rows + inside % piece_rows
        order = (iota(shape, 0) == place).astype(F32).astype(BF16)
        made = dot(plain_ref[top : top + len(members) * height], order).astype(BF16)
        top += len(members) * height
        for at, f in enumerate(members):
            ordered[f] = made[at * height : (at + 1) * height]
    for f in range(facets):
        here = ordered[f]
        rows_ref[f, :, :facet_rows] = here
        rows_ref[f, :block_rows, facet_rows:] = -here[block_rows:]
        rows_ref[f, block_rows:, facet_rows:] = here[:block_rows]
    shape = (facets, SUBGRID)
    firsts = jnp.zeros(shape, jnp.int32)
    for f in range(facets):
        firsts = jnp.where(iota(shape, 0) == f, offsets_ref[f, 1], firsts)
    for ri, value in enumerate(cis(firsts * cell_of(iota(shape, 1)))):
        shift_ref[ri] = value * (1.0 / CONTRIB)


def grid_kernel(
    own_ref,
    other_ref,
    rows_ref,
    weights_ref,
    shift_ref,
    wave_ref,
    centre_ref,
    ev_ref,
    seen_ref,
    narrowed_ref,
    give_ref,
    res_hbm,
    res_ref,
    left_ref,
    grid_ref,
    back_ref,
    both_ref,
    narrow_ref,
    res_sem,
):
    facets = rows_ref.shape[0]
    pairs = own_ref.shape[0] // facets
    patch_rows = seen_ref.shape[1]
    block_rows = patch_rows * PATCH
    vis = seen_ref.shape[3]
    for f in range(facets):
        right = [
            ref[y * facets + f, ri] for ri in range(2) for ref in (own_ref, other_ref) for y in range(pairs)
        ]
        part = dot(rows_ref[f], jnp.concatenate(right, axis=0)).astype(BF16)
        for ri in range(2):
            to = (pl.ds(f * block_rows, block_rows), pl.ds(ri * CONTRIB, CONTRIB))
            left_ref[to] = part[ri * block_rows : (ri + 1) * block_rows]
    shift_real, shift_imag = shift_ref[0], shift_ref[1]
    halves = SUBGRID // LANES
    pair = 2 * GROUP
    tile = (pair, LANES)
    same = iota(tile, 0) % GROUP == iota(tile, 1) % GROUP
    upper, lower = same & (iota(tile, 0) < GROUP), same & (iota(tile, 0) >= GROUP)
    own = iota((PATCH, LANES), 1) % GROUP

    def predicted(h):
        wide = dot(left_ref[...], weights_ref[:, 2 * h * LANES : 2 * (h + 1) * LANES])
        total = [jnp.zeros((block_rows, LANES), F32)] * 2
        for f in range(facets):
            part = wide[f * block_rows : (f + 1) * block_rows]
            lanes = slice(h * LANES, (h + 1) * LANES)
            made = times(
                part[:, :LANES], part[:, LANES:], shift_real[f : f + 1, lanes], shift_imag[f : f + 1, lanes]
            )
            total = [old + new for old, new in zip(total, made)]
        for ri in range(2):
            grid_ref[h, ri] = total[ri].astype(BF16).astype(F32)

    def degrid(p, h):
        middle = PATCH // 2
        made = []
        for ri in range(2):
            sums, differences = [], []
            for k in range(0, middle, 2):
                after, before = (
                    [grid_ref[h, ri, pl.ds(p * PATCH + at + k + i, 1), :] for i in range(2)]
                    for at in (middle, 0)
                )
                add = [one + two for one, two in zip(after, before)]
                take = [one - two for one, two in zip(after, before)]
                for tiles, (one, two) in ((sums, add), (differences, take)):
                    tiles.append(jnp.where(upper, one, jnp.where(lower, two, 0.0)))
            made.append([jnp.concatenate(tiles, axis=0).astype(BF16) for tiles in (sums, differences)])
        (sr, dr), (si, di) = made
        return dot(block([[sr, -si], [si, sr], [dr, -di], [di, dr]]), ev_ref[p, h])

    def weigh(p, h, inner):
        height = LANES // 2
        sums = [jnp.zeros((pair, vis), F32)] * 2
        for k in range(0, height, pair):
            cosine, sine = (wave_ref[p, h, ri, pl.ds(k, pair), :] for ri in range(2))
            sr, si, dr, di = (inner[at + k : at + k + pair] for at in range(0, 4 * height, height))
            sums = [sums[0] + (cosine * sr - sine * di), sums[1] + (cosine * si + sine * dr)]
        centre = centre_ref[p, h, 0], centre_ref[p, h, 1]
        sums = times(*(value + pltpu.roll(value, GROUP, 0) for value in sums), *centre)
        res = []
        for ri, value in enumerate(sums):
            model = value * (1.0 / PATCH)
            seen = seen_ref[ri, p, pl.ds(h * GROUP, GROUP), :].astype(F32)
            rounded = (jnp.concatenate([seen, seen], axis=0) - model).astype(BF16)
            res_ref[ri, p, pl.ds(h * GROUP, GROUP), :] = rounded[:GROUP]
            res.append(rounded.astype(F32))
        res = times_conj(*res, *centre)
        weighted = [
            wave_ref[p, h, wave, pl.ds(k, pair), :] * res[ri]
            for wave in range(2)
            for ri in range(2)
            for k in range(0, height, pair)
        ]
        return jnp.concatenate(weighted, axis=0).astype(BF16)

    def regrid(p, h, back):
        height = LANES // 2
        quarters = [back[at : at + height] for at in range(0, 4 * height, height)]
        near, far = [part[:, :LANES] for part in quarters], [part[:, LANES:] for part in quarters]
        ar, ai = near[0] + far[1], near[1] - far[0]
        br, bi = near[2] + far[3], near[3] - far[2]
        both_ref[p, h, 0, :height], both_ref[p, h, 0, height:] = ar - bi, ar + bi
        both_ref[p, h, 1, :height], both_ref[p, h, 1, height:] = ai + br, ai - br
        for ri in range(2):
            cells = both_ref[p, h, ri, pl.ds(0, PATCH, stride=GROUP), :]
            for c in range(1, GROUP):
                cells = jnp.where(own == c, both_ref[p, h, ri, pl.ds(c, PATCH, stride=GROUP), :], cells)
            back_ref[h, ri, pl.ds(p * PATCH, PATCH), :] = cells.astype(BF16).astype(F32)

    def widen(h):
        for f in range(facets):
            lanes = slice(h * LANES, (h + 1) * LANES)
            made = times_conj(
                back_ref[h, 0], back_ref[h, 1], shift_real[f : f + 1, lanes], shift_imag[f : f + 1, lanes]
            )
            for ri in range(2):
                to = (2 * h + ri) * LANES
                narrow_ref[pl.ds(f * block_rows, block_rows), to : to + LANES] = made[ri].astype(BF16)

    tasks = [(p, h) for h in range(halves) for p in range(patch_rows)]
    inner, back = {}, {}
    for h in range(halves):
        predicted(h)
        for p in range(patch_rows):
            inner[p, h] = degrid(p, h)
    narrowed = []

    def finish(task):
        regrid(*task, back.pop(task))
        p, h = task
        if p == patch_rows - 1:
            widen(h)
            lanes = pl.ds(2 * h * LANES, 2 * LANES)
            narrowed.append(dot_t(narrow_ref[:, lanes], weights_ref[:, lanes]))

    for at, task in enumerate(tasks):
        left = weigh(*task, inner.pop(task))
        back[task] = dot_t(left, ev_ref[task[0], task[1]])
        if at:
            finish(tasks[at - 1])
    result = pltpu.make_async_copy(res_ref, res_hbm, res_sem)
    result.start()
    finish(tasks[-1])
    narrowed_ref[...] = sum(narrowed).astype(BF16)
    adjoint_rows(1, rows_ref, narrowed_ref, give_ref)
    result.wait()


def adjoint_rows(half, rows_ref, narrowed_ref, out_ref):
    facets, height, facet_rows = rows_ref.shape[0], rows_ref.shape[1], rows_ref.shape[2] // 2
    block_rows = height // 2
    pairs = out_ref.shape[0] // facets
    piece_rows = out_ref.shape[2]
    for f in range(facets):
        here = pl.ds(f * block_rows, block_rows)
        real, imag = narrowed_ref[here, :CONTRIB], narrowed_ref[here, CONTRIB:]
        lanes = pl.ds(half * (facet_rows // 2), facet_rows // 2)
        product = dot_0(rows_ref[f, :, lanes], block([[real, imag], [imag, -real]])).astype(BF16)
        for y in range(pairs):
            for ri in range(2):
                out_ref[y * facets + f, ri] = product[
                    y * piece_rows : (y + 1) * piece_rows, ri * CONTRIB : (ri + 1) * CONTRIB
                ]


def image_kernel(scale, in_ref, near_ref, far_ref, out_hbm, stage_ref, sem):
    parts = in_ref.shape[0]
    rows, extent = out_hbm.shape[2:]
    far_count = extent // LANES
    real, imag = (
        sum(in_ref[q, ri].astype(F32) for q in range(parts)) * scale for ri in range(2)
    )
    copies = []
    for top in range(0, far_count, CHUNK):
        left = []
        for y1 in range(top, top + CHUNK):
            ar, ai = times_conj(real, imag, far_ref[0, y1 : y1 + 1], far_ref[1, y1 : y1 + 1])
            left.append(jnp.concatenate([ar, ai], axis=1).astype(BF16))
        value = dot_t(jnp.concatenate(left, axis=0), near_ref[...])
        value = (value * (1.0 / math.sqrt(CONTRIB))).astype(BF16)
        for y1 in range(CHUNK):
            for ri in range(2):
                stage_ref[ri, :, pl.ds((top + y1) * LANES, LANES)] = value[
                    y1 * rows : (y1 + 1) * rows, ri * LANES : (ri + 1) * LANES
                ]
        for ri in range(2):
            span = pl.ds(top * LANES, CHUNK * LANES)
            copy = pltpu.make_async_copy(
                stage_ref.at[ri, :, span], out_hbm.at[0, ri, :, span], sem.at[len(copies)]
            )
            copy.start()
            copies.append(copy)
    for copy in copies:
        copy.wait()


HBM = pl.BlockSpec(memory_space=pltpu.HBM)
SMEM = pl.BlockSpec(memory_space=pltpu.SMEM)
VMEM = pl.BlockSpec(memory_space=pltpu.VMEM)


def call(kernel, name, operands, in_specs, outs, scratch=(), out_specs=None, flops=None):
    return pl.pallas_call(
        kernel,
        name=name,
        out_shape=outs,
        in_specs=in_specs,
        out_specs=out_specs or jax.tree.map(lambda _: VMEM, outs),
        scratch_shapes=list(scratch),
        cost_estimate=flops and pl.CostEstimate(flops=flops, bytes_accessed=0, transcendentals=0),
        compiler_params=pltpu.CompilerParams(vmem_limit_bytes=40 * 1024 * 1024),
    )(*operands)


def on_device(facet_image, facet_offsets, subgrid_rows, column_offset, uv_coords, observed):
    shape = jax.ShapeDtypeStruct
    rows, extent = facet_image.shape[2:]
    facets = lax.axis_size("facet")
    parts = lax.axis_size("freq")
    subgrids = subgrid_rows.shape[0]
    block_rows = uv_coords.shape[1] * PATCH
    members = facets * parts // 2
    groups = [
        [(2 * y + (c + f + y) % 2) * facets + f for y in range(parts // 2) for f in range(facets)]
        for c in range(2)
    ]

    def exchange(value):
        return lax.all_to_all(
            value, ("freq", "facet"), split_axis=0, concat_axis=0, axis_index_groups=groups, tiled=True
        )

    def swap(value):
        return lax.ppermute(value, "freq", [(q, q ^ 1) for q in range(parts)])

    pieces = shape((members, 2, rows, CONTRIB), BF16)
    far_count = extent // LANES
    near, far, weights = call(
        phase_kernel,
        "phase",
        (column_offset, facet_offsets),
        [SMEM, VMEM],
        (
            shape((2 * LANES, 2 * CONTRIB), BF16),
            shape((2, far_count, CONTRIB), F32),
            shape((2 * CONTRIB, 2 * SUBGRID), BF16),
        ),
        flops=200_000_000,
    )
    transformed = call(
        column_kernel,
        "column",
        (near, far, facet_image),
        [VMEM] * 3,
        pieces,
    )
    own = exchange(transformed)
    other = swap(own)
    patch_rows, vis = uv_coords.shape[1], uv_coords.shape[3]
    halves = SIDE * PATCH // LANES
    row_products, *tables = call(
        functools.partial(table_kernel, rows),
        "tables",
        (subgrid_rows, facet_offsets, uv_coords),
        [VMEM, VMEM, VMEM],
        (
            shape((facets, 2 * block_rows, 2 * parts * rows), BF16),
            shape((2, facets, SUBGRID), F32),
            shape((patch_rows, halves, 2, LANES // 2, vis), F32),
            shape((patch_rows, halves, 2, 2 * GROUP, vis), F32),
            shape((patch_rows, halves, 2 * LANES, vis), BF16),
        ),
        (
            pltpu.SMEM(subgrid_rows.shape, jnp.int32),
            pltpu.SMEM(facet_offsets.shape, jnp.int32),
            pltpu.VMEM((facets * 2 * block_rows, parts * rows), BF16),
            pltpu.SemaphoreType.DMA((2,)),
        ),
    )
    narrowed, give, residual_vis = call(
        grid_kernel,
        "grid",
        (own, other, row_products, weights, *tables, observed),
        [VMEM] * 9,
        (
            shape((facets * block_rows, 2 * CONTRIB), BF16),
            pieces,
            shape(observed.shape, BF16),
        ),
        (
            pltpu.VMEM(observed.shape, BF16),
            pltpu.VMEM((facets * block_rows, 2 * CONTRIB), BF16),
            pltpu.VMEM((halves, 2, block_rows, LANES), F32),
            pltpu.VMEM((halves, 2, block_rows, LANES), F32),
            pltpu.VMEM((patch_rows, halves, 2, LANES, LANES), F32),
            pltpu.VMEM((facets * block_rows, 2 * SUBGRID), BF16),
            pltpu.SemaphoreType.DMA,
        ),
        (VMEM, VMEM, HBM),
    )
    keep = call(
        functools.partial(adjoint_rows, 0),
        "keep",
        (row_products, narrowed),
        [VMEM] * 2,
        pieces,
    )
    partial = (keep.astype(F32) + swap(give).astype(F32)).astype(BF16)
    shared_scale = 1.0 / CONTRIB / math.sqrt(parts * rows)
    scale = 1.0 / (math.sqrt(vis) * SUBGRID * math.sqrt(subgrids * CONTRIB) * shared_scale)
    image_residual = call(
        functools.partial(image_kernel, scale),
        "image",
        (exchange(partial), near, far),
        [VMEM] * 3,
        shape(facet_image.shape, BF16),
        (
            pltpu.VMEM(facet_image.shape[1:], BF16),
            pltpu.SemaphoreType.DMA((2 * far_count // CHUNK,)),
        ),
        HBM,
    )
    return (image_residual, residual_vis)


def solution(mesh):
    return jax.shard_map(
        on_device,
        mesh=mesh,
        in_specs=(
            P("facet", None, "freq", None),
            P(),
            P(),
            P(),
            P(None, ("freq", "facet"), None, None),
            P(None, ("freq", "facet"), None, None),
        ),
        out_specs=(P("facet", None, "freq", None), P(None, ("freq", "facet"), None, None)),
        check_vma=False,
    )
```
